256 devices in a mesh: tm: 64 (over x, z, core), rows: 4 (over y).
Axes of the slice: x: 4, y: 4, z: 8, core: 2. Of those that a mesh axis runs over, the one named last changes fastest.
Arguments:
- features: bfloat16 [128, 4, 160, 512], P('tm', 'rows'), may hold values from -25 to 25
- norm_gain: float32 [512], replicated, may hold values from 0.1 to 1.9
- norm_bias: float32 [512], replicated, may hold values from -1 to 1
- weight: bfloat16 [3, 3, 3, 512, 256], replicated, may hold values from -0.0546875 to 0.0546875
- upstream: bfloat16 [128, 4, 160, 256], P('tm', 'rows'), may hold values from -20 to 20
Outputs:
- grad_features: bfloat16 [128, 4, 160, 512], P('tm', 'rows')
- grad_weight: float32 [3, 3, 3, 512, 256], P(None, None, None, 'tm', 'rows')
- grad_gain: float32 [512], replicated
- grad_bias: float32 [512], replicated
The draws below stay inside these ranges and needn't reach their ends.
All inputs are finite; a program needn't handle non-finite values.
Results may differ from the reference program's by a relative error of at most 0.0015.
Values may be sent and summed in bfloat16 or wider, within the bound.
No kernel may reach another device: no remote copies, remote signals or barrier semaphores. Data moves between devices by JAX's collectives and lax.ppermute only.
A program may use at most 64 MiB of HBM per device.

```python
import jax
import jax.numpy as jnp
from jax import lax

C = 512
CO = 256
GROUPS = 32
CLIPS = 1
TF = 2
HD = 1
W = 160
FRAMES = 128
CLIP_FRAMES = 128
H = 4


def draw_features(key, part):
    keys = jax.random.split(key, 4)
    shape_all = (FRAMES, H, W, C)
    position = (jnp.arange(FRAMES) % CLIP_FRAMES).astype(jnp.float32) / max(CLIP_FRAMES - 1, 1)
    ramp = (1.0 + 2.0 * position)[:, None, None, None]
    chan_scale = jnp.exp(jax.random.uniform(keys[2], (C,), jnp.float32, -0.7, 0.7))
    blocks = H // HD
    order = jax.random.permutation(keys[3], blocks).astype(jnp.float32)
    level = order / max(blocks - 1, 1)
    block_of_row = jnp.arange(H) // HD
    row_level = jnp.take(level, block_of_row)
    row_scale = jnp.power(0.35, row_level)[None, :, None, None]
    base = jnp.clip(jax.random.normal(keys[0], shape_all, jnp.float32), -4.0, 4.0)
    return (base * ramp * chan_scale * row_scale).astype(jnp.bfloat16)


def draw_upstream(key, part):
    keys = jax.random.split(key, 3)
    shape_all = (FRAMES, H, W, CO)
    chan_offset = 0.4 * jnp.clip(jax.random.normal(keys[1], (CO,), jnp.float32), -3.0, 3.0)
    base = jnp.clip(jax.random.normal(keys[0], shape_all, jnp.float32), -5.0, 5.0)
    chosen = jax.random.permutation(keys[2], CO)
    frame_block = jnp.arange(FRAMES) // TF
    target = jnp.take(chosen, frame_block % CO)
    marked = (jnp.arange(CO)[None, :] == target[:, None]).astype(jnp.float32)
    boost = (1.0 + 2.0 * marked)[:, None, None, :]
    return ((base + chan_offset) * boost).astype(jnp.bfloat16)


def noise(rng, extent, width, reach, dtype=jnp.bfloat16):
    result = jax.random.normal(rng, extent, jnp.float32) * width
    return jnp.minimum(jnp.maximum(result, -reach), reach).astype(dtype)


def setup_inputs(seed: int = 0) -> dict:
    arg_keys = jax.random.split(jax.random.key(seed), 6)
    return {
        "features": draw_features(jax.random.fold_in(arg_keys[5], 71), 0),
        "norm_gain": jnp.clip(1.0 + 0.18 * jax.random.normal(arg_keys[1], (C,), jnp.float32), 0.1, 1.9),
        "norm_bias": jnp.clip(jax.random.uniform(arg_keys[2], (C,), jnp.float32, -1.0, 1.0), -1.0, 1.0),
        "weight": noise(arg_keys[3], (3, 3, 3, C, CO), (27 * C) ** -0.5, 0.0546875),
        "upstream": draw_upstream(jax.random.fold_in(arg_keys[5], 71), 0),
    }


epsilon = 1e-06

def reference(features, norm_gain, norm_bias, weight, upstream):
    group_size = C // GROUPS
    floats = features.astype(jnp.float32)
    grouped = floats.reshape(CLIPS, CLIP_FRAMES, H, W, GROUPS, group_size)
    centre_val = lax.optimization_barrier(jnp.mean(grouped, axis=(1, 2, 3, 5), keepdims=True))
    diffs = grouped - centre_val
    spread = lax.optimization_barrier(jnp.mean(diffs * diffs, axis=(1, 2, 3, 5), keepdims=True))
    inverse = lax.rsqrt(spread + epsilon)
    normed = (diffs * inverse).reshape(CLIPS, CLIP_FRAMES, H, W, C)
    preact = normed * norm_gain + norm_bias
    sig_val = jax.nn.sigmoid(preact)
    hidden = (preact * sig_val).astype(jnp.bfloat16)
    padded = jnp.concatenate([hidden[:, :1], hidden[:, :1], hidden], axis=1)
    padded = jnp.pad(padded, ((0, 0), (0, 0), (1, 1), (1, 1), (0, 0)))
    up_clips = upstream.reshape(CLIPS, CLIP_FRAMES, H, W, CO)
    up_flat = up_clips.reshape(-1, CO)
    grad_taps = []
    for time_tap in range(3):
        for row_tap in range(3):
            for col_tap in range(3):
                slab = padded[:, time_tap:time_tap + CLIP_FRAMES, row_tap:row_tap + H, col_tap:col_tap + W].reshape(-1, C)
                grad_taps.append(lax.dot_general(slab, up_flat, (((0,), (0,)), ((), ())), preferred_element_type=jnp.float32))
    grad_weight = jnp.stack(grad_taps).reshape(3, 3, 3, C, CO)
    up_padded = jnp.pad(up_clips, ((0, 0), (2, 2), (1, 1), (1, 1), (0, 0)))
    dense = jnp.zeros((CLIPS * (CLIP_FRAMES + 2) * H * W, C), jnp.float32)
    for time_tap in range(3):
        for row_tap in range(3):
            for col_tap in range(3):
                slab = up_padded[:, 2 - time_tap:4 - time_tap + CLIP_FRAMES, 2 - row_tap:2 - row_tap + H, 2 - col_tap:2 - col_tap + W].reshape(-1, CO)
                dense = dense + jnp.dot(slab, weight[time_tap, row_tap, col_tap].T, preferred_element_type=jnp.float32)
    dense = dense.reshape(CLIPS, CLIP_FRAMES + 2, H, W, C)
    grad_hidden = dense[:, 2:].at[:, 0].add(dense[:, 0] + dense[:, 1])
    grad_act = grad_hidden * sig_val * (1.0 + preact * (1.0 - sig_val))
    clip_gain = lax.optimization_barrier(jnp.sum(grad_act * normed, axis=(1, 2, 3)))
    clip_bias = lax.optimization_barrier(jnp.sum(grad_act, axis=(1, 2, 3)))
    grad_gain = lax.optimization_barrier(jnp.sum(clip_gain, axis=0))
    grad_bias = lax.optimization_barrier(jnp.sum(clip_bias, axis=0))
    count_clip = CLIP_FRAMES * H * W * group_size
    first_term = jnp.repeat(lax.optimization_barrier(jnp.sum((norm_gain * clip_bias).reshape(CLIPS, GROUPS, group_size), axis=2)) / count_clip, group_size, axis=1)
    second_term = jnp.repeat(lax.optimization_barrier(jnp.sum((norm_gain * clip_gain).reshape(CLIPS, GROUPS, group_size), axis=2)) / count_clip, group_size, axis=1)
    inverse_chan = jnp.repeat(inverse.reshape(CLIPS, GROUPS), group_size, axis=1)
    first_term = first_term[:, None, None, None, :]
    second_term = second_term[:, None, None, None, :]
    inverse_chan = inverse_chan[:, None, None, None, :]
    grad_features = (inverse_chan * (grad_act * norm_gain - first_term - normed * second_term)).astype(jnp.bfloat16)
    return (grad_features.reshape(FRAMES, H, W, C), grad_weight, grad_gain, grad_bias)
```

```python
import functools

import jax
import jax.numpy as jnp
from jax import lax
from jax.experimental import pallas as pl
from jax.experimental.pallas import tpu as pltpu
from jax.sharding import PartitionSpec as P

GROUPS = 32
EPS = 1e-06
TEAM = 4
F32 = jnp.float32
BF16 = jnp.bfloat16


def iota(shape, dim):
    return lax.broadcasted_iota(jnp.int32, shape, dim)


def exact_dot(a, b, dims=((1,), (0,))):
    return lax.dot_general(
        a, b, (dims, ((), ())), precision=lax.Precision.HIGHEST, preferred_element_type=F32
    )


def members(chans, offset):
    size = chans // GROUPS
    return (iota((chans, 128), 0) // size + offset == iota((chans, 128), 1)).astype(F32)


def col_shifts(slab):
    cols = slab.shape[0]
    wide = slab.astype(F32)
    row = iota(wide.shape, 0)
    ahead = jnp.where(row < cols - 1, pltpu.roll(wide, cols - 1, 0), 0.0).astype(BF16)
    behind = jnp.where(row > 0, pltpu.roll(wide, 1, 0), 0.0).astype(BF16)
    return ahead, slab, behind


def pack_kernel(teams, feats_ref, up_ref, load_ref, stat_ref):
    positions, chans = feats_ref.shape
    cols = up_ref.shape[1]
    rows = load_ref.shape[1]
    feats = feats_ref[...]
    lane = iota((chans, chans), 1)
    wide = chans // TEAM
    step = chans // teams
    source = (lane % wide) // step * (step * TEAM) + lane // wide * step + lane % step
    mover = (iota((chans, chans), 0) == source).astype(BF16)
    moved = jnp.dot(feats, mover, preferred_element_type=F32).astype(BF16)
    outs = up_ref.shape[2] // rows
    for r in range(rows):
        pair = jnp.concatenate(
            [up_ref[0, :, r * outs : (r + 1) * outs], up_ref[1, :, r * outs : (r + 1) * outs]], axis=1
        )
        for j in range(TEAM):
            load_ref[j, r, 0:positions, :] = moved[:, j * wide : (j + 1) * wide]
            load_ref[j, r, positions : positions + cols, :] = pair
    floats = feats.astype(F32)
    first = members(chans, 0)
    second = members(chans, GROUPS)
    total = jnp.broadcast_to(jnp.sum(floats, axis=0, keepdims=True), (8, chans))
    mean = exact_dot(total, first) / (positions * (chans // GROUPS))
    diffs = floats - exact_dot(mean, first, ((1,), (1,)))[0:1]
    squares = jnp.broadcast_to(jnp.sum(diffs * diffs, axis=0, keepdims=True), (8, chans))
    stat = mean + exact_dot(squares, second)
    stat_ref[...] = jnp.broadcast_to(stat[0:1], stat_ref.shape)


def act_kernel(
    feats_ref, gain_ref, bias_ref, stats_ref, up_ref, later_ref, above_ref, below_ref, weight_ref,
    act_ref, sums_ref, norm_ref, slabs, acc,
):
    step = pl.program_id(0)
    time_tap = step // 3
    row_tap = step % 3
    time_index = lax.axis_index("tm")
    row_index = lax.axis_index("rows")
    positions, chans = acc.shape
    cols = up_ref.shape[1]

    @pl.when(step == 0)
    def _():
        acc[...] = jnp.zeros_like(acc)
        more = (time_index < lax.axis_size("tm") - 1).astype(F32)
        up_ok = (row_index > 0).astype(F32)
        down_ok = (row_index < lax.axis_size("rows") - 1).astype(F32)
        for f in range(4):
            own = up_ref[f] if f < 2 else later_ref[f - 2]
            tail = jnp.float32(1.0) if f < 2 else more
            for r, slab, keep in ((0, above_ref[f], up_ok), (1, own, None), (2, below_ref[f], down_ok)):
                scale = tail if keep is None else keep * tail
                slab = (slab.astype(F32) * scale).astype(BF16)
                for c, moved in enumerate(col_shifts(slab)):
                    slabs[c, r, f] = moved

    def product(slab, c):
        return lax.dot_general(
            slab, weight_ref[0, 0, c], (((1,), (1,)), ((), ())), preferred_element_type=F32
        )

    total = acc[...]
    for c in range(3):
        slab = slabs[c, 2 - row_tap, pl.ds(2 - time_tap, 2)].reshape(positions, -1)
        total = total + product(slab, c)
    acc[...] = total

    @pl.when(jnp.logical_and(time_index == 0, time_tap == 0))
    def _():
        for c in range(3):
            both = slabs[c, 2 - row_tap, pl.ds(0, 2)].reshape(positions, -1)
            both = product(both, c)
            acc[0:cols, :] += both[0:cols] + both[cols:]

    @pl.when(jnp.logical_and(time_index == 0, time_tap == 1))
    def _():
        for c in range(3):
            acc[0:cols, :] += product(slabs[c, 2 - row_tap, 0], c)

    @pl.when(step == pl.num_programs(0) - 1)
    def _():
        stats = stats_ref[...]
        devices = stats.shape[0]
        size = chans // GROUPS
        first = members(chans, 0)
        second = members(chans, GROUPS)
        centre = jnp.sum(stats, axis=0, keepdims=True) / devices
        spans = stats - centre
        spans = jnp.sum(spans * spans, axis=0, keepdims=True)
        dims = ((1,), (1,))
        parts = exact_dot(jnp.broadcast_to(jnp.sum(stats, axis=0, keepdims=True), (8, 128)), second, dims)
        parts = parts / (devices * positions * size)
        parts = parts + exact_dot(jnp.broadcast_to(spans, (8, 128)), first, dims) / devices
        inverse = lax.rsqrt(parts + EPS)
        centre = exact_dot(jnp.broadcast_to(centre, (8, 128)), first, dims)
        norm_ref[0:8] = centre
        norm_ref[8:16] = inverse
        normed = (feats_ref[...].astype(F32) - centre[0:1]) * inverse[0:1]
        preact = normed * gain_ref[...] + bias_ref[...]
        sig = 1.0 / (1.0 + jnp.exp(-preact))
        act = acc[...] * sig * (1.0 + preact * (1.0 - sig))
        act_ref[...] = act
        gains = jnp.sum(act * normed, axis=0, keepdims=True)
        biases = jnp.sum(act, axis=0, keepdims=True)
        pieces = chans // 128
        for p in range(pieces):
            sums_ref[p : p + 1, :] = gains[:, p * 128 : (p + 1) * 128]
            sums_ref[pieces + p : pieces + p + 1, :] = biases[:, p * 128 : (p + 1) * 128]


def weight_kernel(teams, load_ref, halo_ref, norm_ref, gain_ref, bias_ref, sums_ref, out_ref, hidden, acc):
    time_index = lax.axis_index("tm")
    rows = load_ref.shape[1]
    cols = hidden.shape[2]
    chans = gain_ref.shape[1]
    wide = chans // TEAM
    step = chans // teams
    spot = time_index % TEAM
    lane = iota((chans, wide), 1)
    mover = (iota((chans, wide), 0) == lane // step * (step * TEAM) + spot * step + lane % step).astype(F32)

    def slice_of(value):
        return exact_dot(value, mover)[0:1]

    centre = slice_of(norm_ref[0:8])
    inverse = slice_of(norm_ref[8:16])
    gain = slice_of(jnp.broadcast_to(gain_ref[...], (8, chans)))
    bias = slice_of(jnp.broadcast_to(bias_ref[...], (8, chans)))

    def silu(value):
        preact = (value.astype(F32) - centre) * inverse * gain + bias
        return (preact * (1.0 / (1.0 + jnp.exp(-preact)))).astype(BF16)

    frames = 2 * TEAM
    for f in range(frames + 2):
        hidden[f, 0] = jnp.zeros(hidden.shape[2:], BF16)
        hidden[f, rows + 1] = jnp.zeros(hidden.shape[2:], BF16)
    for j in range(TEAM):
        for r in range(rows):
            for f in range(2):
                hidden[2 + 2 * j + f, 1 + r] = silu(load_ref[j, r, f * cols : (f + 1) * cols, :])
    for r in range(rows):
        for f in range(2):
            source = jnp.where(time_index < TEAM, load_ref[0, r, 0:cols, :], halo_ref[r, f * cols : (f + 1) * cols, :])
            hidden[f, 1 + r] = silu(source)

    lanes = iota((cols, 128), 1) < 64
    for j in range(TEAM):
        halves = [[], []]
        for r in range(rows):
            pair = load_ref[j, r, 2 * cols : 3 * cols, :].astype(F32)
            row = iota(pair.shape, 0)
            ahead = jnp.where(row < cols - 1, pltpu.roll(pair, cols - 1, 0), 0.0)
            behind = jnp.where(row > 0, pltpu.roll(pair, 1, 0), 0.0)
            left = jnp.where(lanes, ahead, pltpu.roll(pair, 64, 1))
            right = jnp.where(lanes, pltpu.roll(ahead, 64, 1), pair)
            halves[0].append(jnp.concatenate([left, behind[:, 0:64]], axis=1))
            halves[1].append(jnp.concatenate([right, behind[:, 64:128]], axis=1))
        for f in range(2):
            ups = jnp.concatenate(halves[f], axis=0).astype(BF16)
            taps = [
                hidden[2 * j + f + a, b : b + rows].reshape(rows * cols, wide) for a in range(3) for b in range(3)
            ]
            term = lax.dot_general(
                ups, jnp.concatenate(taps, axis=1), (((0,), (0,)), ((), ())), preferred_element_type=F32
            )
            if j == 0 and f == 0:
                acc[...] = term
            else:
                acc[...] += term

    groups = out_ref.shape[0]
    tail = None
    for ab in range(9):
        block = acc[:, ab * wide : (ab + 1) * wide].T
        out_ref[:, ab * step : (ab + 1) * step, :] = block[:, 0:128].reshape(groups, step, 128)
        last = block[:, 128:192]
        if ab % 2 == 0:
            tail = last
        if ab % 2 == 1 or ab == 8:
            both = jnp.concatenate([tail, last], axis=1)
            at = (9 + ab // 2) * step
            out_ref[:, at : at + step, :] = both.reshape(groups, step, 128)
    out_ref[:, 14 * step :, :] = jnp.broadcast_to(sums_ref[...][None], (groups,) + sums_ref.shape)


def unpack_kernel(load_ref, grad_ref, sums_ref):
    step = grad_ref.shape[2]
    total = load_ref[0]
    for g in range(1, load_ref.shape[0]):
        total = total + load_ref[g]
    for ab in range(9):
        part = total[ab * step : (ab + 1) * step]
        grad_ref[ab, 0] = part[:, 0:64]
        grad_ref[ab, 1] = part[:, 64:128]
        at = (9 + ab // 2) * step
        side = 64 * (ab % 2)
        grad_ref[ab, 2] = total[at : at + step, side : side + 64]
    sums_ref[...] = jnp.broadcast_to(total[14 * step :][None], sums_ref.shape)


def final_kernel(count, sums_ref, act_ref, feats_ref, norm_ref, gain_ref, out_ref, gain_out_ref, bias_out_ref):
    chans = gain_ref.shape[1]
    pieces = chans // 128
    total = sums_ref[0]
    for g in range(1, sums_ref.shape[0]):
        total = total + sums_ref[g]
    gains = jnp.concatenate([total[p : p + 1] for p in range(pieces)], axis=1)
    biases = jnp.concatenate([total[pieces + p : pieces + p + 1] for p in range(pieces)], axis=1)
    gain_out_ref[...] = gains
    bias_out_ref[...] = biases
    gain = gain_ref[...]
    owner = members(chans, 0)

    def spread(value):
        value = exact_dot(jnp.broadcast_to(value, (8, chans)), owner) / count
        return exact_dot(value, owner, ((1,), (1,)))[0:1]

    first = spread(gain * biases)
    second = spread(gain * gains)
    centre = norm_ref[0:1]
    inverse = norm_ref[8:9]
    normed = (feats_ref[...].astype(F32) - centre) * inverse
    out_ref[...] = (inverse * (act_ref[...] * gain - first - normed * second)).astype(BF16)


def on_device(features, norm_gain, norm_bias, weight, upstream):
    frames, rows_dev, cols, chans = features.shape
    outs = upstream.shape[3]
    tms = lax.axis_size("tm")
    rows = lax.axis_size("rows")
    devices = tms * rows
    positions = frames * rows_dev * cols
    step = chans // tms
    groups = tms // TEAM
    wide = chans // TEAM
    count = positions * devices * (chans // GROUPS)
    params = pltpu.CompilerParams(vmem_limit_bytes=60 * 1024 * 1024)

    feats = features.reshape(positions, chans)
    ups = upstream.reshape(frames, cols, outs)
    gain = norm_gain.reshape(1, chans)
    bias = norm_bias.reshape(1, chans)

    later = lax.ppermute(ups, "tm", [((i + 1) % tms, i) for i in range(tms)])
    four = jnp.concatenate([ups, later], axis=0)
    above = lax.ppermute(four, "rows", [(i, (i + 1) % rows) for i in range(rows)])
    below = lax.ppermute(four, "rows", [((i + 1) % rows, i) for i in range(rows)])

    load, stat = pl.pallas_call(
        functools.partial(pack_kernel, tms),
        out_shape=(
            jax.ShapeDtypeStruct((TEAM, rows, positions + cols, wide), BF16),
            jax.ShapeDtypeStruct((devices, 128), F32),
        ),
        compiler_params=params,
        name="pack",
    )(feats, ups)
    teams = [[TEAM * rows * g + i for i in range(TEAM * rows)] for g in range(groups)]
    load = lax.all_to_all(
        load.reshape(TEAM * rows, positions + cols, wide),
        ("tm", "rows"), 0, 0, tiled=True, axis_index_groups=teams,
    ).reshape(TEAM, rows, positions + cols, wide)
    halo = lax.ppermute(load[TEAM - 1, :, :positions], "tm", [(i, (i + TEAM) % tms) for i in range(tms)])
    stats = lax.all_to_all(stat, ("tm", "rows"), 0, 0, tiled=True)

    whole = lambda shape: pl.BlockSpec(shape, lambda s: (0,) * len(shape))
    act, sums, norm = pl.pallas_call(
        act_kernel,
        grid=(9,),
        in_specs=[
            whole((positions, chans)), whole((1, chans)), whole((1, chans)), whole((devices, 128)),
            whole((2, cols, outs)), whole((2, cols, outs)), whole((4, cols, outs)), whole((4, cols, outs)),
            pl.BlockSpec((1, 1, 3, chans, outs), lambda s: (s // 3, s % 3, 0, 0, 0)),
        ],
        out_specs=(whole((positions, chans)), whole((8, 128)), whole((16, chans))),
        out_shape=(
            jax.ShapeDtypeStruct((positions, chans), F32),
            jax.ShapeDtypeStruct((8, 128), F32),
            jax.ShapeDtypeStruct((16, chans), F32),
        ),
        scratch_shapes=[pltpu.VMEM((3, 3, 4, cols, outs), BF16), pltpu.VMEM((positions, chans), F32)],
        compiler_params=params,
        name="act",
    )(feats, gain, bias, stats, ups, later, above, below, weight)

    part = pl.pallas_call(
        functools.partial(weight_kernel, tms),
        out_shape=jax.ShapeDtypeStruct((groups, 14 * step + 8, 128), F32),
        scratch_shapes=[
            pltpu.VMEM((2 * TEAM + 2, rows + 2, cols, wide), BF16),
            pltpu.VMEM((3 * 64, 9 * wide), F32),
        ],
        compiler_params=params,
        name="wgrad",
    )(load, halo, norm, gain, bias, sums)
    ranks = [[TEAM * g + j for g in range(groups)] for j in range(TEAM)]
    part = lax.all_to_all(part, "tm", 0, 0, tiled=True, axis_index_groups=ranks)

    grad_weight, sums = pl.pallas_call(
        unpack_kernel,
        out_shape=(
            jax.ShapeDtypeStruct((9, 3, step, outs // rows), F32),
            jax.ShapeDtypeStruct((TEAM * rows, 8, 128), F32),
        ),
        compiler_params=params,
        name="unpack",
    )(part)
    sums = lax.all_to_all(sums, ("tm", "rows"), 0, 0, tiled=True, axis_index_groups=teams)

    grad_features, grad_gain, grad_bias = pl.pallas_call(
        functools.partial(final_kernel, count),
        out_shape=(
            jax.ShapeDtypeStruct((positions, chans), BF16),
            jax.ShapeDtypeStruct((1, chans), F32),
            jax.ShapeDtypeStruct((1, chans), F32),
        ),
        compiler_params=params,
        name="final",
    )(sums, act, feats, norm, gain)
    return (
        grad_features.reshape(features.shape),
        grad_weight.reshape(3, 3, 3, step, outs // rows),
        grad_gain.reshape(chans),
        grad_bias.reshape(chans),
    )


def solution(mesh):
    in_specs = (P("tm", "rows", None, None), P(), P(), P(), P("tm", "rows", None, None))
    out_specs = (P("tm", "rows", None, None), P(None, None, None, "tm", "rows"), P(), P())
    return jax.shard_map(
        on_device, mesh=mesh, in_specs=in_specs, out_specs=out_specs, check_vma=False
    )
```

```python
import functools

import jax
import jax.numpy as jnp
from jax import lax
from jax.experimental import pallas as pl
from jax.experimental.pallas import tpu as pltpu
from jax.sharding import PartitionSpec as P


GROUPS = 32
EPS = 1e-06
TEAM = 4
F32 = jnp.float32
BF16 = jnp.bfloat16


def iota(shape, dim):
    return lax.broadcasted_iota(jnp.int32, shape, dim)


def exact_dot(a, b, dims=((1,), (0,))):
    return lax.dot_general(
        a, b, (dims, ((), ())), precision=lax.Precision.HIGHEST, preferred_element_type=F32
    )


def members(chans, offset):
    size = chans // GROUPS
    return (iota((chans, 128), 0) // size + offset == iota((chans, 128), 1)).astype(F32)


def col_shifts(slab):
    cols = slab.shape[0]
    wide = slab.astype(F32)
    row = iota(wide.shape, 0)
    ahead = jnp.where(row < cols - 1, pltpu.roll(wide, cols - 1, 0), 0.0).astype(BF16)
    behind = jnp.where(row > 0, pltpu.roll(wide, 1, 0), 0.0).astype(BF16)
    return ahead, slab, behind


def pack_kernel(teams, feats_ref, up_ref, load_ref):
    positions, chans = feats_ref.shape
    cols = up_ref.shape[1]
    rows = load_ref.shape[1]
    feats = feats_ref[...]
    lane = iota((chans, chans), 1)
    wide = chans // TEAM
    step = chans // teams
    source = (lane % wide) // step * (step * TEAM) + lane // wide * step + lane % step
    mover = (iota((chans, chans), 0) == source).astype(BF16)
    moved = jnp.dot(feats, mover, preferred_element_type=F32).astype(BF16)
    outs = up_ref.shape[2] // rows
    for r in range(rows):
        pair = jnp.concatenate(
            [up_ref[0, :, r * outs : (r + 1) * outs], up_ref[1, :, r * outs : (r + 1) * outs]], axis=1
        )
        for j in range(TEAM):
            load_ref[j, r, 0:positions, :] = moved[:, j * wide : (j + 1) * wide]
            load_ref[j, r, positions : positions + cols, :] = pair
    floats = feats.astype(F32)
    first = members(chans, 0)
    second = members(chans, GROUPS)
    total = jnp.broadcast_to(jnp.sum(floats, axis=0, keepdims=True), (8, chans))
    mean = exact_dot(total, first) / (positions * (chans // GROUPS))
    diffs = floats - exact_dot(mean, first, ((1,), (1,)))[0:1]
    squares = jnp.broadcast_to(jnp.sum(diffs * diffs, axis=0, keepdims=True), (8, chans))
    stat = mean + exact_dot(squares, second)
    high = stat.astype(BF16).astype(F32)
    mid = (stat - high).astype(BF16).astype(F32)
    low = stat - high - mid
    row = iota((8, 128), 0)
    parts = jnp.where(row == 0, high, jnp.where(row == 1, mid, jnp.where(row == 2, low, 0.0)))
    parts = jnp.concatenate([parts, jnp.zeros_like(parts)], axis=0).astype(BF16)
    for r in range(rows):
        for j in range(TEAM):
            load_ref[j, r, positions + cols :, :] = parts


def combine_kernel(count, load_ref, dense_ref, out_ref):
    stats = []
    for j in range(load_ref.shape[0]):
        for r in range(load_ref.shape[1]):
            parts = load_ref[j, r].astype(F32)
            stats.append(parts[0:1] + parts[1:2] + parts[2:3])
    total = stats[0]
    for stat in stats[1:]:
        total = total + stat
    mean = total / len(stats)
    spans = jnp.zeros_like(mean)
    for stat in stats:
        spans = spans + (stat - mean) * (stat - mean)
    lane = iota((8, 128), 1)
    moved = pltpu.roll(jnp.broadcast_to(spans, (8, 128)), GROUPS, 1)
    result = jnp.where(lane < GROUPS, jnp.broadcast_to(mean, (8, 128)), total + count * moved)
    out_ref[...] = jnp.broadcast_to(result[None], out_ref.shape)


def dense_kernel(up_ref, later_ref, above_ref, below_ref, weight_ref, out_ref, slabs):
    step = pl.program_id(0)
    time_tap = step // 3
    row_tap = step % 3
    time_index = lax.axis_index("tm")
    row_index = lax.axis_index("rows")
    positions = out_ref.shape[0]
    cols = up_ref.shape[1]

    @pl.when(step == 0)
    def _():
        out_ref[...] = jnp.zeros_like(out_ref)
        more = (time_index < lax.axis_size("tm") - 1).astype(F32)
        up_ok = (row_index > 0).astype(F32)
        down_ok = (row_index < lax.axis_size("rows") - 1).astype(F32)
        for f in range(4):
            own = up_ref[f] if f < 2 else later_ref[f - 2]
            tail = jnp.float32(1.0) if f < 2 else more
            for r, slab, keep in ((0, above_ref[f], up_ok), (1, own, None), (2, below_ref[f], down_ok)):
                scale = tail if keep is None else keep * tail
                slab = (slab.astype(F32) * scale).astype(BF16)
                for c, moved in enumerate(col_shifts(slab)):
                    slabs[c, r, f] = moved

    def product(slab, c):
        return lax.dot_general(
            slab, weight_ref[0, 0, c], (((1,), (1,)), ((), ())), preferred_element_type=F32
        )

    total = out_ref[...]
    for c in range(3):
        slab = slabs[c, 2 - row_tap, pl.ds(2 - time_tap, 2)].reshape(positions, -1)
        total = total + product(slab, c)
    out_ref[...] = total

    @pl.when(jnp.logical_and(time_index == 0, time_tap == 0))
    def _():
        for c in range(3):
            both = slabs[c, 2 - row_tap, pl.ds(0, 2)].reshape(positions, -1)
            both = product(both, c)
            out_ref[0:cols, :] += both[0:cols] + both[cols:]

    @pl.when(jnp.logical_and(time_index == 0, time_tap == 1))
    def _():
        for c in range(3):
            out_ref[0:cols, :] += product(slabs[c, 2 - row_tap, 0], c)


def norm_rows(stats_ref, chans, positions):
    stats = jnp.concatenate([stats_ref[g, 0:1] for g in range(stats_ref.shape[0])], axis=0)
    devices = stats.shape[0]
    size = chans // GROUPS
    first = members(chans, 0)
    second = members(chans, GROUPS)
    total = jnp.sum(stats, axis=0, keepdims=True)
    centre = total / devices
    spans = stats - centre
    spans = jnp.sum(spans * spans, axis=0, keepdims=True)
    dims = ((1,), (1,))
    parts = exact_dot(jnp.broadcast_to(total, (8, 128)), second, dims) / (devices * positions * size)
    parts = parts + exact_dot(jnp.broadcast_to(spans, (8, 128)), first, dims) / devices
    inverse = lax.rsqrt(parts + EPS)
    centre = exact_dot(jnp.broadcast_to(centre, (8, 128)), first, dims)
    return centre, inverse


def act_kernel(positions, feats_ref, gain_ref, bias_ref, stats_ref, dense_ref, act_ref, sums_ref, norm_ref):
    chans = gain_ref.shape[1]
    centre, inverse = norm_rows(stats_ref, chans, positions)
    norm_ref[0:8] = centre
    norm_ref[8:16] = inverse
    centre = centre[0:1]
    inverse = inverse[0:1]
    normed = (feats_ref[...].astype(F32) - centre) * inverse
    preact = normed * gain_ref[...] + bias_ref[...]
    sig = 1.0 / (1.0 + jnp.exp(-preact))
    act = dense_ref[...] * sig * (1.0 + preact * (1.0 - sig))
    act_ref[...] = act
    gains = jnp.sum(act * normed, axis=0, keepdims=True)
    biases = jnp.sum(act, axis=0, keepdims=True)
    pieces = chans // 128
    rows = [gains[:, p * 128 : (p + 1) * 128] for p in range(pieces)]
    rows = rows + [biases[:, p * 128 : (p + 1) * 128] for p in range(pieces)]
    sums_ref[...] = jnp.broadcast_to(jnp.concatenate(rows, axis=0)[None], sums_ref.shape)


def append_kernel(part_ref, load_ref, out_ref):
    total = load_ref[0]
    for g in range(1, load_ref.shape[0]):
        total = total + load_ref[g]
    out_ref[...] = jnp.broadcast_to(total[None], out_ref.shape)


def weight_kernel(teams, load_ref, halo_ref, norm_ref, gain_ref, bias_ref, out_ref, hidden, acc):
    time_index = lax.axis_index("tm")
    rows = load_ref.shape[1]
    cols = hidden.shape[2]
    chans = gain_ref.shape[1]
    wide = chans // TEAM
    step = chans // teams
    spot = time_index % TEAM
    lane = iota((chans, wide), 1)
    mover = (iota((chans, wide), 0) == lane // step * (step * TEAM) + spot * step + lane % step).astype(F32)

    def slice_of(value):
        return exact_dot(value, mover)[0:1]

    centre = slice_of(norm_ref[0:8])
    inverse = slice_of(norm_ref[8:16])
    gain = slice_of(jnp.broadcast_to(gain_ref[...], (8, chans)))
    bias = slice_of(jnp.broadcast_to(bias_ref[...], (8, chans)))

    def silu(value):
        preact = (value.astype(F32) - centre) * inverse * gain + bias
        return (preact * (1.0 / (1.0 + jnp.exp(-preact)))).astype(BF16)

    frames = 2 * TEAM
    for f in range(frames + 2):
        hidden[f, 0] = jnp.zeros(hidden.shape[2:], BF16)
        hidden[f, rows + 1] = jnp.zeros(hidden.shape[2:], BF16)
    for j in range(TEAM):
        for r in range(rows):
            for f in range(2):
                hidden[2 + 2 * j + f, 1 + r] = silu(load_ref[j, r, f * cols : (f + 1) * cols, :])
    for r in range(rows):
        for f in range(2):
            source = jnp.where(time_index < TEAM, load_ref[0, r, 0:cols, :], halo_ref[r, f * cols : (f + 1) * cols, :])
            hidden[f, 1 + r] = silu(source)

    lanes = iota((cols, 128), 1) < 64
    for j in range(TEAM):
        halves = [[], []]
        for r in range(rows):
            pair = load_ref[j, r, 2 * cols : 3 * cols, :].astype(F32)
            row = iota(pair.shape, 0)
            ahead = jnp.where(row < cols - 1, pltpu.roll(pair, cols - 1, 0), 0.0)
            behind = jnp.where(row > 0, pltpu.roll(pair, 1, 0), 0.0)
            left = jnp.where(lanes, ahead, pltpu.roll(pair, 64, 1))
            right = jnp.where(lanes, pltpu.roll(ahead, 64, 1), pair)
            halves[0].append(jnp.concatenate([left, behind[:, 0:64]], axis=1))
            halves[1].append(jnp.concatenate([right, behind[:, 64:128]], axis=1))
        for f in range(2):
            ups = jnp.concatenate(halves[f], axis=0).astype(BF16)
            taps = [
                hidden[2 * j + f + a, b : b + rows].reshape(rows * cols, wide) for a in range(3) for b in range(3)
            ]
            term = lax.dot_general(
                ups, jnp.concatenate(taps, axis=1), (((0,), (0,)), ((), ())), preferred_element_type=F32
            )
            if j == 0 and f == 0:
                acc[...] = term
            else:
                acc[...] += term

    groups = out_ref.shape[0]
    tail = None
    for ab in range(9):
        block = acc[:, ab * wide : (ab + 1) * wide].T
        out_ref[:, ab * step : (ab + 1) * step, :] = block[:, 0:128].reshape(groups, step, 128)
        last = block[:, 128:192]
        if ab % 2 == 0:
            tail = last
        if ab % 2 == 1 or ab == 8:
            both = jnp.concatenate([tail, last], axis=1)
            at = (9 + ab // 2) * step
            out_ref[:, at : at + step, :] = both.reshape(groups, step, 128)


def final_kernel(
    count, load_ref, act_ref, feats_ref, norm_ref, gain_ref, out_ref, grad_ref, gain_out_ref, bias_out_ref
):
    chans = gain_ref.shape[1]
    pieces = chans // 128
    step = grad_ref.shape[2]
    total = load_ref[0]
    for g in range(1, load_ref.shape[0]):
        total = total + load_ref[g]
    for ab in range(9):
        part = total[ab * step : (ab + 1) * step]
        grad_ref[ab, 0] = part[:, 0:64]
        grad_ref[ab, 1] = part[:, 64:128]
        at = (9 + ab // 2) * step
        side = 64 * (ab % 2)
        grad_ref[ab, 2] = total[at : at + step, side : side + 64]
    total = total[14 * step :]
    gains = jnp.concatenate([total[p : p + 1] for p in range(pieces)], axis=1)
    biases = jnp.concatenate([total[pieces + p : pieces + p + 1] for p in range(pieces)], axis=1)
    gain_out_ref[...] = gains
    bias_out_ref[...] = biases
    gain = gain_ref[...]
    owner = members(chans, 0)

    def spread(value):
        value = exact_dot(jnp.broadcast_to(value, (8, chans)), owner) / count
        return exact_dot(value, owner, ((1,), (1,)))[0:1]

    first = spread(gain * biases)
    second = spread(gain * gains)
    centre = norm_ref[0:1]
    inverse = norm_ref[8:9]
    normed = (feats_ref[...].astype(F32) - centre) * inverse
    out_ref[...] = (inverse * (act_ref[...] * gain - first - normed * second)).astype(BF16)


def on_device(features, norm_gain, norm_bias, weight, upstream):
    frames, rows_dev, cols, chans = features.shape
    outs = upstream.shape[3]
    tms = lax.axis_size("tm")
    rows = lax.axis_size("rows")
    devices = tms * rows
    positions = frames * rows_dev * cols
    step = chans // tms
    groups = tms // TEAM
    wide = chans // TEAM
    count = positions * devices * (chans // GROUPS)
    params = pltpu.CompilerParams(vmem_limit_bytes=60 * 1024 * 1024)

    feats = features.reshape(positions, chans)
    ups = upstream.reshape(frames, cols, outs)
    gain = norm_gain.reshape(1, chans)
    bias = norm_bias.reshape(1, chans)

    later = lax.ppermute(ups, "tm", [((i + 1) % tms, i) for i in range(tms)])
    four = jnp.concatenate([ups, later], axis=0)
    above = lax.ppermute(four, "rows", [(i, (i + 1) % rows) for i in range(rows)])
    below = lax.ppermute(four, "rows", [((i + 1) % rows, i) for i in range(rows)])

    length = positions + cols + 16
    load = pl.pallas_call(
        functools.partial(pack_kernel, tms),
        out_shape=jax.ShapeDtypeStruct((TEAM, rows, length, wide), BF16),
        compiler_params=params,
        name="pack",
    )(feats, ups)
    size = TEAM * rows
    teams = [[size * g + i for i in range(size)] for g in range(groups)]
    ranks = [[TEAM * g + j for g in range(groups)] for j in range(TEAM)]

    def in_teams(value):
        return lax.all_to_all(value, ("tm", "rows"), 0, 0, tiled=True, axis_index_groups=teams)

    def in_ranks(value):
        return lax.all_to_all(value, "tm", 0, 0, tiled=True, axis_index_groups=ranks)

    load = in_teams(load.reshape(size, length, wide)).reshape(TEAM, rows, length, wide)
    halo = lax.ppermute(load[TEAM - 1, :, :positions], "tm", [(i, (i + TEAM) % tms) for i in range(tms)])

    def whole(shape):
        return pl.BlockSpec(shape, lambda *s: (0,) * len(shape))

    dense_call = pl.pallas_call(
        dense_kernel,
        grid=(9,),
        in_specs=[
            whole((2, cols, outs)), whole((2, cols, outs)), whole((4, cols, outs)), whole((4, cols, outs)),
            pl.BlockSpec((1, 1, 3, chans, outs), lambda s: (s // 3, s % 3, 0, 0, 0)),
        ],
        out_specs=whole((positions, chans)),
        out_shape=jax.ShapeDtypeStruct((positions, chans), F32),
        scratch_shapes=[pltpu.VMEM((3, 3, 4, cols, outs), BF16)],
        compiler_params=params,
        name="dense",
    )
    dense = dense_call(ups, later, above, below, weight)

    stats = pl.pallas_call(
        functools.partial(combine_kernel, float(positions * (chans // GROUPS))),
        grid=(1,),
        in_specs=[
            pl.BlockSpec((TEAM, rows, 16, wide), lambda s: (0, 0, (positions + cols) // 16, 0)),
            pl.BlockSpec(memory_space=pl.ANY),
        ],
        out_specs=whole((groups, 8, 128)),
        out_shape=jax.ShapeDtypeStruct((groups, 8, 128), F32),
        compiler_params=params,
        name="combine",
    )(load, dense)
    stats = in_ranks(stats)

    act, sums, norm = pl.pallas_call(
        functools.partial(act_kernel, positions * size),
        out_shape=(
            jax.ShapeDtypeStruct((positions, chans), F32),
            jax.ShapeDtypeStruct((size, 8, 128), F32),
            jax.ShapeDtypeStruct((16, chans), F32),
        ),
        compiler_params=params,
        name="act",
    )(feats, gain, bias, stats, dense)
    sums = in_teams(sums)

    part = pl.pallas_call(
        functools.partial(weight_kernel, tms),
        out_shape=jax.ShapeDtypeStruct((groups, 14 * step + 8, 128), F32),
        scratch_shapes=[
            pltpu.VMEM((2 * TEAM + 2, rows + 2, cols, wide), BF16),
            pltpu.VMEM((3 * 64, 9 * wide), F32),
        ],
        compiler_params=params,
        name="wgrad",
    )(load, halo, norm, gain, bias)
    part = pl.pallas_call(
        append_kernel,
        grid=(1,),
        in_specs=[pl.BlockSpec(memory_space=pl.ANY), whole((size, 8, 128))],
        out_specs=pl.BlockSpec((groups, 8, 128), lambda s: (0, 14 * step // 8, 0)),
        out_shape=jax.ShapeDtypeStruct((groups, 14 * step + 8, 128), F32),
        input_output_aliases={0: 0},
        compiler_params=params,
        name="append",
    )(part, sums)
    part = in_ranks(part)

    grad_features, grad_weight, grad_gain, grad_bias = pl.pallas_call(
        functools.partial(final_kernel, count),
        out_shape=(
            jax.ShapeDtypeStruct((positions, chans), BF16),
            jax.ShapeDtypeStruct((9, 3, step, outs // rows), F32),
            jax.ShapeDtypeStruct((1, chans), F32),
            jax.ShapeDtypeStruct((1, chans), F32),
        ),
        compiler_params=params,
        name="final",
    )(part, act, feats, norm, gain)
    return (
        grad_features.reshape(features.shape),
        grad_weight.reshape(3, 3, 3, step, outs // rows),
        grad_gain.reshape(chans),
        grad_bias.reshape(chans),
    )


def solution(mesh):
    in_specs = (P("tm", "rows", None, None), P(), P(), P(), P("tm", "rows", None, None))
    out_specs = (P("tm", "rows", None, None), P(None, None, None, "tm", "rows"), P(), P())
    return jax.shard_map(on_device, mesh=mesh, in_specs=in_specs, out_specs=out_specs, check_vma=False)
```

```python
import functools

import jax
import jax.numpy as jnp
from jax import lax
from jax.experimental import pallas as pl
from jax.experimental.pallas import tpu as pltpu
from jax.sharding import PartitionSpec as P


GROUPS = 32
EPS = 1e-06
TEAM = 4
F32 = jnp.float32
BF16 = jnp.bfloat16


def iota(shape, dim):
    return lax.broadcasted_iota(jnp.int32, shape, dim)


def exact_dot(a, b, dims=((1,), (0,))):
    return lax.dot_general(
        a, b, (dims, ((), ())), precision=lax.Precision.HIGHEST, preferred_element_type=F32
    )


def members(chans, offset):
    size = chans // GROUPS
    return (iota((chans, 128), 0) // size + offset == iota((chans, 128), 1)).astype(F32)


def col_shifts(slab):
    cols = slab.shape[0]
    wide = slab.astype(F32)
    row = iota(wide.shape, 0)
    ahead = jnp.where(row < cols - 1, pltpu.roll(wide, cols - 1, 0), 0.0).astype(BF16)
    behind = jnp.where(row > 0, pltpu.roll(wide, 1, 0), 0.0).astype(BF16)
    return ahead, slab, behind


def pack_kernel(teams, feats_ref, up_ref, load_ref):
    positions, chans = feats_ref.shape
    cols = up_ref.shape[1]
    rows = load_ref.shape[1]
    feats = feats_ref[...]
    lane = iota((chans, chans), 1)
    wide = chans // TEAM
    step = chans // teams
    source = (lane % wide) // step * (step * TEAM) + lane // wide * step + lane % step
    mover = (iota((chans, chans), 0) == source).astype(BF16)
    moved = jnp.dot(feats, mover, preferred_element_type=F32).astype(BF16)
    outs = up_ref.shape[2] // rows
    for r in range(rows):
        pair = jnp.concatenate(
            [up_ref[0, :, r * outs : (r + 1) * outs], up_ref[1, :, r * outs : (r + 1) * outs]], axis=1
        )
        for j in range(TEAM):
            load_ref[j, r, 0:positions, :] = moved[:, j * wide : (j + 1) * wide]
            load_ref[j, r, positions : positions + cols, :] = pair
    floats = feats.astype(F32)
    first = members(chans, 0)
    second = members(chans, GROUPS)
    total = jnp.broadcast_to(jnp.sum(floats, axis=0, keepdims=True), (8, chans))
    mean = exact_dot(total, first) / (positions * (chans // GROUPS))
    diffs = floats - exact_dot(mean, first, ((1,), (1,)))[0:1]
    squares = jnp.broadcast_to(jnp.sum(diffs * diffs, axis=0, keepdims=True), (8, chans))
    stat = mean + exact_dot(squares, second)
    high = stat.astype(BF16).astype(F32)
    mid = (stat - high).astype(BF16).astype(F32)
    low = stat - high - mid
    row = iota((8, 128), 0)
    parts = jnp.where(row == 0, high, jnp.where(row == 1, mid, jnp.where(row == 2, low, 0.0)))
    parts = jnp.concatenate([parts, jnp.zeros_like(parts)], axis=0).astype(BF16)
    for r in range(rows):
        for j in range(TEAM):
            load_ref[j, r, positions + cols :, :] = parts


def combine_kernel(count, load_ref, out_ref):
    stats = []
    for j in range(load_ref.shape[0]):
        for r in range(load_ref.shape[1]):
            parts = load_ref[j, r, load_ref.shape[2] - 16 :].astype(F32)
            stats.append(parts[0:1] + parts[1:2] + parts[2:3])
    total = stats[0]
    for stat in stats[1:]:
        total = total + stat
    mean = total / len(stats)
    spans = jnp.zeros_like(mean)
    for stat in stats:
        spans = spans + (stat - mean) * (stat - mean)
    lane = iota((8, 128), 1)
    moved = pltpu.roll(jnp.broadcast_to(spans, (8, 128)), GROUPS, 1)
    result = jnp.where(lane < GROUPS, jnp.broadcast_to(mean, (8, 128)), total + count * moved)
    out_ref[...] = jnp.broadcast_to(result[None], out_ref.shape)


def dense_kernel(now_ref, later_ref, weight_ref, out_ref, slabs):
    step = pl.program_id(0)
    time_tap = step // 3
    row_tap = step % 3
    time_index = lax.axis_index("tm")
    row_index = lax.axis_index("rows")
    positions = out_ref.shape[0]
    cols = now_ref.shape[2]

    @pl.when(step == 0)
    def _():
        out_ref[...] = jnp.zeros_like(out_ref)
        more = (time_index < lax.axis_size("tm") - 1).astype(F32)
        up_ok = (row_index > 0).astype(F32)
        down_ok = (row_index < lax.axis_size("rows") - 1).astype(F32)
        for f in range(4):
            source = now_ref if f < 2 else later_ref
            tail = jnp.float32(1.0) if f < 2 else more
            for r, keep in ((0, up_ok), (1, jnp.float32(1.0)), (2, down_ok)):
                slab = (source[r, f % 2].astype(F32) * (keep * tail)).astype(BF16)
                for c, moved in enumerate(col_shifts(slab)):
                    slabs[c, r, f] = moved

    def product(slab, c):
        return lax.dot_general(
            slab, weight_ref[0, 0, c], (((1,), (1,)), ((), ())), preferred_element_type=F32
        )

    total = out_ref[...]
    for c in range(3):
        slab = slabs[c, 2 - row_tap, pl.ds(2 - time_tap, 2)].reshape(positions, -1)
        total = total + product(slab, c)
    out_ref[...] = total

    @pl.when(jnp.logical_and(time_index == 0, time_tap == 0))
    def _():
        for c in range(3):
            both = slabs[c, 2 - row_tap, pl.ds(0, 2)].reshape(positions, -1)
            both = product(both, c)
            out_ref[0:cols, :] += both[0:cols] + both[cols:]

    @pl.when(jnp.logical_and(time_index == 0, time_tap == 1))
    def _():
        for c in range(3):
            out_ref[0:cols, :] += product(slabs[c, 2 - row_tap, 0], c)


def norm_rows(stats_ref, chans, positions):
    stats = jnp.concatenate([stats_ref[g, 0:1] for g in range(stats_ref.shape[0])], axis=0)
    devices = stats.shape[0]
    size = chans // GROUPS
    first = members(chans, 0)
    second = members(chans, GROUPS)
    total = jnp.sum(stats, axis=0, keepdims=True)
    centre = total / devices
    spans = stats - centre
    spans = jnp.sum(spans * spans, axis=0, keepdims=True)
    dims = ((1,), (1,))
    parts = exact_dot(jnp.broadcast_to(total, (8, 128)), second, dims) / (devices * positions * size)
    parts = parts + exact_dot(jnp.broadcast_to(spans, (8, 128)), first, dims) / devices
    inverse = lax.rsqrt(parts + EPS)
    centre = exact_dot(jnp.broadcast_to(centre, (8, 128)), first, dims)
    return centre, inverse


def act_kernel(positions, feats_ref, gain_ref, bias_ref, stats_ref, dense_ref, act_ref, sums_ref, norm_ref):
    chans = gain_ref.shape[1]
    centre, inverse = norm_rows(stats_ref, chans, positions)
    norm_ref[0:8] = centre
    norm_ref[8:16] = inverse
    centre = centre[0:1]
    inverse = inverse[0:1]
    normed = (feats_ref[...].astype(F32) - centre) * inverse
    preact = normed * gain_ref[...] + bias_ref[...]
    sig = 1.0 / (1.0 + jnp.exp(-preact))
    act = dense_ref[...] * sig * (1.0 + preact * (1.0 - sig))
    act_ref[...] = act
    gains = jnp.sum(act * normed, axis=0, keepdims=True)
    biases = jnp.sum(act, axis=0, keepdims=True)
    pieces = chans // 128
    rows = [gains[:, p * 128 : (p + 1) * 128] for p in range(pieces)]
    rows = rows + [biases[:, p * 128 : (p + 1) * 128] for p in range(pieces)]
    sums_ref[...] = jnp.broadcast_to(jnp.concatenate(rows, axis=0)[None], sums_ref.shape)


def append_kernel(part_ref, load_ref, out_ref):
    total = load_ref[0]
    for g in range(1, load_ref.shape[0]):
        total = total + load_ref[g]
    place = (out_ref.shape[0],) + total.shape
    out_ref[:, out_ref.shape[1] - total.shape[0] :, :] = jnp.broadcast_to(total[None], place)


def weight_kernel(teams, load_ref, halo_ref, norm_ref, gain_ref, bias_ref, out_ref, hidden, acc):
    time_index = lax.axis_index("tm")
    rows = load_ref.shape[1]
    cols = hidden.shape[2]
    chans = gain_ref.shape[1]
    wide = chans // TEAM
    step = chans // teams
    spot = time_index % TEAM
    lane = iota((chans, wide), 1)
    mover = (iota((chans, wide), 0) == lane // step * (step * TEAM) + spot * step + lane % step).astype(F32)

    def slice_of(value):
        return exact_dot(value, mover)[0:1]

    centre = slice_of(norm_ref[0:8])
    inverse = slice_of(norm_ref[8:16])
    gain = slice_of(jnp.broadcast_to(gain_ref[...], (8, chans)))
    bias = slice_of(jnp.broadcast_to(bias_ref[...], (8, chans)))

    def silu(value):
        preact = (value.astype(F32) - centre) * inverse * gain + bias
        return (preact * (1.0 / (1.0 + jnp.exp(-preact)))).astype(BF16)

    frames = 2 * TEAM
    for f in range(frames + 2):
        hidden[f, 0] = jnp.zeros(hidden.shape[2:], BF16)
        hidden[f, rows + 1] = jnp.zeros(hidden.shape[2:], BF16)
    opening = (time_index < TEAM).astype(F32)
    for j in range(TEAM):
        for r in range(rows):
            for f in range(2):
                value = silu(load_ref[j, r, f * cols : (f + 1) * cols, :])
                hidden[2 + 2 * j + f, 1 + r] = value
                if j == 0 and f == 0:
                    value = (value.astype(F32) * opening).astype(BF16)
                    hidden[0, 1 + r] = value
                    hidden[1, 1 + r] = value

    lanes = iota((cols, 128), 1) < 64
    more = (time_index < lax.axis_size("tm") - TEAM).astype(F32)
    for j in range(TEAM + 1):
        halves = [[], []]
        for r in range(rows):
            if j < TEAM:
                pair = load_ref[j, r, 2 * cols : 3 * cols, :].astype(F32)
            else:
                pair = halo_ref[r].astype(F32) * more
            row = iota(pair.shape, 0)
            ahead = jnp.where(row < cols - 1, pltpu.roll(pair, cols - 1, 0), 0.0)
            behind = jnp.where(row > 0, pltpu.roll(pair, 1, 0), 0.0)
            left = jnp.where(lanes, ahead, pltpu.roll(pair, 64, 1))
            right = jnp.where(lanes, pltpu.roll(ahead, 64, 1), pair)
            halves[0].append(jnp.concatenate([left, behind[:, 0:64]], axis=1))
            halves[1].append(jnp.concatenate([right, behind[:, 64:128]], axis=1))
        for f in range(2):
            ups = jnp.concatenate(halves[f], axis=0).astype(BF16)
            frame = 2 * j + f
            depth = min(3, frames + 2 - frame)
            taps = [
                hidden[frame + a, b : b + rows].reshape(rows * cols, wide) for a in range(depth) for b in range(3)
            ]
            term = lax.dot_general(
                ups, jnp.concatenate(taps, axis=1), (((0,), (0,)), ((), ())), preferred_element_type=F32
            )
            if frame == 0:
                acc[...] = term
            else:
                acc[:, 0 : 3 * depth * wide] += term

    groups = out_ref.shape[0]
    tail = None
    for ab in range(9):
        block = acc[:, ab * wide : (ab + 1) * wide].T
        out_ref[:, ab * step : (ab + 1) * step, :] = block[:, 0:128].reshape(groups, step, 128)
        last = block[:, 128:192]
        if ab % 2 == 0:
            tail = last
        if ab % 2 == 1 or ab == 8:
            both = jnp.concatenate([tail, last], axis=1)
            at = (9 + ab // 2) * step
            out_ref[:, at : at + step, :] = both.reshape(groups, step, 128)


def final_kernel(
    count, load_ref, act_ref, feats_ref, norm_ref, gain_ref, out_ref, grad_ref, gain_out_ref, bias_out_ref
):
    chans = gain_ref.shape[1]
    pieces = chans // 128
    step = grad_ref.shape[2]
    total = load_ref[0]
    for g in range(1, load_ref.shape[0]):
        total = total + load_ref[g]
    for ab in range(9):
        part = total[ab * step : (ab + 1) * step]
        grad_ref[ab, 0] = part[:, 0:64]
        grad_ref[ab, 1] = part[:, 64:128]
        at = (9 + ab // 2) * step
        side = 64 * (ab % 2)
        grad_ref[ab, 2] = total[at : at + step, side : side + 64]
    total = total[14 * step :]
    gains = jnp.concatenate([total[p : p + 1] for p in range(pieces)], axis=1)
    biases = jnp.concatenate([total[pieces + p : pieces + p + 1] for p in range(pieces)], axis=1)
    gain_out_ref[...] = gains
    bias_out_ref[...] = biases
    gain = gain_ref[...]
    owner = members(chans, 0)

    def spread(value):
        value = exact_dot(jnp.broadcast_to(value, (8, chans)), owner) / count
        return exact_dot(value, owner, ((1,), (1,)))[0:1]

    first = spread(gain * biases)
    second = spread(gain * gains)
    centre = norm_ref[0:1]
    inverse = norm_ref[8:9]
    normed = (feats_ref[...].astype(F32) - centre) * inverse
    out_ref[...] = (inverse * (act_ref[...] * gain - first - normed * second)).astype(BF16)


def on_device(features, norm_gain, norm_bias, weight, upstream):
    frames, rows_dev, cols, chans = features.shape
    outs = upstream.shape[3]
    tms = lax.axis_size("tm")
    rows = lax.axis_size("rows")
    devices = tms * rows
    positions = frames * rows_dev * cols
    step = chans // tms
    groups = tms // TEAM
    wide = chans // TEAM
    count = positions * devices * (chans // GROUPS)
    vmem = pl.BlockSpec(memory_space=pltpu.VMEM)

    def params(mebibytes):
        return pltpu.CompilerParams(vmem_limit_bytes=mebibytes * 1024 * 1024)

    feats = features.reshape(positions, chans)
    ups = upstream.reshape(frames, cols, outs)
    gain = norm_gain.reshape(1, chans)
    bias = norm_bias.reshape(1, chans)
    size = TEAM * rows
    length = positions + cols + 16
    teams = [[size * g + i for i in range(size)] for g in range(groups)]
    ranks = [[TEAM * g + j for g in range(groups)] for j in range(TEAM)]

    def in_teams(value):
        return lax.all_to_all(value, ("tm", "rows"), 0, 0, tiled=True, axis_index_groups=teams)

    def in_ranks(value):
        return lax.all_to_all(value, "tm", 0, 0, tiled=True, axis_index_groups=ranks)

    above = lax.ppermute(ups, "rows", [(i, (i + 1) % rows) for i in range(rows)])
    below = lax.ppermute(ups, "rows", [((i + 1) % rows, i) for i in range(rows)])

    load = pl.pallas_call(
        functools.partial(pack_kernel, tms),
        out_shape=jax.ShapeDtypeStruct((TEAM, rows, length, wide), BF16),
        compiler_params=params(62),
        name="pack",
    )(feats, ups)
    load = in_teams(load.reshape(size, length, wide)).reshape(TEAM, rows, length, wide)

    now = jnp.stack([above, ups, below])
    later = lax.ppermute(now, "tm", [((i + 1) % tms, i) for i in range(tms)])
    halo = lax.ppermute(
        load[0, :, positions : positions + cols], "tm", [((i + TEAM) % tms, i) for i in range(tms)]
    )

    def whole(shape):
        return pl.BlockSpec(shape, lambda *s: (0,) * len(shape))

    dense_call = pl.pallas_call(
        dense_kernel,
        grid=(9,),
        in_specs=[
            whole((3, frames, cols, outs)), whole((3, frames, cols, outs)),
            pl.BlockSpec((1, 1, 3, chans, outs), lambda s: (s // 3, s % 3, 0, 0, 0)),
        ],
        out_specs=whole((positions, chans)),
        out_shape=jax.ShapeDtypeStruct((positions, chans), F32),
        scratch_shapes=[pltpu.VMEM((3, 3, 4, cols, outs), BF16)],
        compiler_params=params(62),
        name="dense",
    )
    dense = dense_call(now, later, weight)

    stats = pl.pallas_call(
        functools.partial(combine_kernel, float(positions * (chans // GROUPS))),
        in_specs=[vmem],
        out_specs=vmem,
        out_shape=jax.ShapeDtypeStruct((groups, 8, 128), F32),
        compiler_params=params(16),
        name="combine",
    )(load)
    stats = in_ranks(stats)

    act, sums, norm = pl.pallas_call(
        functools.partial(act_kernel, positions * size),
        in_specs=[pl.BlockSpec(), pl.BlockSpec(), pl.BlockSpec(), vmem, pl.BlockSpec()],
        out_shape=(
            jax.ShapeDtypeStruct((positions, chans), F32),
            jax.ShapeDtypeStruct((size, 8, 128), F32),
            jax.ShapeDtypeStruct((16, chans), F32),
        ),
        compiler_params=params(62),
        name="act",
    )(feats, gain, bias, stats, dense)
    sums = in_teams(sums)

    weight_call = pl.pallas_call(
        functools.partial(weight_kernel, tms),
        in_specs=[vmem] + [pl.BlockSpec()] * 4,
        out_specs=vmem,
        out_shape=jax.ShapeDtypeStruct((groups, 14 * step + 8, 128), F32),
        scratch_shapes=[
            pltpu.VMEM((2 * TEAM + 2, rows + 2, cols, wide), BF16),
            pltpu.VMEM((3 * 64, 9 * wide), F32),
        ],
        compiler_params=params(61),
        name="wgrad",
    )
    part = weight_call(load, halo, norm, gain, bias)
    part = pl.pallas_call(
        append_kernel,
        in_specs=[vmem, vmem],
        out_specs=vmem,
        out_shape=jax.ShapeDtypeStruct((groups, 14 * step + 8, 128), F32),
        input_output_aliases={0: 0},
        compiler_params=params(16),
        name="append",
    )(part, sums)
    part = in_ranks(part)

    grad_features, grad_weight, grad_gain, grad_bias = pl.pallas_call(
        functools.partial(final_kernel, count),
        in_specs=[vmem] + [pl.BlockSpec()] * 4,
        out_shape=(
            jax.ShapeDtypeStruct((positions, chans), BF16),
            jax.ShapeDtypeStruct((9, 3, step, outs // rows), F32),
            jax.ShapeDtypeStruct((1, chans), F32),
            jax.ShapeDtypeStruct((1, chans), F32),
        ),
        compiler_params=params(16),
        name="final",
    )(part, act, feats, norm, gain)
    return (
        grad_features.reshape(features.shape),
        grad_weight.reshape(3, 3, 3, step, outs // rows),
        grad_gain.reshape(chans),
        grad_bias.reshape(chans),
    )


def solution(mesh):
    in_specs = (P("tm", "rows", None, None), P(), P(), P(), P("tm", "rows", None, None))
    out_specs = (P("tm", "rows", None, None), P(None, None, None, "tm", "rows"), P(), P())
    return jax.shard_map(on_device, mesh=mesh, in_specs=in_specs, out_specs=out_specs, check_vma=False)
```

```python
import functools

import jax
import jax.numpy as jnp
from jax import lax
from jax.experimental import pallas as pl
from jax.experimental.pallas import tpu as pltpu
from jax.sharding import PartitionSpec as P


GROUPS = 32
EPS = 1e-06
TEAM = 4
EDGES = ((0, -1), (0, 1), (1, 0), (1, -1), (1, 1))
F32 = jnp.float32
BF16 = jnp.bfloat16


def iota(shape, dim):
    return lax.broadcasted_iota(jnp.int32, shape, dim)


def shift_of(value):
    return value.bit_length() - 1


def exact_dot(a, ones, dims=((1,), (0,))):
    high = a.astype(BF16).astype(F32)
    rest = a - high
    mid = rest.astype(BF16).astype(F32)
    parts = jnp.concatenate([high, mid, rest - mid, jnp.zeros_like(a)], axis=0).astype(BF16)
    out = lax.dot_general(parts, ones, (dims, ((), ())), preferred_element_type=F32)
    return out[0:8] + out[8:16] + out[16:24]


def ones_where(mask):
    return jnp.where(mask, 1.0, 0.0).astype(BF16)


def members(chans, offset):
    bits = shift_of(chans // GROUPS)
    return ones_where(lax.shift_right_logical(iota((chans, 128), 0), bits) == iota((chans, 128), 1) - offset)


def sources(lane, chans, teams, spot):
    step = chans // teams
    return (lane & -step) * TEAM + spot * step + (lane & (step - 1))


def sigmoid(value):
    return 0.5 * jnp.tanh(0.5 * value) + 0.5


def col_shifts(slab):
    cols = slab.shape[0]
    wide = slab.astype(F32)
    row = iota(wide.shape, 0)
    ahead = jnp.where(row < cols - 1, pltpu.roll(wide, cols - 1, 0), 0.0).astype(BF16)
    behind = jnp.where(row > 0, pltpu.roll(wide, 1, 0), 0.0).astype(BF16)
    return ahead, slab, behind


def pack_kernel(teams, feats_ref, up_ref, load_ref):
    positions, chans = feats_ref.shape
    cols = up_ref.shape[1]
    rows = load_ref.shape[1]
    feats = feats_ref[...]
    wide = chans // TEAM
    lane = iota((1, chans), 1)
    source = sources(lane & (wide - 1), chans, teams, lax.shift_right_logical(lane, shift_of(wide)))
    mover = ones_where(iota((chans, chans), 0) == source)
    moved = jnp.dot(feats, mover, preferred_element_type=F32).astype(BF16)
    outs = up_ref.shape[2] // rows
    for r in range(rows):
        pair = jnp.concatenate(
            [up_ref[0, :, r * outs : (r + 1) * outs], up_ref[1, :, r * outs : (r + 1) * outs]], axis=1
        )
        for j in range(TEAM):
            load_ref[j, r, 0:positions, :] = moved[:, j * wide : (j + 1) * wide]
            load_ref[j, r, positions : positions + cols, :] = pair
    floats = feats.astype(F32)
    first = members(chans, 0)
    second = members(chans, GROUPS)
    total = jnp.broadcast_to(jnp.sum(floats, axis=0, keepdims=True), (8, chans))
    mean = exact_dot(total, first) / (positions * (chans // GROUPS))
    diffs = floats - exact_dot(mean, first, ((1,), (1,)))[0:1]
    squares = jnp.broadcast_to(jnp.sum(diffs * diffs, axis=0, keepdims=True), (8, chans))
    stat = mean + exact_dot(squares, second)
    high = stat.astype(BF16).astype(F32)
    mid = (stat - high).astype(BF16).astype(F32)
    low = stat - high - mid
    row = iota((8, 128), 0)
    parts = jnp.where(row == 0, high, jnp.where(row == 1, mid, jnp.where(row == 2, low, 0.0)))
    parts = jnp.concatenate([parts, jnp.zeros_like(parts)], axis=0).astype(BF16)
    for r in range(rows):
        for j in range(TEAM):
            load_ref[j, r, positions + cols :, :] = parts


def combine_kernel(count, load_ref, out_ref):
    stats = []
    for j in range(load_ref.shape[0]):
        for r in range(load_ref.shape[1]):
            parts = load_ref[j, r, load_ref.shape[2] - 16 :].astype(F32)
            stats.append(parts[0:1] + parts[1:2] + parts[2:3])
    total = stats[0]
    for stat in stats[1:]:
        total = total + stat
    mean = total / len(stats)
    spans = jnp.zeros_like(mean)
    for stat in stats:
        spans = spans + (stat - mean) * (stat - mean)
    lane = iota((8, 128), 1)
    moved = pltpu.roll(jnp.broadcast_to(spans, (8, 128)), GROUPS, 1)
    result = jnp.where(lane < GROUPS, jnp.broadcast_to(mean, (8, 128)), total + count * moved)
    out_ref[...] = jnp.broadcast_to(result[None], out_ref.shape)


def dense_kernel(
    up_ref, above_ref, below_ref, later_ref, later_above_ref, later_below_ref, weight_ref, out_ref, slabs
):
    step = pl.program_id(0)
    time_tap = step // 3
    row_tap = step % 3
    time_index = lax.axis_index("tm")
    row_index = lax.axis_index("rows")
    positions = out_ref.shape[0]
    cols = up_ref.shape[1]

    @pl.when(step == 0)
    def _():
        out_ref[...] = jnp.zeros_like(out_ref)
        more = (time_index < lax.axis_size("tm") - 1).astype(F32)
        up_ok = (row_index > 0).astype(F32)
        down_ok = (row_index < lax.axis_size("rows") - 1).astype(F32)
        for f in range(4):
            trio = (above_ref, up_ref, below_ref) if f < 2 else (later_above_ref, later_ref, later_below_ref)
            tail = jnp.float32(1.0) if f < 2 else more
            for r, keep in enumerate((up_ok, jnp.float32(1.0), down_ok)):
                slab = (trio[r][f % 2].astype(F32) * (keep * tail)).astype(BF16)
                for c, moved in enumerate(col_shifts(slab)):
                    slabs[c, r, f] = moved

    def product(slab, c):
        return lax.dot_general(
            slab, weight_ref[0, 0, c], (((1,), (1,)), ((), ())), preferred_element_type=F32
        )

    total = out_ref[...]
    for c in range(3):
        slab = slabs[c, 2 - row_tap, pl.ds(2 - time_tap, 2)].reshape(positions, -1)
        total = total + product(slab, c)
    out_ref[...] = total

    @pl.when(jnp.logical_and(time_index == 0, time_tap == 0))
    def _():
        for c in range(3):
            both = slabs[c, 2 - row_tap, pl.ds(0, 2)].reshape(positions, -1)
            both = product(both, c)
            out_ref[0:cols, :] += both[0:cols] + both[cols:]

    @pl.when(jnp.logical_and(time_index == 0, time_tap == 1))
    def _():
        for c in range(3):
            out_ref[0:cols, :] += product(slabs[c, 2 - row_tap, 0], c)


def norm_rows(stats_ref, chans, positions):
    stats = jnp.concatenate([stats_ref[g, 0:1] for g in range(stats_ref.shape[0])], axis=0)
    devices = stats.shape[0]
    size = chans // GROUPS
    first = members(chans, 0)
    second = members(chans, GROUPS)
    total = jnp.sum(stats, axis=0, keepdims=True)
    centre = total / devices
    spans = stats - centre
    spans = jnp.sum(spans * spans, axis=0, keepdims=True)
    dims = ((1,), (1,))
    parts = exact_dot(jnp.broadcast_to(total, (8, 128)), second, dims) / (devices * positions * size)
    parts = parts + exact_dot(jnp.broadcast_to(spans, (8, 128)), first, dims) / devices
    inverse = lax.rsqrt(parts + EPS)
    centre = exact_dot(jnp.broadcast_to(centre, (8, 128)), first, dims)
    return centre, inverse


def act_kernel(positions, feats_ref, gain_ref, bias_ref, stats_ref, dense_ref, act_ref, sums_ref, norm_ref):
    chans = gain_ref.shape[1]
    centre, inverse = norm_rows(stats_ref, chans, positions)
    norm_ref[0:8] = centre
    norm_ref[8:16] = inverse
    centre = centre[0:1]
    inverse = inverse[0:1]
    normed = (feats_ref[...].astype(F32) - centre) * inverse
    preact = normed * gain_ref[...] + bias_ref[...]
    sig = sigmoid(preact)
    act = dense_ref[...] * sig * (1.0 + preact * (1.0 - sig))
    act_ref[...] = act
    gains = jnp.sum(act * normed, axis=0, keepdims=True)
    biases = jnp.sum(act, axis=0, keepdims=True)
    pieces = chans // 128
    rows = [gains[:, p * 128 : (p + 1) * 128] for p in range(pieces)]
    rows = rows + [biases[:, p * 128 : (p + 1) * 128] for p in range(pieces)]
    sums_ref[...] = jnp.broadcast_to(jnp.concatenate(rows, axis=0)[None], sums_ref.shape)


def append_kernel(part_ref, load_ref, out_ref):
    total = load_ref[0]
    for g in range(1, load_ref.shape[0]):
        total = total + load_ref[g]
    place = (out_ref.shape[0],) + total.shape
    out_ref[:, out_ref.shape[1] - total.shape[0] :, :] = jnp.broadcast_to(total[None], place)


def weight_kernel(teams, load_ref, halo_ref, norm_ref, gain_ref, bias_ref, out_ref, hidden, acc):
    time_index = lax.axis_index("tm")
    rows = load_ref.shape[1]
    cols = hidden.shape[2]
    chans = gain_ref.shape[1]
    wide = chans // TEAM
    step = chans // teams
    mover = ones_where(
        iota((chans, wide), 0) == sources(iota((1, wide), 1), chans, teams, time_index & (TEAM - 1))
    )

    def slice_of(value):
        return exact_dot(value, mover)[0:1]

    centre = slice_of(norm_ref[0:8])
    inverse = slice_of(norm_ref[8:16])
    gain = slice_of(jnp.broadcast_to(gain_ref[...], (8, chans)))
    bias = slice_of(jnp.broadcast_to(bias_ref[...], (8, chans)))

    def silu(value):
        preact = (value.astype(F32) - centre) * inverse * gain + bias
        return (preact * sigmoid(preact)).astype(BF16)

    frames = 2 * TEAM
    for f in range(frames + 2):
        hidden[f, 0] = jnp.zeros(hidden.shape[2:], BF16)
        hidden[f, rows + 1] = jnp.zeros(hidden.shape[2:], BF16)
    opening = (time_index < TEAM).astype(F32)
    for j in range(TEAM):
        for r in range(rows):
            for f in range(2):
                value = silu(load_ref[j, r, f * cols : (f + 1) * cols, :])
                hidden[2 + 2 * j + f, 1 + r] = value
                if j == 0 and f == 0:
                    value = (value.astype(F32) * opening).astype(BF16)
                    hidden[0, 1 + r] = value
                    hidden[1, 1 + r] = value

    lanes = iota((cols, 128), 1) < 64
    more = (time_index < lax.axis_size("tm") - TEAM).astype(F32)
    for j in range(TEAM + 1):
        halves = [[], []]
        for r in range(rows):
            if j < TEAM:
                pair = load_ref[j, r, 2 * cols : 3 * cols, :].astype(F32)
            else:
                pair = halo_ref[r].astype(F32) * more
            row = iota(pair.shape, 0)
            ahead = jnp.where(row < cols - 1, pltpu.roll(pair, cols - 1, 0), 0.0)
            behind = jnp.where(row > 0, pltpu.roll(pair, 1, 0), 0.0)
            left = jnp.where(lanes, ahead, pltpu.roll(pair, 64, 1))
            right = jnp.where(lanes, pltpu.roll(ahead, 64, 1), pair)
            halves[0].append(jnp.concatenate([left, behind[:, 0:64]], axis=1))
            halves[1].append(jnp.concatenate([right, behind[:, 64:128]], axis=1))
        for f in range(2):
            ups = jnp.concatenate(halves[f], axis=0).astype(BF16)
            frame = 2 * j + f
            depth = min(3, frames + 2 - frame)
            taps = [
                hidden[frame + a, b : b + rows].reshape(rows * cols, wide) for a in range(depth) for b in range(3)
            ]
            term = lax.dot_general(
                ups, jnp.concatenate(taps, axis=1), (((0,), (0,)), ((), ())), preferred_element_type=F32
            )
            if frame == 0:
                acc[...] = term
            else:
                acc[:, 0 : 3 * depth * wide] += term

    groups = out_ref.shape[0]
    tail = None
    for ab in range(9):
        block = acc[:, ab * wide : (ab + 1) * wide].T
        out_ref[:, ab * step : (ab + 1) * step, :] = block[:, 0:128].reshape(groups, step, 128)
        last = block[:, 128:192]
        if ab % 2 == 0:
            tail = last
        if ab % 2 == 1 or ab == 8:
            both = jnp.concatenate([tail, last], axis=1)
            at = (9 + ab // 2) * step
            out_ref[:, at : at + step, :] = both.reshape(groups, step, 128)


def final_kernel(
    count, load_ref, act_ref, feats_ref, norm_ref, gain_ref, out_ref, grad_ref, gain_out_ref, bias_out_ref
):
    chans = gain_ref.shape[1]
    pieces = chans // 128
    step = grad_ref.shape[2]
    total = load_ref[0]
    for g in range(1, load_ref.shape[0]):
        total = total + load_ref[g]
    for ab in range(9):
        part = total[ab * step : (ab + 1) * step]
        grad_ref[ab, 0] = part[:, 0:64]
        grad_ref[ab, 1] = part[:, 64:128]
        at = (9 + ab // 2) * step
        side = 64 * (ab % 2)
        grad_ref[ab, 2] = total[at : at + step, side : side + 64]
    total = total[14 * step :]
    gains = jnp.concatenate([total[p : p + 1] for p in range(pieces)], axis=1)
    biases = jnp.concatenate([total[pieces + p : pieces + p + 1] for p in range(pieces)], axis=1)
    gain_out_ref[...] = gains
    bias_out_ref[...] = biases
    gain = gain_ref[...]
    owner = members(chans, 0)

    def spread(value):
        value = exact_dot(jnp.broadcast_to(value, (8, chans)), owner) / count
        return exact_dot(value, owner, ((1,), (1,)))[0:1]

    first = spread(gain * biases)
    second = spread(gain * gains)
    centre = norm_ref[0:1]
    inverse = norm_ref[8:9]
    normed = (feats_ref[...].astype(F32) - centre) * inverse
    out_ref[...] = (inverse * (act_ref[...] * gain - first - normed * second)).astype(BF16)


def on_device(features, norm_gain, norm_bias, weight, upstream):
    frames, rows_dev, cols, chans = features.shape
    outs = upstream.shape[3]
    tms = lax.axis_size("tm")
    rows = lax.axis_size("rows")
    devices = tms * rows
    positions = frames * rows_dev * cols
    step = chans // tms
    groups = tms // TEAM
    wide = chans // TEAM
    count = positions * devices * (chans // GROUPS)
    vmem = pl.BlockSpec(memory_space=pltpu.VMEM)

    def params(mebibytes):
        return pltpu.CompilerParams(vmem_limit_bytes=mebibytes * 1024 * 1024)

    feats = features.reshape(positions, chans)
    ups = upstream.reshape(frames, cols, outs)
    gain = norm_gain.reshape(1, chans)
    bias = norm_bias.reshape(1, chans)
    size = TEAM * rows
    length = positions + cols + 16
    teams = [[size * g + i for i in range(size)] for g in range(groups)]
    ranks = [[TEAM * g + j for g in range(groups)] for j in range(TEAM)]

    def in_teams(value):
        return lax.all_to_all(value, ("tm", "rows"), 0, 0, tiled=True, axis_index_groups=teams)

    def in_ranks(value):
        return lax.all_to_all(value, "tm", 0, 0, tiled=True, axis_index_groups=ranks)

    def neighbour(tm_step, row_step):
        pairs = [
            (((t + tm_step) % tms) * rows + (r + row_step) % rows, t * rows + r)
            for t in range(tms)
            for r in range(rows)
        ]
        return lax.ppermute(ups, ("tm", "rows"), pairs)

    halos = [neighbour(a, b) for a, b in EDGES]

    load = pl.pallas_call(
        functools.partial(pack_kernel, tms),
        out_shape=jax.ShapeDtypeStruct((TEAM, rows, length, wide), BF16),
        compiler_params=params(62),
        name="pack",
    )(feats, ups)
    load = in_teams(load.reshape(size, length, wide)).reshape(TEAM, rows, length, wide)

    halo = lax.ppermute(
        load[0, :, positions : positions + cols], "tm", [((i + TEAM) % tms, i) for i in range(tms)]
    )

    def whole(shape):
        return pl.BlockSpec(shape, lambda *s: (0,) * len(shape))

    dense_call = pl.pallas_call(
        dense_kernel,
        grid=(9,),
        in_specs=[
            *[whole((frames, cols, outs))] * 6,
            pl.BlockSpec((1, 1, 3, chans, outs), lambda s: (s // 3, s % 3, 0, 0, 0)),
        ],
        out_specs=whole((positions, chans)),
        out_shape=jax.ShapeDtypeStruct((positions, chans), F32),
        scratch_shapes=[pltpu.VMEM((3, 3, 4, cols, outs), BF16)],
        compiler_params=params(62),
        name="dense",
    )
    dense = dense_call(ups, *halos, weight)

    stats = pl.pallas_call(
        functools.partial(combine_kernel, float(positions * (chans // GROUPS))),
        in_specs=[vmem],
        out_specs=vmem,
        out_shape=jax.ShapeDtypeStruct((groups, 8, 128), F32),
        compiler_params=params(16),
        name="combine",
    )(load)
    stats = in_ranks(stats)

    act, sums, norm = pl.pallas_call(
        functools.partial(act_kernel, positions * size),
        in_specs=[pl.BlockSpec(), pl.BlockSpec(), pl.BlockSpec(), vmem, pl.BlockSpec()],
        out_shape=(
            jax.ShapeDtypeStruct((positions, chans), F32),
            jax.ShapeDtypeStruct((size, 8, 128), F32),
            jax.ShapeDtypeStruct((16, chans), F32),
        ),
        compiler_params=params(62),
        name="act",
    )(feats, gain, bias, stats, dense)
    sums = in_teams(sums)

    weight_call = pl.pallas_call(
        functools.partial(weight_kernel, tms),
        in_specs=[vmem] + [pl.BlockSpec()] * 4,
        out_specs=vmem,
        out_shape=jax.ShapeDtypeStruct((groups, 14 * step + 8, 128), F32),
        scratch_shapes=[
            pltpu.VMEM((2 * TEAM + 2, rows + 2, cols, wide), BF16),
            pltpu.VMEM((3 * 64, 9 * wide), F32),
        ],
        compiler_params=params(61),
        name="wgrad",
    )
    part = weight_call(load, halo, norm, gain, bias)
    part = pl.pallas_call(
        append_kernel,
        in_specs=[vmem, vmem],
        out_specs=vmem,
        out_shape=jax.ShapeDtypeStruct((groups, 14 * step + 8, 128), F32),
        input_output_aliases={0: 0},
        compiler_params=params(16),
        name="append",
    )(part, sums)
    part = in_ranks(part)

    grad_features, grad_weight, grad_gain, grad_bias = pl.pallas_call(
        functools.partial(final_kernel, count),
        in_specs=[vmem] + [pl.BlockSpec()] * 4,
        out_shape=(
            jax.ShapeDtypeStruct((positions, chans), BF16),
            jax.ShapeDtypeStruct((9, 3, step, outs // rows), F32),
            jax.ShapeDtypeStruct((1, chans), F32),
            jax.ShapeDtypeStruct((1, chans), F32),
        ),
        compiler_params=params(16),
        name="final",
    )(part, act, feats, norm, gain)
    return (
        grad_features.reshape(features.shape),
        grad_weight.reshape(3, 3, 3, step, outs // rows),
        grad_gain.reshape(chans),
        grad_bias.reshape(chans),
    )


def solution(mesh):
    in_specs = (P("tm", "rows", None, None), P(), P(), P(), P("tm", "rows", None, None))
    out_specs = (P("tm", "rows", None, None), P(None, None, None, "tm", "rows"), P(), P())
    return jax.shard_map(on_device, mesh=mesh, in_specs=in_specs, out_specs=out_specs, check_vma=False)
```

```python
import functools

import jax
import jax.numpy as jnp
from jax import lax
from jax.experimental import pallas as pl
from jax.experimental.pallas import tpu as pltpu
from jax.sharding import PartitionSpec as P


GROUPS = 32
EPS = 1e-06
TEAM = 4
EDGES = ((0, -1), (0, 1), (1, 0), (1, -1), (1, 1))
F32 = jnp.float32
BF16 = jnp.bfloat16


def iota(shape, dim):
    return lax.broadcasted_iota(jnp.int32, shape, dim)


def shift_of(value):
    return value.bit_length() - 1


def exact_dot(a, ones, dims=((1,), (0,))):
    high = a.astype(BF16).astype(F32)
    rest = a - high
    mid = rest.astype(BF16).astype(F32)
    parts = jnp.concatenate([high, mid, rest - mid, jnp.zeros_like(a)], axis=0).astype(BF16)
    out = lax.dot_general(parts, ones, (dims, ((), ())), preferred_element_type=F32)
    return out[0:8] + out[8:16] + out[16:24]


def ones_where(mask):
    return jnp.where(mask, 1.0, 0.0).astype(BF16)


def members(chans, offset):
    bits = shift_of(chans // GROUPS)
    return ones_where(lax.shift_right_logical(iota((chans, 128), 0), bits) == iota((chans, 128), 1) - offset)


def sources(lane, step, chip, core):
    owner = lax.shift_right_logical(lane, shift_of(step))
    place = lax.shift_right_logical(owner, 2) * 32 + (owner & 3) * 4
    place = place + lax.shift_right_logical(chip, 1) * 16 + (chip & 1) * 2 + core
    return place * step + (lane & (step - 1))


def sigmoid(value):
    return 0.5 * jnp.tanh(0.5 * value) + 0.5


def col_shifts(slab):
    cols = slab.shape[0]
    wide = slab.astype(F32)
    row = iota(wide.shape, 0)
    ahead = jnp.where(row < cols - 1, pltpu.roll(wide, cols - 1, 0), 0.0).astype(BF16)
    behind = jnp.where(row > 0, pltpu.roll(wide, 1, 0), 0.0).astype(BF16)
    return ahead, slab, behind


def pack_kernel(teams, feats_ref, up_ref, load_ref):
    positions, chans = feats_ref.shape
    cols = up_ref.shape[1]
    rows = load_ref.shape[1]
    feats = feats_ref[...]
    core = lax.axis_index("tm") & 1
    lane = iota((1, chans), 1)
    source = sources(
        lane & 63, chans // teams, lax.shift_right_logical(lane, 7), lax.shift_right_logical(lane, 6) & 1
    )
    mover = ones_where(iota((chans, chans), 0) == source)
    moved = jnp.dot(feats, mover, preferred_element_type=F32)
    outs = up_ref.shape[2] // rows
    left = iota((cols, 128), 1) < 64
    for j in range(TEAM):
        early = moved[0:cols, j * 128 : (j + 1) * 128]
        late = moved[cols:, j * 128 : (j + 1) * 128]
        lower = jnp.where(left, early, pltpu.roll(late, 64, 1)).astype(BF16)
        upper = jnp.where(left, pltpu.roll(early, 64, 1), late).astype(BF16)
        keep = jnp.where(core == 0, lower, upper)
        send = jnp.where(core == 0, upper, lower)
        for r in range(rows):
            load_ref[j, r, 0:cols, :] = keep
            load_ref[j, r, cols : 2 * cols, :] = send
    for r in range(rows):
        pair = jnp.concatenate(
            [up_ref[0, :, r * outs : (r + 1) * outs], up_ref[1, :, r * outs : (r + 1) * outs]], axis=1
        )
        for j in range(TEAM):
            load_ref[j, r, 2 * cols : 3 * cols, :] = pair
    floats = feats.astype(F32)
    first = members(chans, 0)
    second = members(chans, GROUPS)
    total = jnp.broadcast_to(jnp.sum(floats, axis=0, keepdims=True), (8, chans))
    mean = exact_dot(total, first) / (positions * (chans // GROUPS))
    diffs = floats - exact_dot(mean, first, ((1,), (1,)))[0:1]
    squares = jnp.broadcast_to(jnp.sum(diffs * diffs, axis=0, keepdims=True), (8, chans))
    stat = mean + exact_dot(squares, second)
    high = stat.astype(BF16).astype(F32)
    mid = (stat - high).astype(BF16).astype(F32)
    low = stat - high - mid
    row = iota((8, 128), 0)
    parts = jnp.where(row == 0, high, jnp.where(row == 1, mid, jnp.where(row == 2, low, 0.0)))
    parts = jnp.concatenate([parts, jnp.zeros_like(parts)], axis=0).astype(BF16)
    for r in range(rows):
        for j in range(TEAM):
            load_ref[j, r, 3 * cols :, :] = parts


def combine_kernel(count, load_ref, out_ref):
    stats = []
    for j in range(load_ref.shape[0]):
        for r in range(load_ref.shape[1]):
            parts = load_ref[j, r, load_ref.shape[2] - 16 :].astype(F32)
            stats.append(parts[0:1] + parts[1:2] + parts[2:3])
    total = stats[0]
    for stat in stats[1:]:
        total = total + stat
    mean = total / len(stats)
    spans = jnp.zeros_like(mean)
    for stat in stats:
        spans = spans + (stat - mean) * (stat - mean)
    lane = iota((8, 128), 1)
    moved = pltpu.roll(jnp.broadcast_to(spans, (8, 128)), GROUPS, 1)
    result = jnp.where(lane < GROUPS, jnp.broadcast_to(mean, (8, 128)), total + count * moved)
    out_ref[...] = jnp.broadcast_to(result[None], out_ref.shape)


def dense_kernel(
    up_ref, above_ref, below_ref, later_ref, later_above_ref, later_below_ref, weight_ref, out_ref, slabs
):
    step = pl.program_id(0)
    time_tap = step // 3
    row_tap = step % 3
    time_index = lax.axis_index("tm")
    row_index = lax.axis_index("rows")
    positions = out_ref.shape[0]
    cols = up_ref.shape[1]

    @pl.when(step == 0)
    def _():
        out_ref[...] = jnp.zeros_like(out_ref)
        more = (time_index < lax.axis_size("tm") - 1).astype(F32)
        up_ok = (row_index > 0).astype(F32)
        down_ok = (row_index < lax.axis_size("rows") - 1).astype(F32)
        for f in range(4):
            trio = (above_ref, up_ref, below_ref) if f < 2 else (later_above_ref, later_ref, later_below_ref)
            tail = jnp.float32(1.0) if f < 2 else more
            for r, keep in enumerate((up_ok, jnp.float32(1.0), down_ok)):
                slab = (trio[r][f % 2].astype(F32) * (keep * tail)).astype(BF16)
                for c, moved in enumerate(col_shifts(slab)):
                    slabs[c, r, f] = moved

    def product(slab, c):
        return lax.dot_general(
            slab, weight_ref[0, 0, c], (((1,), (1,)), ((), ())), preferred_element_type=F32
        )

    total = out_ref[...]
    for c in range(3):
        slab = slabs[c, 2 - row_tap, pl.ds(2 - time_tap, 2)].reshape(positions, -1)
        total = total + product(slab, c)
    out_ref[...] = total

    @pl.when(jnp.logical_and(time_index == 0, time_tap == 0))
    def _():
        for c in range(3):
            both = slabs[c, 2 - row_tap, pl.ds(0, 2)].reshape(positions, -1)
            both = product(both, c)
            out_ref[0:cols, :] += both[0:cols] + both[cols:]

    @pl.when(jnp.logical_and(time_index == 0, time_tap == 1))
    def _():
        for c in range(3):
            out_ref[0:cols, :] += product(slabs[c, 2 - row_tap, 0], c)


def norm_rows(stats_ref, chans, positions):
    stats = jnp.concatenate([stats_ref[g, 0:1] for g in range(stats_ref.shape[0])], axis=0)
    devices = stats.shape[0]
    size = chans // GROUPS
    first = members(chans, 0)
    second = members(chans, GROUPS)
    total = jnp.sum(stats, axis=0, keepdims=True)
    centre = total / devices
    spans = stats - centre
    spans = jnp.sum(spans * spans, axis=0, keepdims=True)
    dims = ((1,), (1,))
    parts = exact_dot(jnp.broadcast_to(total, (8, 128)), second, dims) / (devices * positions * size)
    parts = parts + exact_dot(jnp.broadcast_to(spans, (8, 128)), first, dims) / devices
    inverse = lax.rsqrt(parts + EPS)
    centre = exact_dot(jnp.broadcast_to(centre, (8, 128)), first, dims)
    return centre, inverse


def act_kernel(positions, feats_ref, gain_ref, bias_ref, stats_ref, dense_ref, act_ref, sums_ref, norm_ref):
    chans = gain_ref.shape[1]
    centre, inverse = norm_rows(stats_ref, chans, positions)
    norm_ref[0:8] = centre
    norm_ref[8:16] = inverse
    centre = centre[0:1]
    inverse = inverse[0:1]
    normed = (feats_ref[...].astype(F32) - centre) * inverse
    preact = normed * gain_ref[...] + bias_ref[...]
    sig = sigmoid(preact)
    act = dense_ref[...] * sig * (1.0 + preact * (1.0 - sig))
    act_ref[...] = act
    gains = jnp.sum(act * normed, axis=0, keepdims=True)
    biases = jnp.sum(act, axis=0, keepdims=True)
    pieces = chans // 128
    rows = [gains[:, p * 128 : (p + 1) * 128] for p in range(pieces)]
    rows = rows + [biases[:, p * 128 : (p + 1) * 128] for p in range(pieces)]
    sums_ref[...] = jnp.broadcast_to(jnp.concatenate(rows, axis=0)[None], sums_ref.shape)


def append_kernel(part_ref, load_ref, out_ref):
    total = load_ref[0]
    for g in range(1, load_ref.shape[0]):
        total = total + load_ref[g]
    place = (out_ref.shape[0],) + total.shape
    out_ref[:, out_ref.shape[1] - total.shape[0] :, :] = jnp.broadcast_to(total[None], place)


def weight_kernel(
    teams, load_ref, other_ref, halo0_ref, halo1_ref, moved0_ref, moved1_ref, norm_ref, gain_ref, bias_ref,
    out_ref, hidden, acc,
):
    time_index = lax.axis_index("tm")
    core = time_index & 1
    rows = load_ref.shape[1]
    cols = hidden.shape[3]
    chans = gain_ref.shape[1]
    step = chans // teams
    chip = (lax.shift_right_logical(time_index, 4) & 1) * 2 + (lax.shift_right_logical(time_index, 1) & 1)
    mover = ones_where(iota((chans, 128), 0) == sources(iota((1, 128), 1) & 63, step, chip, core))

    def slice_of(value):
        return exact_dot(value, mover)[0:1]

    centre = slice_of(norm_ref[0:8])
    inverse = slice_of(norm_ref[8:16])
    gain = slice_of(jnp.broadcast_to(gain_ref[...], (8, chans)))
    bias = slice_of(jnp.broadcast_to(bias_ref[...], (8, chans)))
    left = iota((cols, 128), 1) < 64
    start = (time_index & ~19) == 0
    end = (time_index | 19) == lax.axis_size("tm") - 1

    for x in range(2):
        for q in range(6):
            hidden[x, q, 0] = jnp.zeros(hidden.shape[3:], BF16)
            hidden[x, q, rows + 1] = jnp.zeros(hidden.shape[3:], BF16)
        for q in range(4):
            for r in range(rows):
                j = 2 * x + q // 2
                pair = jnp.where(core == q % 2, load_ref[j, r, 0:cols, :], other_ref[j, r, 0:cols, :])
                preact = (pair.astype(F32) - centre) * inverse * gain + bias
                value = preact * sigmoid(preact)
                hidden[x, q + 1, r + 1] = value.astype(BF16)
                if q == 0:
                    before = jnp.zeros_like(value)
                    if x == 0:
                        before = jnp.where(start, jnp.where(left, value, pltpu.roll(value, 64, 1)), before)
                    hidden[x, 0, r + 1] = before.astype(BF16)
                    hidden[x, 5, r + 1] = jnp.zeros(hidden.shape[3:], BF16)

    for x in range(2):
        for q in range(5):
            sides = [[], [], []]
            for r in range(rows):
                j = 2 * x + q // 2
                if q < 4:
                    pair = jnp.where(
                        core == q % 2, load_ref[j, r, 2 * cols : 3 * cols, :], other_ref[j, r, cols : 2 * cols, :]
                    )
                else:
                    near, far = ((halo0_ref, moved0_ref), (halo1_ref, moved1_ref))[x]
                    pair = jnp.where(core == 0, near[r], far[r])
                wide = pair.astype(F32)
                if q == 4 and x == 1:
                    wide = jnp.where(end, 0.0, wide)
                row = iota(wide.shape, 0)
                sides[0].append(jnp.where(row < cols - 1, pltpu.roll(wide, cols - 1, 0), 0.0).astype(BF16))
                sides[1].append(wide.astype(BF16))
                sides[2].append(jnp.where(row > 0, pltpu.roll(wide, 1, 0), 0.0).astype(BF16))
            ups = jnp.concatenate([jnp.concatenate(side, axis=0) for side in sides], axis=1)
            taps = [
                hidden[x, q + n, b : b + rows].reshape(rows * cols, 128) for b in range(3) for n in range(2)
            ]
            term = lax.dot_general(
                ups, jnp.concatenate(taps, axis=1), (((0,), (0,)), ((), ())), preferred_element_type=F32
            )
            if x == 0 and q == 0:
                acc[...] = term
            else:
                acc[...] += term

    groups = out_ref.shape[0]
    low = iota((192, 128), 1) < 64

    def store(index, block):
        out_ref[:, index * step : (index + 1) * step, :] = block.reshape(groups, step, 128)

    thirds = []
    for b in range(3):
        blocks = [acc[c * 128 : (c + 1) * 128, b * 256 : (b + 1) * 256].T for c in range(3)]
        first = blocks[0][0:192] + pltpu.roll(blocks[0][64:256], 64, 1)
        second = pltpu.roll(blocks[1][0:192], 64, 1) + blocks[1][64:256]
        both = jnp.where(low, first, second)
        for a in range(3):
            store(3 * a + b, both[a * 64 : (a + 1) * 64])
        thirds.append(blocks[2][0:192] + pltpu.roll(blocks[2][64:256], 64, 1))
    both = jnp.where(low, thirds[0], pltpu.roll(thirds[1], 64, 1))
    for a in range(3):
        store(9 + a, both[a * 64 : (a + 1) * 64])
    store(12, jnp.where(low[0:64], thirds[2][0:64], pltpu.roll(thirds[2][64:128], 64, 1)))
    store(13, thirds[2][128:192])


def final_kernel(
    count, load_ref, act_ref, feats_ref, norm_ref, gain_ref, out_ref, grad_ref, gain_out_ref, bias_out_ref
):
    chans = gain_ref.shape[1]
    pieces = chans // 128
    step = grad_ref.shape[2]
    total = load_ref[0]
    for g in range(1, load_ref.shape[0]):
        total = total + load_ref[g]
    for a in range(3):
        for b in range(3):
            part = total[(3 * a + b) * step : (3 * a + b + 1) * step]
            grad_ref[3 * a + b, 0] = part[:, 0:64]
            grad_ref[3 * a + b, 1] = part[:, 64:128]
            index = 9 + a if b < 2 else 12 + a // 2
            side = 64 * (b if b < 2 else a % 2)
            grad_ref[3 * a + b, 2] = total[index * step : (index + 1) * step, side : side + 64]
    total = total[14 * step :]
    gains = jnp.concatenate([total[p : p + 1] for p in range(pieces)], axis=1)
    biases = jnp.concatenate([total[pieces + p : pieces + p + 1] for p in range(pieces)], axis=1)
    gain_out_ref[...] = gains
    bias_out_ref[...] = biases
    gain = gain_ref[...]
    owner = members(chans, 0)

    def spread(value):
        value = exact_dot(jnp.broadcast_to(value, (8, chans)), owner) / count
        return exact_dot(value, owner, ((1,), (1,)))[0:1]

    first = spread(gain * biases)
    second = spread(gain * gains)
    centre = norm_ref[0:1]
    inverse = norm_ref[8:9]
    normed = (feats_ref[...].astype(F32) - centre) * inverse
    out_ref[...] = (inverse * (act_ref[...] * gain - first - normed * second)).astype(BF16)


def on_device(features, norm_gain, norm_bias, weight, upstream):
    frames, rows_dev, cols, chans = features.shape
    outs = upstream.shape[3]
    tms = lax.axis_size("tm")
    rows = lax.axis_size("rows")
    devices = tms * rows
    positions = frames * rows_dev * cols
    step = chans // tms
    groups = tms // (2 * TEAM)
    wide = chans // TEAM
    count = positions * devices * (chans // GROUPS)
    vmem = pl.BlockSpec(memory_space=pltpu.VMEM)

    def params(mebibytes):
        return pltpu.CompilerParams(vmem_limit_bytes=mebibytes * 1024 * 1024)

    feats = features.reshape(positions, chans)
    ups = upstream.reshape(frames, cols, outs)
    gain = norm_gain.reshape(1, chans)
    bias = norm_bias.reshape(1, chans)
    size = TEAM * rows
    length = positions + cols + 16
    places = [(big, z) for big in range(groups // 4) for z in range(4)]
    chips = [(x, z) for x in range(2) for z in range(2)]

    def place(outer, inner, core):
        return outer[0] * 32 + inner[0] * 16 + outer[1] * 4 + inner[1] * 2 + core

    every = range(rows)
    teams = [[place(o, i, c) * rows + r for i in chips for r in every] for o in places for c in range(2)]
    pairs = [[place(o, i, c) * rows + r for i in chips for c in range(2) for r in every] for o in places]
    stars = [[place(o, i, c) for o in places for c in range(2)] for i in chips]
    ranks = [[place(o, i, c) for o in places] for i in chips for c in range(2)]

    def in_teams(value):
        return lax.all_to_all(value, ("tm", "rows"), 0, 0, tiled=True, axis_index_groups=teams)

    def in_pairs(value):
        return lax.all_to_all(value, ("tm", "rows"), 0, 0, tiled=True, axis_index_groups=pairs)

    def in_stars(value):
        return lax.all_to_all(value, "tm", 0, 0, tiled=True, axis_index_groups=stars)

    def in_ranks(value):
        return lax.all_to_all(value, "tm", 0, 0, tiled=True, axis_index_groups=ranks)

    def neighbour(tm_step, row_step):
        moves = [
            (((t + tm_step) % tms) * rows + (r + row_step) % rows, t * rows + r)
            for t in range(tms)
            for r in range(rows)
        ]
        return lax.ppermute(ups, ("tm", "rows"), moves)

    halos = [neighbour(a, b) for a, b in EDGES]

    load = pl.pallas_call(
        functools.partial(pack_kernel, tms),
        out_shape=jax.ShapeDtypeStruct((TEAM, rows, length, wide), BF16),
        compiler_params=params(62),
        name="pack",
    )(feats, ups)
    load = in_teams(load.reshape(size, length, wide)).reshape(TEAM, rows, length, wide)

    other = lax.ppermute(load[:, :, cols : 3 * cols], "tm", [(t, t ^ 1) for t in range(tms)])
    opens = lax.shift_right_logical(lax.axis_index("tm"), 2) & 3 == 0
    runs = [load[2 * x, :, 2 * cols : 3 * cols] for x in range(2)]
    halo = []
    for x in range(2):
        moves = []
        for o in places:
            goal = (o[0], o[1] + 1) if o[1] < 3 else ((o[0] + x) % (groups // 4), 0)
            moves += [(place(goal, i, 0), place(o, i, 0)) for i in chips]
        halo.append(lax.ppermute(jnp.where(opens, runs[1 - x], runs[x]), "tm", moves))
    for x in range(2):
        halo.append(lax.ppermute(halo[x], "tm", [(t, t + 1) for t in range(0, tms, 2)]))

    def whole(shape):
        return pl.BlockSpec(shape, lambda *s: (0,) * len(shape))

    dense_call = pl.pallas_call(
        dense_kernel,
        grid=(9,),
        in_specs=[
            *[whole((frames, cols, outs))] * 6,
            pl.BlockSpec((1, 1, 3, chans, outs), lambda s: (s // 3, s % 3, 0, 0, 0)),
        ],
        out_specs=whole((positions, chans)),
        out_shape=jax.ShapeDtypeStruct((positions, chans), F32),
        scratch_shapes=[pltpu.VMEM((3, 3, 4, cols, outs), BF16)],
        compiler_params=params(62),
        name="dense",
    )
    dense = dense_call(ups, *halos, weight)

    stats = pl.pallas_call(
        functools.partial(combine_kernel, float(positions * (chans // GROUPS))),
        in_specs=[vmem],
        out_specs=vmem,
        out_shape=jax.ShapeDtypeStruct((2 * groups, 8, 128), F32),
        compiler_params=params(16),
        name="combine",
    )(load)
    stats = in_stars(stats)

    act, sums, norm = pl.pallas_call(
        functools.partial(act_kernel, positions * size),
        in_specs=[pl.BlockSpec(), pl.BlockSpec(), pl.BlockSpec(), vmem, pl.BlockSpec()],
        out_shape=(
            jax.ShapeDtypeStruct((positions, chans), F32),
            jax.ShapeDtypeStruct((2 * size, 8, 128), F32),
            jax.ShapeDtypeStruct((16, chans), F32),
        ),
        compiler_params=params(62),
        name="act",
    )(feats, gain, bias, stats, dense)
    sums = in_pairs(sums)

    weight_call = pl.pallas_call(
        functools.partial(weight_kernel, tms),
        in_specs=[vmem] + [pl.BlockSpec()] * 8,
        out_specs=vmem,
        out_shape=jax.ShapeDtypeStruct((groups, 14 * step + 8, 128), F32),
        scratch_shapes=[
            pltpu.VMEM((2, 6, rows + 2, cols, 128), BF16),
            pltpu.VMEM((384, 768), F32),
        ],
        compiler_params=params(61),
        name="wgrad",
    )
    part = weight_call(load, other, *halo, norm, gain, bias)
    part = pl.pallas_call(
        append_kernel,
        in_specs=[vmem, vmem],
        out_specs=vmem,
        out_shape=jax.ShapeDtypeStruct((groups, 14 * step + 8, 128), F32),
        input_output_aliases={0: 0},
        compiler_params=params(16),
        name="append",
    )(part, sums)
    part = in_ranks(part)

    grad_features, grad_weight, grad_gain, grad_bias = pl.pallas_call(
        functools.partial(final_kernel, count),
        in_specs=[vmem] + [pl.BlockSpec()] * 4,
        out_shape=(
            jax.ShapeDtypeStruct((positions, chans), BF16),
            jax.ShapeDtypeStruct((9, 3, step, outs // rows), F32),
            jax.ShapeDtypeStruct((1, chans), F32),
            jax.ShapeDtypeStruct((1, chans), F32),
        ),
        compiler_params=params(16),
        name="final",
    )(part, act, feats, norm, gain)
    return (
        grad_features.reshape(features.shape),
        grad_weight.reshape(3, 3, 3, step, outs // rows),
        grad_gain.reshape(chans),
        grad_bias.reshape(chans),
    )


def solution(mesh):
    in_specs = (P("tm", "rows", None, None), P(), P(), P(), P("tm", "rows", None, None))
    out_specs = (P("tm", "rows", None, None), P(None, None, None, "tm", "rows"), P(), P())
    return jax.shard_map(on_device, mesh=mesh, in_specs=in_specs, out_specs=out_specs, check_vma=False)
```

```python
import functools

import jax
import jax.numpy as jnp
from jax import lax
from jax.experimental import pallas as pl
from jax.experimental.pallas import tpu as pltpu
from jax.sharding import PartitionSpec as P


GROUPS = 32
EPS = 1e-06
TEAM = 4
EDGES = ((0, -1), (0, 1), (1, 0), (1, -1), (1, 1))
F32 = jnp.float32
BF16 = jnp.bfloat16


def iota(shape, dim):
    return lax.broadcasted_iota(jnp.int32, shape, dim)


def shift_of(value):
    return value.bit_length() - 1


def exact_dot(a, ones, dims=((1,), (0,))):
    high = a.astype(BF16).astype(F32)
    rest = a - high
    mid = rest.astype(BF16).astype(F32)
    parts = jnp.concatenate([high, mid, rest - mid, jnp.zeros_like(a)], axis=0).astype(BF16)
    out = lax.dot_general(parts, ones, (dims, ((), ())), preferred_element_type=F32)
    return out[0:8] + out[8:16] + out[16:24]


def ones_where(mask):
    return jnp.where(mask, 1.0, 0.0).astype(BF16)


def members(chans, offset):
    bits = shift_of(chans // GROUPS)
    return ones_where(lax.shift_right_logical(iota((chans, 128), 0), bits) == iota((chans, 128), 1) - offset)


def sources(lane, step, chip, core):
    owner = lax.shift_right_logical(lane, shift_of(step))
    place = lax.shift_right_logical(owner, 2) * 32 + (owner & 3) * 4
    place = place + lax.shift_right_logical(chip, 1) * 16 + (chip & 1) * 2 + core
    return place * step + (lane & (step - 1))


def sigmoid(value):
    return 0.5 * jnp.tanh(0.5 * value) + 0.5


def col_shifts(slab):
    cols = slab.shape[0]
    wide = slab.astype(F32)
    row = iota(wide.shape, 0)
    ahead = jnp.where(row < cols - 1, pltpu.roll(wide, cols - 1, 0), 0.0).astype(BF16)
    behind = jnp.where(row > 0, pltpu.roll(wide, 1, 0), 0.0).astype(BF16)
    return ahead, slab, behind


def pack_kernel(teams, feats_ref, up_ref, load_ref):
    positions, chans = feats_ref.shape
    cols = up_ref.shape[1]
    rows = load_ref.shape[1]
    feats = feats_ref[...]
    core = lax.axis_index("tm") & 1
    lane = iota((1, chans), 1)
    source = sources(
        lane & 63, chans // teams, lax.shift_right_logical(lane, 7), lax.shift_right_logical(lane, 6) & 1
    )
    mover = ones_where(iota((chans, chans), 0) == source)
    moved = jnp.dot(feats, mover, preferred_element_type=F32)
    outs = up_ref.shape[2] // rows
    left = iota((cols, 128), 1) < 64
    for j in range(TEAM):
        early = moved[0:cols, j * 128 : (j + 1) * 128]
        late = moved[cols:, j * 128 : (j + 1) * 128]
        lower = jnp.where(left, early, pltpu.roll(late, 64, 1)).astype(BF16)
        upper = jnp.where(left, pltpu.roll(early, 64, 1), late).astype(BF16)
        keep = jnp.where(core == 0, lower, upper)
        send = jnp.where(core == 0, upper, lower)
        for r in range(rows):
            load_ref[j, r, 0:cols, :] = keep
            load_ref[j, r, cols : 2 * cols, :] = send
    for r in range(rows):
        pair = jnp.concatenate(
            [up_ref[0, :, r * outs : (r + 1) * outs], up_ref[1, :, r * outs : (r + 1) * outs]], axis=1
        )
        for j in range(TEAM):
            load_ref[j, r, 2 * cols : 3 * cols, :] = pair
    floats = feats.astype(F32)
    first = members(chans, 0)
    second = members(chans, GROUPS)
    total = jnp.broadcast_to(jnp.sum(floats, axis=0, keepdims=True), (8, chans))
    mean = exact_dot(total, first) / (positions * (chans // GROUPS))
    diffs = floats - exact_dot(mean, first, ((1,), (1,)))[0:1]
    squares = jnp.broadcast_to(jnp.sum(diffs * diffs, axis=0, keepdims=True), (8, chans))
    stat = mean + exact_dot(squares, second)
    high = stat.astype(BF16).astype(F32)
    mid = (stat - high).astype(BF16).astype(F32)
    low = stat - high - mid
    row = iota((8, 128), 0)
    parts = jnp.where(row == 0, high, jnp.where(row == 1, mid, jnp.where(row == 2, low, 0.0)))
    parts = jnp.concatenate([parts, jnp.zeros_like(parts)], axis=0).astype(BF16)
    for r in range(rows):
        for j in range(TEAM):
            load_ref[j, r, 3 * cols :, :] = parts


def combine_kernel(count, load_ref, out_ref):
    stats = []
    for j in range(load_ref.shape[0]):
        for r in range(load_ref.shape[1]):
            parts = load_ref[j, r, load_ref.shape[2] - 16 :].astype(F32)
            stats.append(parts[0:1] + parts[1:2] + parts[2:3])
    total = stats[0]
    for stat in stats[1:]:
        total = total + stat
    mean = total / len(stats)
    spans = jnp.zeros_like(mean)
    for stat in stats:
        spans = spans + (stat - mean) * (stat - mean)
    lane = iota((8, 128), 1)
    moved = pltpu.roll(jnp.broadcast_to(spans, (8, 128)), GROUPS, 1)
    result = jnp.where(lane < GROUPS, jnp.broadcast_to(mean, (8, 128)), total + count * moved)
    out_ref[...] = jnp.broadcast_to(result[None], out_ref.shape)


def dense_kernel(
    up_ref, above_ref, below_ref, later_ref, later_above_ref, later_below_ref, weight_ref, out_ref, slabs
):
    step = pl.program_id(0)
    time_tap = step // 3
    row_tap = step % 3
    time_index = lax.axis_index("tm")
    row_index = lax.axis_index("rows")
    positions = out_ref.shape[0]
    cols = up_ref.shape[1]

    @pl.when(step == 0)
    def _():
        out_ref[...] = jnp.zeros_like(out_ref)
        more = (time_index < lax.axis_size("tm") - 1).astype(F32)
        up_ok = (row_index > 0).astype(F32)
        down_ok = (row_index < lax.axis_size("rows") - 1).astype(F32)
        for f in range(4):
            trio = (above_ref, up_ref, below_ref) if f < 2 else (later_above_ref, later_ref, later_below_ref)
            tail = jnp.float32(1.0) if f < 2 else more
            for r, keep in enumerate((up_ok, jnp.float32(1.0), down_ok)):
                slab = (trio[r][f % 2].astype(F32) * (keep * tail)).astype(BF16)
                for c, moved in enumerate(col_shifts(slab)):
                    slabs[c, r, f] = moved

    def product(slab, c):
        return lax.dot_general(
            slab, weight_ref[0, 0, c], (((1,), (1,)), ((), ())), preferred_element_type=F32
        )

    total = out_ref[...]
    for c in range(3):
        slab = slabs[c, 2 - row_tap, pl.ds(2 - time_tap, 2)].reshape(positions, -1)
        total = total + product(slab, c)
    out_ref[...] = total

    @pl.when(jnp.logical_and(time_index == 0, time_tap == 0))
    def _():
        for c in range(3):
            both = slabs[c, 2 - row_tap, pl.ds(0, 2)].reshape(positions, -1)
            both = product(both, c)
            out_ref[0:cols, :] += both[0:cols] + both[cols:]

    @pl.when(jnp.logical_and(time_index == 0, time_tap == 1))
    def _():
        for c in range(3):
            out_ref[0:cols, :] += product(slabs[c, 2 - row_tap, 0], c)


def norm_rows(stats_ref, chans, positions):
    stats = jnp.concatenate([stats_ref[g, 0:1] for g in range(stats_ref.shape[0])], axis=0)
    devices = stats.shape[0]
    size = chans // GROUPS
    first = members(chans, 0)
    second = members(chans, GROUPS)
    total = jnp.sum(stats, axis=0, keepdims=True)
    centre = total / devices
    spans = stats - centre
    spans = jnp.sum(spans * spans, axis=0, keepdims=True)
    dims = ((1,), (1,))
    parts = exact_dot(jnp.broadcast_to(total, (8, 128)), second, dims) / (devices * positions * size)
    parts = parts + exact_dot(jnp.broadcast_to(spans, (8, 128)), first, dims) / devices
    inverse = lax.rsqrt(parts + EPS)
    centre = exact_dot(jnp.broadcast_to(centre, (8, 128)), first, dims)
    return centre, inverse


def act_kernel(
    positions, feats_ref, gain_ref, bias_ref, stats_ref, dense_ref, load_ref, halo0_ref, halo1_ref,
    act_ref, sums_ref, norm_ref, swap_ref, sems,
):
    chans = gain_ref.shape[1]
    cols = halo0_ref.shape[1]
    slots = load_ref.shape[0]
    tail = pl.ds(slots, halo0_ref.shape[0])
    copies = [
        pltpu.make_async_copy(load_ref.at[:, pl.ds(cols, 2 * cols)], swap_ref.at[pl.ds(0, slots)], sems.at[0]),
        pltpu.make_async_copy(halo0_ref, swap_ref.at[tail, pl.ds(0, cols)], sems.at[1]),
        pltpu.make_async_copy(halo1_ref, swap_ref.at[tail, pl.ds(cols, cols)], sems.at[2]),
    ]
    for copy in copies:
        copy.start()
    centre, inverse = norm_rows(stats_ref, chans, positions)
    norm_ref[0:8] = centre
    norm_ref[8:16] = inverse
    centre = centre[0:1]
    inverse = inverse[0:1]
    normed = (feats_ref[...].astype(F32) - centre) * inverse
    preact = normed * gain_ref[...] + bias_ref[...]
    sig = sigmoid(preact)
    act = dense_ref[...] * sig * (1.0 + preact * (1.0 - sig))
    act_ref[...] = act
    gains = jnp.sum(act * normed, axis=0, keepdims=True)
    biases = jnp.sum(act, axis=0, keepdims=True)
    pieces = chans // 128
    rows = [gains[:, p * 128 : (p + 1) * 128] for p in range(pieces)]
    rows = rows + [biases[:, p * 128 : (p + 1) * 128] for p in range(pieces)]
    sums_ref[...] = jnp.broadcast_to(jnp.concatenate(rows, axis=0)[None], sums_ref.shape)
    for copy in copies:
        copy.wait()


def append_kernel(part_ref, load_ref, out_ref, sums, sem):
    total = load_ref[0]
    for g in range(1, load_ref.shape[0]):
        total = total + load_ref[g]
    sums[...] = jnp.broadcast_to(total[None], sums.shape)
    size = sums.shape[1]
    copy = pltpu.make_async_copy(sums, out_ref.at[:, pl.ds(out_ref.shape[1] - size, size)], sem)
    copy.start()
    copy.wait()


def weight_kernel(
    teams, load_ref, other_ref, halo0_ref, halo1_ref, norm_ref, gain_ref, bias_ref, out_ref, hidden, acc
):
    time_index = lax.axis_index("tm")
    core = time_index & 1
    rows = load_ref.shape[1]
    cols = hidden.shape[3]
    chans = gain_ref.shape[1]
    step = chans // teams
    chip = (lax.shift_right_logical(time_index, 4) & 1) * 2 + (lax.shift_right_logical(time_index, 1) & 1)
    mover = ones_where(iota((chans, 128), 0) == sources(iota((1, 128), 1) & 63, step, chip, core))

    def slice_of(value):
        return exact_dot(value, mover)[0:1]

    centre = slice_of(norm_ref[0:8])
    inverse = slice_of(norm_ref[8:16])
    gain = slice_of(jnp.broadcast_to(gain_ref[...], (8, chans)))
    bias = slice_of(jnp.broadcast_to(bias_ref[...], (8, chans)))
    left = iota((cols, 128), 1) < 64
    start = (time_index & ~19) == 0
    end = (time_index | 19) == lax.axis_size("tm") - 1

    for x in range(2):
        for q in range(6):
            hidden[x, q, 0] = jnp.zeros(hidden.shape[3:], BF16)
            hidden[x, q, rows + 1] = jnp.zeros(hidden.shape[3:], BF16)
        for q in range(4):
            for r in range(rows):
                j = 2 * x + q // 2
                pair = jnp.where(core == q % 2, load_ref[j, r, 0:cols, :], other_ref[j * rows + r, 0:cols, :])
                preact = (pair.astype(F32) - centre) * inverse * gain + bias
                value = preact * sigmoid(preact)
                hidden[x, q + 1, r + 1] = value.astype(BF16)
                if q == 0:
                    before = jnp.zeros_like(value)
                    if x == 0:
                        before = jnp.where(start, jnp.where(left, value, pltpu.roll(value, 64, 1)), before)
                    hidden[x, 0, r + 1] = before.astype(BF16)
                    hidden[x, 5, r + 1] = jnp.zeros(hidden.shape[3:], BF16)

    def ups_of(x, q):
        sides = [[], [], []]
        for r in range(rows):
            j = 2 * x + q // 2
            if q < 4:
                pair = jnp.where(
                    core == q % 2,
                    load_ref[j, r, 2 * cols : 3 * cols, :],
                    other_ref[j * rows + r, cols : 2 * cols, :],
                )
            else:
                near = (halo0_ref, halo1_ref)[x]
                pair = jnp.where(
                    core == 0, near[r], other_ref[TEAM * rows + r, x * cols : (x + 1) * cols, :]
                )
            wide = pair.astype(F32)
            if q == 4 and x == 1:
                wide = jnp.where(end, 0.0, wide)
            row = iota(wide.shape, 0)
            sides[0].append(jnp.where(row < cols - 1, pltpu.roll(wide, cols - 1, 0), 0.0).astype(BF16))
            sides[1].append(wide.astype(BF16))
            sides[2].append(jnp.where(row > 0, pltpu.roll(wide, 1, 0), 0.0).astype(BF16))
        return jnp.concatenate([jnp.concatenate(side, axis=0) for side in sides], axis=1)

    def taps_of(x, q, width):
        taps = [hidden[x, q + n, b : b + rows].reshape(rows * cols, 128) for n in range(width) for b in range(3)]
        return jnp.concatenate(taps, axis=1)

    plans = [([(x, q), (x, q + 1)], 2) for x in range(2) for q in (0, 2)] + [([(0, 4), (1, 4)], 1)]
    for index, (units, width) in enumerate(plans):
        term = lax.dot_general(
            jnp.concatenate([ups_of(x, q) for x, q in units], axis=0),
            jnp.concatenate([taps_of(x, q, width) for x, q in units], axis=0),
            (((0,), (0,)), ((), ())),
            preferred_element_type=F32,
        )
        if index == 0:
            acc[...] = term
        else:
            acc[:, 0 : 384 * width] += term

    groups = out_ref.shape[0]
    low = iota((192, 128), 1) < 64

    def store(index, block):
        out_ref[:, index * step : (index + 1) * step, :] = block.reshape(groups, step, 128)

    thirds = []
    for b in range(3):
        blocks = [
            jnp.concatenate(
                [acc[c * 128 : (c + 1) * 128, m + b * 128 : m + (b + 1) * 128].T for m in (0, 384)], axis=0
            )
            for c in range(3)
        ]
        first = blocks[0][0:192] + pltpu.roll(blocks[0][64:256], 64, 1)
        second = pltpu.roll(blocks[1][0:192], 64, 1) + blocks[1][64:256]
        both = jnp.where(low, first, second)
        for a in range(3):
            store(3 * a + b, both[a * 64 : (a + 1) * 64])
        thirds.append(blocks[2][0:192] + pltpu.roll(blocks[2][64:256], 64, 1))
    both = jnp.where(low, thirds[0], pltpu.roll(thirds[1], 64, 1))
    for a in range(3):
        store(9 + a, both[a * 64 : (a + 1) * 64])
    store(12, jnp.where(low[0:64], thirds[2][0:64], pltpu.roll(thirds[2][64:128], 64, 1)))
    store(13, thirds[2][128:192])


def final_kernel(
    count, load_ref, act_ref, feats_ref, norm_ref, gain_ref, out_ref, grad_ref, gain_out_ref, bias_out_ref
):
    chans = gain_ref.shape[1]
    pieces = chans // 128
    step = grad_ref.shape[2]
    total = load_ref[0]
    for g in range(1, load_ref.shape[0]):
        total = total + load_ref[g]
    for a in range(3):
        for b in range(3):
            part = total[(3 * a + b) * step : (3 * a + b + 1) * step]
            grad_ref[3 * a + b, 0] = part[:, 0:64]
            grad_ref[3 * a + b, 1] = part[:, 64:128]
            index = 9 + a if b < 2 else 12 + a // 2
            side = 64 * (b if b < 2 else a % 2)
            grad_ref[3 * a + b, 2] = total[index * step : (index + 1) * step, side : side + 64]
    total = total[14 * step :]
    gains = jnp.concatenate([total[p : p + 1] for p in range(pieces)], axis=1)
    biases = jnp.concatenate([total[pieces + p : pieces + p + 1] for p in range(pieces)], axis=1)
    gain_out_ref[...] = gains
    bias_out_ref[...] = biases
    gain = gain_ref[...]
    owner = members(chans, 0)

    def spread(value):
        value = exact_dot(jnp.broadcast_to(value, (8, chans)), owner) / count
        return exact_dot(value, owner, ((1,), (1,)))[0:1]

    first = spread(gain * biases)
    second = spread(gain * gains)
    centre = norm_ref[0:1]
    inverse = norm_ref[8:9]
    normed = (feats_ref[...].astype(F32) - centre) * inverse
    out_ref[...] = (inverse * (act_ref[...] * gain - first - normed * second)).astype(BF16)


def on_device(features, norm_gain, norm_bias, weight, upstream):
    frames, rows_dev, cols, chans = features.shape
    outs = upstream.shape[3]
    tms = lax.axis_size("tm")
    rows = lax.axis_size("rows")
    devices = tms * rows
    positions = frames * rows_dev * cols
    step = chans // tms
    groups = tms // (2 * TEAM)
    wide = chans // TEAM
    count = positions * devices * (chans // GROUPS)
    vmem = pl.BlockSpec(memory_space=pltpu.VMEM)
    anywhere = pl.BlockSpec(memory_space=pl.ANY)
    far = pl.BlockSpec(memory_space=pltpu.HBM)

    def params(mebibytes):
        return pltpu.CompilerParams(vmem_limit_bytes=mebibytes * 1024 * 1024)

    feats = features.reshape(positions, chans)
    ups = upstream.reshape(frames, cols, outs)
    gain = norm_gain.reshape(1, chans)
    bias = norm_bias.reshape(1, chans)
    size = TEAM * rows
    length = positions + cols + 16
    places = [(big, z) for big in range(groups // 4) for z in range(4)]
    chips = [(x, z) for x in range(2) for z in range(2)]

    def place(outer, inner, core):
        return outer[0] * 32 + inner[0] * 16 + outer[1] * 4 + inner[1] * 2 + core

    every = range(rows)
    teams = [[place(o, i, c) * rows + r for i in chips for r in every] for o in places for c in range(2)]
    pairs = [[place(o, i, c) * rows + r for i in chips for c in range(2) for r in every] for o in places]
    stars = [[place(o, i, c) for o in places for c in range(2)] for i in chips]
    ranks = [[place(o, i, c) for o in places] for i in chips for c in range(2)]

    def in_teams(value):
        return lax.all_to_all(value, ("tm", "rows"), 0, 0, tiled=True, axis_index_groups=teams)

    def in_pairs(value):
        return lax.all_to_all(value, ("tm", "rows"), 0, 0, tiled=True, axis_index_groups=pairs)

    def in_stars(value):
        return lax.all_to_all(value, "tm", 0, 0, tiled=True, axis_index_groups=stars)

    def in_ranks(value):
        return lax.all_to_all(value, "tm", 0, 0, tiled=True, axis_index_groups=ranks)

    def neighbour(tm_step, row_step):
        moves = [
            (((t + tm_step) % tms) * rows + (r + row_step) % rows, t * rows + r)
            for t in range(tms)
            for r in range(rows)
        ]
        return lax.ppermute(ups, ("tm", "rows"), moves)

    halos = [neighbour(a, b) for a, b in EDGES]

    load = pl.pallas_call(
        functools.partial(pack_kernel, tms),
        out_shape=jax.ShapeDtypeStruct((TEAM, rows, length, wide), BF16),
        compiler_params=params(62),
        name="pack",
    )(feats, ups)
    load = in_teams(load.reshape(size, length, wide)).reshape(TEAM, rows, length, wide)

    opens = lax.shift_right_logical(lax.axis_index("tm"), 2) & 3 == 0
    runs = [load[2 * x, :, 2 * cols : 3 * cols] for x in range(2)]
    halo = []
    for x in range(2):
        moves = []
        for o in places:
            goal = (o[0], o[1] + 1) if o[1] < 3 else ((o[0] + x) % (groups // 4), 0)
            moves += [(place(goal, i, 0), place(o, i, 0)) for i in chips]
        halo.append(lax.ppermute(jnp.where(opens, runs[1 - x], runs[x]), "tm", moves))

    def whole(shape):
        return pl.BlockSpec(shape, lambda *s: (0,) * len(shape))

    dense_call = pl.pallas_call(
        dense_kernel,
        grid=(9,),
        in_specs=[
            *[whole((frames, cols, outs))] * 6,
            pl.BlockSpec((1, 1, 3, chans, outs), lambda s: (s // 3, s % 3, 0, 0, 0)),
        ],
        out_specs=whole((positions, chans)),
        out_shape=jax.ShapeDtypeStruct((positions, chans), F32),
        scratch_shapes=[pltpu.VMEM((3, 3, 4, cols, outs), BF16)],
        compiler_params=params(62),
        name="dense",
    )
    dense = dense_call(ups, *halos, weight)

    stats = pl.pallas_call(
        functools.partial(combine_kernel, float(positions * (chans // GROUPS))),
        in_specs=[vmem],
        out_specs=vmem,
        out_shape=jax.ShapeDtypeStruct((2 * groups, 8, 128), F32),
        compiler_params=params(16),
        name="combine",
    )(load)
    stats = in_stars(stats)

    act, sums, norm, swap = pl.pallas_call(
        functools.partial(act_kernel, positions * size),
        in_specs=[pl.BlockSpec()] * 3 + [vmem, pl.BlockSpec()] + [anywhere] * 3,
        out_specs=(pl.BlockSpec(), pl.BlockSpec(), pl.BlockSpec(), anywhere),
        scratch_shapes=[pltpu.SemaphoreType.DMA((3,))],
        out_shape=(
            jax.ShapeDtypeStruct((positions, chans), F32),
            jax.ShapeDtypeStruct((2 * size, 8, 128), F32),
            jax.ShapeDtypeStruct((16, chans), F32),
            jax.ShapeDtypeStruct((size + rows, 2 * cols, 128), BF16),
        ),
        compiler_params=params(62),
        name="act",
    )(feats, gain, bias, stats, dense, load.reshape(size, length, wide), *halo)
    other = lax.ppermute(swap, "tm", [(t, t ^ 1) for t in range(tms)])
    sums = in_pairs(sums)

    weight_call = pl.pallas_call(
        functools.partial(weight_kernel, tms),
        in_specs=[vmem, vmem] + [pl.BlockSpec()] * 5,
        out_specs=vmem,
        out_shape=jax.ShapeDtypeStruct((groups, 14 * step + 8, 128), F32),
        scratch_shapes=[
            pltpu.VMEM((2, 6, rows + 2, cols, 128), BF16),
            pltpu.VMEM((384, 768), F32),
        ],
        compiler_params=params(62),
        name="wgrad",
    )
    part = weight_call(load, other, *halo, norm, gain, bias)
    part = pl.pallas_call(
        append_kernel,
        in_specs=[far, vmem],
        out_specs=far,
        scratch_shapes=[pltpu.VMEM((groups, 8, 128), F32), pltpu.SemaphoreType.DMA],
        out_shape=jax.ShapeDtypeStruct((groups, 14 * step + 8, 128), F32),
        input_output_aliases={0: 0},
        compiler_params=params(62),
        name="append",
    )(part, sums)
    part = in_ranks(part)

    grad_features, grad_weight, grad_gain, grad_bias = pl.pallas_call(
        functools.partial(final_kernel, count),
        in_specs=[vmem] + [pl.BlockSpec()] * 4,
        out_shape=(
            jax.ShapeDtypeStruct((positions, chans), BF16),
            jax.ShapeDtypeStruct((9, 3, step, outs // rows), F32),
            jax.ShapeDtypeStruct((1, chans), F32),
            jax.ShapeDtypeStruct((1, chans), F32),
        ),
        compiler_params=params(16),
        name="final",
    )(part, act, feats, norm, gain)
    return (
        grad_features.reshape(features.shape),
        grad_weight.reshape(3, 3, 3, step, outs // rows),
        grad_gain.reshape(chans),
        grad_bias.reshape(chans),
    )


def solution(mesh):
    in_specs = (P("tm", "rows", None, None), P(), P(), P(), P("tm", "rows", None, None))
    out_specs = (P("tm", "rows", None, None), P(None, None, None, "tm", "rows"), P(), P())
    return jax.shard_map(on_device, mesh=mesh, in_specs=in_specs, out_specs=out_specs, check_vma=False)
```

```python
import functools

import jax
import jax.numpy as jnp
from jax import lax
from jax.experimental import pallas as pl
from jax.experimental.pallas import tpu as pltpu
from jax.sharding import PartitionSpec as P


GROUPS = 32
EPS = 1e-06
TEAM = 4
SHARE = 208
EDGES = ((1, 0), (0, -1), (0, 1), (1, -1), (1, 1))
F32 = jnp.float32
BF16 = jnp.bfloat16


def iota(shape, dim):
    return lax.broadcasted_iota(jnp.int32, shape, dim)


def shift_of(value):
    return value.bit_length() - 1


def exact_dot(a, ones, dims=((1,), (0,))):
    high = a.astype(BF16).astype(F32)
    rest = a - high
    mid = rest.astype(BF16).astype(F32)
    parts = jnp.concatenate([high, mid, rest - mid, jnp.zeros_like(a)], axis=0).astype(BF16)
    out = lax.dot_general(parts, ones, (dims, ((), ())), preferred_element_type=F32)
    return out[0:8] + out[8:16] + out[16:24]


def ones_where(mask):
    return jnp.where(mask, 1.0, 0.0).astype(BF16)


def members(chans, offset):
    bits = shift_of(chans // GROUPS)
    return ones_where(lax.shift_right_logical(iota((chans, 128), 0), bits) == iota((chans, 128), 1) - offset)


def sources(lane, step, chip, core):
    owner = lax.shift_right_logical(lane, shift_of(step))
    place = lax.shift_right_logical(owner, 2) * 32 + (owner & 3) * 4
    place = place + lax.shift_right_logical(chip, 1) * 16 + (chip & 1) * 2 + core
    return place * step + (lane & (step - 1))


def sigmoid(value):
    return 0.5 * jnp.tanh(0.5 * value) + 0.5


def col_shifts(slab):
    cols = slab.shape[0]
    wide = slab.astype(F32)
    row = iota(wide.shape, 0)
    ahead = jnp.where(row < cols - 1, pltpu.roll(wide, cols - 1, 0), 0.0).astype(BF16)
    behind = jnp.where(row > 0, pltpu.roll(wide, 1, 0), 0.0).astype(BF16)
    return ahead, slab, behind


def pack_kernel(teams, feats_ref, up_ref, later_ref, load_ref):
    positions, chans = feats_ref.shape
    cols = up_ref.shape[1]
    rows = load_ref.shape[1]
    feats = feats_ref[...]
    core = lax.axis_index("tm") & 1
    lane = iota((1, chans), 1)
    source = sources(
        lane & 63, chans // teams, lax.shift_right_logical(lane, 7), lax.shift_right_logical(lane, 6) & 1
    )
    mover = ones_where(iota((chans, chans), 0) == source)
    moved = jnp.dot(feats, mover, preferred_element_type=F32)
    outs = up_ref.shape[2] // rows
    left = iota((cols, 128), 1) < 64
    for j in range(TEAM):
        early = moved[0:cols, j * 128 : (j + 1) * 128]
        late = moved[cols:, j * 128 : (j + 1) * 128]
        lower = jnp.where(left, early, pltpu.roll(late, 64, 1)).astype(BF16)
        upper = jnp.where(left, pltpu.roll(early, 64, 1), late).astype(BF16)
        keep = jnp.where(core == 0, lower, upper)
        send = jnp.where(core == 0, upper, lower)
        for r in range(rows):
            load_ref[j, r, 0:cols, :] = keep
            load_ref[j, r, cols : 2 * cols, :] = send
    order = lax.axis_index("tm") & 3
    for r in range(rows):
        own, after = (
            jnp.concatenate(
                [ref[0, :, r * outs : (r + 1) * outs], ref[1, :, r * outs : (r + 1) * outs]], axis=1
            )
            for ref in (up_ref, later_ref)
        )
        for d in range(4):

            @pl.when(order == d)
            def _():
                first = d * (SHARE - cols)
                share = jnp.concatenate([own[first:], after[0 : min(cols, SHARE - cols + first)]], axis=0)
                for j in range(TEAM):
                    load_ref[j, r, 2 * cols : 2 * cols + share.shape[0], :] = share

    floats = feats.astype(F32)
    first = members(chans, 0)
    second = members(chans, GROUPS)
    total = jnp.broadcast_to(jnp.sum(floats, axis=0, keepdims=True), (8, chans))
    mean = exact_dot(total, first) / (positions * (chans // GROUPS))
    diffs = floats - exact_dot(mean, first, ((1,), (1,)))[0:1]
    squares = jnp.broadcast_to(jnp.sum(diffs * diffs, axis=0, keepdims=True), (8, chans))
    stat = mean + exact_dot(squares, second)
    high = stat.astype(BF16).astype(F32)
    mid = (stat - high).astype(BF16).astype(F32)
    low = stat - high - mid
    row = iota((8, 128), 0)
    parts = jnp.where(row == 0, high, jnp.where(row == 1, mid, jnp.where(row == 2, low, 0.0)))
    parts = jnp.concatenate([parts, jnp.zeros_like(parts)], axis=0).astype(BF16)
    for r in range(rows):
        for j in range(TEAM):
            load_ref[j, r, 2 * cols + SHARE :, :] = parts


def combine_kernel(count, load_ref, out_ref, swap_ref):
    stats = []
    for j in range(load_ref.shape[0]):
        for r in range(load_ref.shape[1]):
            parts = load_ref[j, r, load_ref.shape[2] - 16 :].astype(F32)
            stats.append(parts[0:1] + parts[1:2] + parts[2:3])
    total = stats[0]
    for stat in stats[1:]:
        total = total + stat
    mean = total / len(stats)
    spans = jnp.zeros_like(mean)
    for stat in stats:
        spans = spans + (stat - mean) * (stat - mean)
    lane = iota((8, 128), 1)
    moved = pltpu.roll(jnp.broadcast_to(spans, (8, 128)), GROUPS, 1)
    result = jnp.where(lane < GROUPS, jnp.broadcast_to(mean, (8, 128)), total + count * moved)
    out_ref[...] = jnp.broadcast_to(result[None], out_ref.shape)
    size = swap_ref.shape[2]
    start = load_ref.shape[2] - 16 - size
    swap_ref[...] = load_ref[:, :, start : start + size, :]


def dense_kernel(
    up_ref, above_ref, below_ref, later_ref, later_above_ref, later_below_ref, weight_ref, out_ref, slabs
):
    step = pl.program_id(0)
    time_tap = step // 3
    row_tap = step % 3
    time_index = lax.axis_index("tm")
    row_index = lax.axis_index("rows")
    positions = out_ref.shape[0]
    cols = up_ref.shape[1]

    @pl.when(step == 0)
    def _():
        out_ref[...] = jnp.zeros_like(out_ref)
        more = (time_index < lax.axis_size("tm") - 1).astype(F32)
        up_ok = (row_index > 0).astype(F32)
        down_ok = (row_index < lax.axis_size("rows") - 1).astype(F32)
        for f in range(4):
            trio = (above_ref, up_ref, below_ref) if f < 2 else (later_above_ref, later_ref, later_below_ref)
            tail = jnp.float32(1.0) if f < 2 else more
            for r, keep in enumerate((up_ok, jnp.float32(1.0), down_ok)):
                slab = (trio[r][f % 2].astype(F32) * (keep * tail)).astype(BF16)
                for c, moved in enumerate(col_shifts(slab)):
                    slabs[c, r, f] = moved

    def product(slab, c):
        return lax.dot_general(
            slab, weight_ref[0, 0, c], (((1,), (1,)), ((), ())), preferred_element_type=F32
        )

    total = out_ref[...]
    for c in range(3):
        slab = slabs[c, 2 - row_tap, pl.ds(2 - time_tap, 2)].reshape(positions, -1)
        total = total + product(slab, c)
    out_ref[...] = total

    @pl.when(jnp.logical_and(time_index == 0, time_tap == 0))
    def _():
        for c in range(3):
            both = slabs[c, 2 - row_tap, pl.ds(0, 2)].reshape(positions, -1)
            both = product(both, c)
            out_ref[0:cols, :] += both[0:cols] + both[cols:]

    @pl.when(jnp.logical_and(time_index == 0, time_tap == 1))
    def _():
        for c in range(3):
            out_ref[0:cols, :] += product(slabs[c, 2 - row_tap, 0], c)


def norm_rows(stats_ref, chans, positions):
    stats = jnp.concatenate([stats_ref[g, 0:1] for g in range(stats_ref.shape[0])], axis=0)
    devices = stats.shape[0]
    size = chans // GROUPS
    first = members(chans, 0)
    second = members(chans, GROUPS)
    total = jnp.sum(stats, axis=0, keepdims=True)
    centre = total / devices
    spans = stats - centre
    spans = jnp.sum(spans * spans, axis=0, keepdims=True)
    dims = ((1,), (1,))
    parts = exact_dot(jnp.broadcast_to(total, (8, 128)), second, dims) / (devices * positions * size)
    parts = parts + exact_dot(jnp.broadcast_to(spans, (8, 128)), first, dims) / devices
    inverse = lax.rsqrt(parts + EPS)
    centre = exact_dot(jnp.broadcast_to(centre, (8, 128)), first, dims)
    return centre, inverse


def act_kernel(positions, feats_ref, gain_ref, bias_ref, stats_ref, dense_ref, act_ref, sums_ref, norm_ref):
    chans = gain_ref.shape[1]
    centre, inverse = norm_rows(stats_ref, chans, positions)
    norm_ref[0:8] = centre
    norm_ref[8:16] = inverse
    centre = centre[0:1]
    inverse = inverse[0:1]
    normed = (feats_ref[...].astype(F32) - centre) * inverse
    preact = normed * gain_ref[...] + bias_ref[...]
    sig = sigmoid(preact)
    act = dense_ref[...] * sig * (1.0 + preact * (1.0 - sig))
    act_ref[...] = act
    gains = jnp.sum(act * normed, axis=0, keepdims=True)
    biases = jnp.sum(act, axis=0, keepdims=True)
    pieces = chans // 128
    rows = [gains[:, p * 128 : (p + 1) * 128] for p in range(pieces)]
    rows = rows + [biases[:, p * 128 : (p + 1) * 128] for p in range(pieces)]
    sums_ref[...] = jnp.broadcast_to(jnp.concatenate(rows, axis=0)[None], sums_ref.shape)


def append_kernel(part_ref, load_ref, out_ref, sums, sem):
    total = load_ref[0]
    for g in range(1, load_ref.shape[0]):
        total = total + load_ref[g]
    sums[...] = jnp.broadcast_to(total[None], sums.shape)
    size = sums.shape[1]
    copy = pltpu.make_async_copy(sums, out_ref.at[:, pl.ds(out_ref.shape[1] - size, size)], sem)
    copy.start()
    copy.wait()


def weight_kernel(
    teams, load_ref, other_ref, norm_ref, gain_ref, bias_ref, out_ref, hidden, acc
):
    time_index = lax.axis_index("tm")
    core = time_index & 1
    rows = load_ref.shape[1]
    cols = hidden.shape[3]
    chans = gain_ref.shape[1]
    step = chans // teams
    chip = (lax.shift_right_logical(time_index, 4) & 1) * 2 + (lax.shift_right_logical(time_index, 1) & 1)
    mover = ones_where(iota((chans, 128), 0) == sources(iota((1, 128), 1) & 63, step, chip, core))

    def slice_of(value):
        return exact_dot(value, mover)[0:1]

    centre = slice_of(norm_ref[0:8])
    inverse = slice_of(norm_ref[8:16])
    gain = slice_of(jnp.broadcast_to(gain_ref[...], (8, chans)))
    bias = slice_of(jnp.broadcast_to(bias_ref[...], (8, chans)))
    left = iota((cols, 128), 1) < 64
    start = (time_index & ~19) == 0
    end = (time_index | 19) == lax.axis_size("tm") - 1

    for x in range(2):
        for q in range(6):
            hidden[x, q, 0] = jnp.zeros(hidden.shape[3:], BF16)
            hidden[x, q, rows + 1] = jnp.zeros(hidden.shape[3:], BF16)
        for q in range(4):
            for r in range(rows):
                j = 2 * x + q // 2
                pair = jnp.where(core == q % 2, load_ref[j, r, 0:cols, :], other_ref[j, r, 0:cols, :])
                preact = (pair.astype(F32) - centre) * inverse * gain + bias
                value = preact * sigmoid(preact)
                hidden[x, q + 1, r + 1] = value.astype(BF16)
                if q == 0:
                    before = jnp.zeros_like(value)
                    if x == 0:
                        before = jnp.where(start, jnp.where(left, value, pltpu.roll(value, 64, 1)), before)
                    hidden[x, 0, r + 1] = before.astype(BF16)
                    hidden[x, 5, r + 1] = jnp.zeros(hidden.shape[3:], BF16)

    def share_of(x, d, r, first, last):
        j = 2 * x + d // 2
        return jnp.where(
            core == d % 2,
            load_ref[j, r, 2 * cols + first : 2 * cols + last, :],
            other_ref[j, r, cols + first : cols + last, :],
        )

    def ups_of(x, q):
        sides = [[], [], []]
        for r in range(rows):
            pieces = []
            for d in range(4):
                first = max(q * cols, d * SHARE) - d * SHARE
                last = min((q + 1) * cols, (d + 1) * SHARE) - d * SHARE
                if first < last:
                    pieces.append(share_of(x, d, r, first, last))
            pair = jnp.concatenate(pieces, axis=0)
            wide = pair.astype(F32)
            if q == 4 and x == 1:
                wide = jnp.where(end, 0.0, wide)
            row = iota(wide.shape, 0)
            sides[0].append(jnp.where(row < cols - 1, pltpu.roll(wide, cols - 1, 0), 0.0).astype(BF16))
            sides[1].append(wide.astype(BF16))
            sides[2].append(jnp.where(row > 0, pltpu.roll(wide, 1, 0), 0.0).astype(BF16))
        return jnp.concatenate([jnp.concatenate(side, axis=0) for side in sides], axis=1)

    def taps_of(x, q, width):
        taps = [hidden[x, q + n, b : b + rows].reshape(rows * cols, 128) for n in range(width) for b in range(3)]
        return jnp.concatenate(taps, axis=1)

    plans = [([(x, q), (x, q + 1)], 2) for x in range(2) for q in (0, 2)] + [([(0, 4), (1, 4)], 1)]
    for index, (units, width) in enumerate(plans):
        term = lax.dot_general(
            jnp.concatenate([ups_of(x, q) for x, q in units], axis=0),
            jnp.concatenate([taps_of(x, q, width) for x, q in units], axis=0),
            (((0,), (0,)), ((), ())),
            preferred_element_type=F32,
        )
        if index == 0:
            acc[...] = term
        else:
            acc[:, 0 : 384 * width] += term

    groups = out_ref.shape[0]
    low = iota((192, 128), 1) < 64

    def store(index, block):
        out_ref[:, index * step : (index + 1) * step, :] = block.reshape(groups, step, 128)

    thirds = []
    for b in range(3):
        blocks = [
            jnp.concatenate(
                [acc[c * 128 : (c + 1) * 128, m + b * 128 : m + (b + 1) * 128].T for m in (0, 384)], axis=0
            )
            for c in range(3)
        ]
        first = blocks[0][0:192] + pltpu.roll(blocks[0][64:256], 64, 1)
        second = pltpu.roll(blocks[1][0:192], 64, 1) + blocks[1][64:256]
        both = jnp.where(low, first, second)
        for a in range(3):
            store(3 * a + b, both[a * 64 : (a + 1) * 64])
        thirds.append(blocks[2][0:192] + pltpu.roll(blocks[2][64:256], 64, 1))
    both = jnp.where(low, thirds[0], pltpu.roll(thirds[1], 64, 1))
    for a in range(3):
        store(9 + a, both[a * 64 : (a + 1) * 64])
    store(12, jnp.where(low[0:64], thirds[2][0:64], pltpu.roll(thirds[2][64:128], 64, 1)))
    store(13, thirds[2][128:192])


def final_kernel(
    count, load_ref, act_ref, feats_ref, norm_ref, gain_ref, out_ref, grad_ref, gain_out_ref, bias_out_ref
):
    chans = gain_ref.shape[1]
    pieces = chans // 128
    step = grad_ref.shape[2]
    total = load_ref[0]
    for g in range(1, load_ref.shape[0]):
        total = total + load_ref[g]
    for a in range(3):
        for b in range(3):
            part = total[(3 * a + b) * step : (3 * a + b + 1) * step]
            grad_ref[3 * a + b, 0] = part[:, 0:64]
            grad_ref[3 * a + b, 1] = part[:, 64:128]
            index = 9 + a if b < 2 else 12 + a // 2
            side = 64 * (b if b < 2 else a % 2)
            grad_ref[3 * a + b, 2] = total[index * step : (index + 1) * step, side : side + 64]
    total = total[14 * step :]
    gains = jnp.concatenate([total[p : p + 1] for p in range(pieces)], axis=1)
    biases = jnp.concatenate([total[pieces + p : pieces + p + 1] for p in range(pieces)], axis=1)
    gain_out_ref[...] = gains
    bias_out_ref[...] = biases
    gain = gain_ref[...]
    owner = members(chans, 0)

    def spread(value):
        value = exact_dot(jnp.broadcast_to(value, (8, chans)), owner) / count
        return exact_dot(value, owner, ((1,), (1,)))[0:1]

    first = spread(gain * biases)
    second = spread(gain * gains)
    centre = norm_ref[0:1]
    inverse = norm_ref[8:9]
    normed = (feats_ref[...].astype(F32) - centre) * inverse
    out_ref[...] = (inverse * (act_ref[...] * gain - first - normed * second)).astype(BF16)


def on_device(features, norm_gain, norm_bias, weight, upstream):
    frames, rows_dev, cols, chans = features.shape
    outs = upstream.shape[3]
    tms = lax.axis_size("tm")
    rows = lax.axis_size("rows")
    devices = tms * rows
    positions = frames * rows_dev * cols
    step = chans // tms
    groups = tms // (2 * TEAM)
    wide = chans // TEAM
    count = positions * devices * (chans // GROUPS)
    vmem = pl.BlockSpec(memory_space=pltpu.VMEM)
    far = pl.BlockSpec(memory_space=pltpu.HBM)

    def params(mebibytes):
        return pltpu.CompilerParams(vmem_limit_bytes=mebibytes * 1024 * 1024)

    feats = features.reshape(positions, chans)
    ups = upstream.reshape(frames, cols, outs)
    gain = norm_gain.reshape(1, chans)
    bias = norm_bias.reshape(1, chans)
    size = TEAM * rows
    length = positions + SHARE + 16
    places = [(big, z) for big in range(groups // 4) for z in range(4)]
    chips = [(x, z) for x in range(2) for z in range(2)]

    def place(outer, inner, core):
        return outer[0] * 32 + inner[0] * 16 + outer[1] * 4 + inner[1] * 2 + core

    every = range(rows)
    teams = [[place(o, i, c) * rows + r for i in chips for r in every] for o in places for c in range(2)]
    pairs = [[place(o, i, c) * rows + r for i in chips for c in range(2) for r in every] for o in places]
    stars = [[place(o, i, c) for o in places for c in range(2)] for i in chips]
    ranks = [[place(o, i, c) for o in places] for i in chips for c in range(2)]

    def in_teams(value):
        return lax.all_to_all(value, ("tm", "rows"), 0, 0, tiled=True, axis_index_groups=teams)

    def in_pairs(value):
        return lax.all_to_all(value, ("tm", "rows"), 0, 0, tiled=True, axis_index_groups=pairs)

    def in_stars(value):
        return lax.all_to_all(value, "tm", 0, 0, tiled=True, axis_index_groups=stars)

    def in_ranks(value):
        return lax.all_to_all(value, "tm", 0, 0, tiled=True, axis_index_groups=ranks)

    def neighbour(tm_step, row_step):
        moves = [
            (((t + tm_step) % tms) * rows + (r + row_step) % rows, t * rows + r)
            for t in range(tms)
            for r in range(rows)
        ]
        return lax.ppermute(ups, ("tm", "rows"), moves)

    halos = [neighbour(a, b) for a, b in EDGES]

    load = pl.pallas_call(
        functools.partial(pack_kernel, tms),
        out_shape=jax.ShapeDtypeStruct((TEAM, rows, length, wide), BF16),
        compiler_params=params(62),
        name="pack",
    )(feats, ups, halos[0])
    load = in_teams(load.reshape(size, length, wide)).reshape(TEAM, rows, length, wide)

    def whole(shape):
        return pl.BlockSpec(shape, lambda *s: (0,) * len(shape))

    dense_call = pl.pallas_call(
        dense_kernel,
        grid=(9,),
        in_specs=[
            *[whole((frames, cols, outs))] * 6,
            pl.BlockSpec((1, 1, 3, chans, outs), lambda s: (s // 3, s % 3, 0, 0, 0)),
        ],
        out_specs=whole((positions, chans)),
        out_shape=jax.ShapeDtypeStruct((positions, chans), F32),
        scratch_shapes=[pltpu.VMEM((3, 3, 4, cols, outs), BF16)],
        compiler_params=params(62),
        name="dense",
    )
    dense = dense_call(ups, halos[1], halos[2], halos[0], halos[3], halos[4], weight)

    stats, swap = pl.pallas_call(
        functools.partial(combine_kernel, float(positions * (chans // GROUPS))),
        in_specs=[vmem],
        out_shape=(
            jax.ShapeDtypeStruct((2 * groups, 8, 128), F32),
            jax.ShapeDtypeStruct((TEAM, rows, cols + SHARE, 128), BF16),
        ),
        compiler_params=params(60),
        name="combine",
    )(load)
    other = lax.ppermute(swap, "tm", [(t, t ^ 1) for t in range(tms)])
    stats = in_stars(stats)

    act, sums, norm = pl.pallas_call(
        functools.partial(act_kernel, positions * size),
        in_specs=[pl.BlockSpec()] * 3 + [vmem, pl.BlockSpec()],
        out_shape=(
            jax.ShapeDtypeStruct((positions, chans), F32),
            jax.ShapeDtypeStruct((2 * size, 8, 128), F32),
            jax.ShapeDtypeStruct((16, chans), F32),
        ),
        compiler_params=params(62),
        name="act",
    )(feats, gain, bias, stats, dense)
    sums = in_pairs(sums)

    weight_call = pl.pallas_call(
        functools.partial(weight_kernel, tms),
        in_specs=[vmem, vmem] + [pl.BlockSpec()] * 3,
        out_specs=vmem,
        out_shape=jax.ShapeDtypeStruct((groups, 14 * step + 8, 128), F32),
        scratch_shapes=[
            pltpu.VMEM((2, 6, rows + 2, cols, 128), BF16),
            pltpu.VMEM((384, 768), F32),
        ],
        compiler_params=params(62),
        name="wgrad",
    )
    part = weight_call(load, other, norm, gain, bias)
    part = pl.pallas_call(
        append_kernel,
        in_specs=[far, vmem],
        out_specs=far,
        scratch_shapes=[pltpu.VMEM((groups, 8, 128), F32), pltpu.SemaphoreType.DMA],
        out_shape=jax.ShapeDtypeStruct((groups, 14 * step + 8, 128), F32),
        input_output_aliases={0: 0},
        compiler_params=params(62),
        name="append",
    )(part, sums)
    part = in_ranks(part)

    grad_features, grad_weight, grad_gain, grad_bias = pl.pallas_call(
        functools.partial(final_kernel, count),
        in_specs=[vmem] + [pl.BlockSpec()] * 4,
        out_shape=(
            jax.ShapeDtypeStruct((positions, chans), BF16),
            jax.ShapeDtypeStruct((9, 3, step, outs // rows), F32),
            jax.ShapeDtypeStruct((1, chans), F32),
            jax.ShapeDtypeStruct((1, chans), F32),
        ),
        compiler_params=params(16),
        name="final",
    )(part, act, feats, norm, gain)
    return (
        grad_features.reshape(features.shape),
        grad_weight.reshape(3, 3, 3, step, outs // rows),
        grad_gain.reshape(chans),
        grad_bias.reshape(chans),
    )


def solution(mesh):
    in_specs = (P("tm", "rows", None, None), P(), P(), P(), P("tm", "rows", None, None))
    out_specs = (P("tm", "rows", None, None), P(None, None, None, "tm", "rows"), P(), P())
    return jax.shard_map(on_device, mesh=mesh, in_specs=in_specs, out_specs=out_specs, check_vma=False)
```

```python
import functools

import jax
import jax.numpy as jnp
from jax import lax
from jax.experimental import pallas as pl
from jax.experimental.pallas import tpu as pltpu
from jax.sharding import PartitionSpec as P


GROUPS = 32
EPS = 1e-06
TEAM = 4
SHARES = ((0, 192), (192, 384), (384, 576), (576, 800))
HALF = 112
EDGES = ((1, 0), (0, -1), (0, 1), (1, -1), (1, 1))
F32 = jnp.float32
BF16 = jnp.bfloat16


def iota(shape, dim):
    return lax.broadcasted_iota(jnp.int32, shape, dim)


def shift_of(value):
    return value.bit_length() - 1


def exact_dot(a, ones, dims=((1,), (0,))):
    high = a.astype(BF16).astype(F32)
    rest = a - high
    mid = rest.astype(BF16).astype(F32)
    parts = jnp.concatenate([high, mid, rest - mid, jnp.zeros_like(a)], axis=0).astype(BF16)
    out = lax.dot_general(parts, ones, (dims, ((), ())), preferred_element_type=F32)
    return out[0:8] + out[8:16] + out[16:24]


def ones_where(mask):
    return jnp.where(mask, 1.0, 0.0).astype(BF16)


def members(chans, offset):
    bits = shift_of(chans // GROUPS)
    return ones_where(lax.shift_right_logical(iota((chans, 128), 0), bits) == iota((chans, 128), 1) - offset)


def sources(lane, chans, teams, spot):
    step = chans // teams
    return (lane & -step) * TEAM + spot * step + (lane & (step - 1))


def sigmoid(value):
    return 0.5 * jnp.tanh(0.5 * value) + 0.5


def col_shifts(slab):
    cols = slab.shape[0]
    wide = slab.astype(F32)
    row = iota(wide.shape, 0)
    ahead = jnp.where(row < cols - 1, pltpu.roll(wide, cols - 1, 0), 0.0).astype(BF16)
    behind = jnp.where(row > 0, pltpu.roll(wide, 1, 0), 0.0).astype(BF16)
    return ahead, slab, behind


def pack_kernel(teams, feats_ref, up_ref, later_ref, load_ref):
    positions, chans = feats_ref.shape
    cols = up_ref.shape[1]
    rows = load_ref.shape[1]
    feats = feats_ref[...]
    wide = chans // TEAM
    lane = iota((1, chans), 1)
    source = sources(lane & (wide - 1), chans, teams, lax.shift_right_logical(lane, shift_of(wide)))
    mover = ones_where(iota((chans, chans), 0) == source)
    moved = jnp.dot(feats, mover, preferred_element_type=F32).astype(BF16)
    outs = up_ref.shape[2] // rows
    for j in range(TEAM):
        for r in range(rows):
            load_ref[j, r, 0:positions, :] = moved[:, j * wide : (j + 1) * wide]
    order = lax.axis_index("tm") & (TEAM - 1)
    for r in range(rows):
        own, after = (
            jnp.concatenate(
                [ref[0, :, r * outs : (r + 1) * outs], ref[1, :, r * outs : (r + 1) * outs]], axis=1
            )
            for ref in (up_ref, later_ref)
        )
        for d in range(TEAM):

            @pl.when(order == d)
            def _():
                first, last = (value - d * cols for value in SHARES[d])
                share = jnp.concatenate([own[first:], after[0 : last - cols]], axis=0)
                size = (last - first) // 2
                for j in range(TEAM):
                    core = j % 2
                    part = share[core * size : (core + 1) * size]
                    load_ref[j, r, positions : positions + size, :] = part

    floats = feats.astype(F32)
    first = members(chans, 0)
    second = members(chans, GROUPS)
    total = jnp.broadcast_to(jnp.sum(floats, axis=0, keepdims=True), (8, chans))
    mean = exact_dot(total, first) / (positions * (chans // GROUPS))
    diffs = floats - exact_dot(mean, first, ((1,), (1,)))[0:1]
    squares = jnp.broadcast_to(jnp.sum(diffs * diffs, axis=0, keepdims=True), (8, chans))
    stat = mean + exact_dot(squares, second)
    high = stat.astype(BF16).astype(F32)
    mid = (stat - high).astype(BF16).astype(F32)
    low = stat - high - mid
    row = iota((8, 128), 0)
    parts = jnp.where(row == 0, high, jnp.where(row == 1, mid, jnp.where(row == 2, low, 0.0)))
    parts = jnp.concatenate([parts, jnp.zeros_like(parts)], axis=0).astype(BF16)
    for r in range(rows):
        for j in range(TEAM):
            load_ref[j, r, positions + HALF :, :] = parts


def combine_kernel(count, load_ref, out_ref, swap_ref):
    stats = []
    for j in range(load_ref.shape[0]):
        for r in range(load_ref.shape[1]):
            parts = load_ref[j, r, load_ref.shape[2] - 16 :].astype(F32)
            stats.append(parts[0:1] + parts[1:2] + parts[2:3])
    total = stats[0]
    for stat in stats[1:]:
        total = total + stat
    mean = total / len(stats)
    spans = jnp.zeros_like(mean)
    for stat in stats:
        spans = spans + (stat - mean) * (stat - mean)
    lane = iota((8, 128), 1)
    moved = pltpu.roll(jnp.broadcast_to(spans, (8, 128)), GROUPS, 1)
    result = jnp.where(lane < GROUPS, jnp.broadcast_to(mean, (8, 128)), total + count * moved)
    out_ref[...] = jnp.broadcast_to(result[None], out_ref.shape)
    start = load_ref.shape[2] - 16 - HALF
    swap_ref[...] = load_ref[:, :, start : start + HALF, :]


def dense_kernel(
    up_ref, above_ref, below_ref, later_ref, later_above_ref, later_below_ref, weight_ref, out_ref, slabs
):
    step = pl.program_id(0)
    time_tap = step // 3
    row_tap = step % 3
    time_index = lax.axis_index("tm")
    row_index = lax.axis_index("rows")
    positions = out_ref.shape[0]
    cols = up_ref.shape[1]

    @pl.when(step == 0)
    def _():
        out_ref[...] = jnp.zeros_like(out_ref)
        more = (time_index < lax.axis_size("tm") - 1).astype(F32)
        up_ok = (row_index > 0).astype(F32)
        down_ok = (row_index < lax.axis_size("rows") - 1).astype(F32)
        for f in range(4):
            trio = (above_ref, up_ref, below_ref) if f < 2 else (later_above_ref, later_ref, later_below_ref)
            tail = jnp.float32(1.0) if f < 2 else more
            for r, keep in enumerate((up_ok, jnp.float32(1.0), down_ok)):
                slab = (trio[r][f % 2].astype(F32) * (keep * tail)).astype(BF16)
                for c, moved in enumerate(col_shifts(slab)):
                    slabs[c, r, f] = moved

    def product(slab, c):
        return lax.dot_general(
            slab, weight_ref[0, 0, c], (((1,), (1,)), ((), ())), preferred_element_type=F32
        )

    total = out_ref[...]
    for c in range(3):
        slab = slabs[c, 2 - row_tap, pl.ds(2 - time_tap, 2)].reshape(positions, -1)
        total = total + product(slab, c)
    out_ref[...] = total

    @pl.when(jnp.logical_and(time_index == 0, time_tap == 0))
    def _():
        for c in range(3):
            both = slabs[c, 2 - row_tap, pl.ds(0, 2)].reshape(positions, -1)
            both = product(both, c)
            out_ref[0:cols, :] += both[0:cols] + both[cols:]

    @pl.when(jnp.logical_and(time_index == 0, time_tap == 1))
    def _():
        for c in range(3):
            out_ref[0:cols, :] += product(slabs[c, 2 - row_tap, 0], c)


def norm_rows(stats_ref, chans, positions):
    stats = jnp.concatenate([stats_ref[g, 0:1] for g in range(stats_ref.shape[0])], axis=0)
    devices = stats.shape[0]
    size = chans // GROUPS
    first = members(chans, 0)
    second = members(chans, GROUPS)
    total = jnp.sum(stats, axis=0, keepdims=True)
    centre = total / devices
    spans = stats - centre
    spans = jnp.sum(spans * spans, axis=0, keepdims=True)
    dims = ((1,), (1,))
    parts = exact_dot(jnp.broadcast_to(total, (8, 128)), second, dims) / (devices * positions * size)
    parts = parts + exact_dot(jnp.broadcast_to(spans, (8, 128)), first, dims) / devices
    inverse = lax.rsqrt(parts + EPS)
    centre = exact_dot(jnp.broadcast_to(centre, (8, 128)), first, dims)
    return centre, inverse


def act_kernel(positions, feats_ref, gain_ref, bias_ref, stats_ref, dense_ref, act_ref, sums_ref, norm_ref):
    chans = gain_ref.shape[1]
    centre, inverse = norm_rows(stats_ref, chans, positions)
    norm_ref[0:8] = centre
    norm_ref[8:16] = inverse
    centre = centre[0:1]
    inverse = inverse[0:1]
    normed = (feats_ref[...].astype(F32) - centre) * inverse
    preact = normed * gain_ref[...] + bias_ref[...]
    sig = sigmoid(preact)
    act = dense_ref[...] * sig * (1.0 + preact * (1.0 - sig))
    act_ref[...] = act
    gains = jnp.sum(act * normed, axis=0, keepdims=True)
    biases = jnp.sum(act, axis=0, keepdims=True)
    pieces = chans // 128
    rows = [gains[:, p * 128 : (p + 1) * 128] for p in range(pieces)]
    rows = rows + [biases[:, p * 128 : (p + 1) * 128] for p in range(pieces)]
    sums_ref[...] = jnp.broadcast_to(jnp.concatenate(rows, axis=0)[None], sums_ref.shape)


def append_kernel(part_ref, load_ref, out_ref):
    total = load_ref[0]
    for g in range(1, load_ref.shape[0]):
        total = total + load_ref[g]
    place = (out_ref.shape[0],) + total.shape
    out_ref[:, out_ref.shape[1] - total.shape[0] :, :] = jnp.broadcast_to(total[None], place)


def weight_kernel(teams, load_ref, other_ref, norm_ref, gain_ref, bias_ref, out_ref, hidden, acc):
    time_index = lax.axis_index("tm")
    rows = load_ref.shape[1]
    cols = hidden.shape[2]
    chans = gain_ref.shape[1]
    wide = chans // TEAM
    step = chans // teams
    mover = ones_where(
        iota((chans, wide), 0) == sources(iota((1, wide), 1), chans, teams, time_index & (TEAM - 1))
    )

    def slice_of(value):
        return exact_dot(value, mover)[0:1]

    centre = slice_of(norm_ref[0:8])
    inverse = slice_of(norm_ref[8:16])
    gain = slice_of(jnp.broadcast_to(gain_ref[...], (8, chans)))
    bias = slice_of(jnp.broadcast_to(bias_ref[...], (8, chans)))

    def silu(value):
        preact = (value.astype(F32) - centre) * inverse * gain + bias
        return (preact * sigmoid(preact)).astype(BF16)

    frames = 2 * TEAM
    for f in range(frames + 2):
        hidden[f, 0] = jnp.zeros(hidden.shape[2:], BF16)
        hidden[f, rows + 1] = jnp.zeros(hidden.shape[2:], BF16)
    opening = (time_index < TEAM).astype(F32)
    for j in range(TEAM):
        for r in range(rows):
            for f in range(2):
                value = silu(load_ref[j, r, f * cols : (f + 1) * cols, :])
                hidden[2 + 2 * j + f, 1 + r] = value
                if j == 0 and f == 0:
                    value = (value.astype(F32) * opening).astype(BF16)
                    hidden[0, 1 + r] = value
                    hidden[1, 1 + r] = value

    base = 2 * cols

    def pieces_of(q, r):
        pieces = []
        for d, (begin, close) in enumerate(SHARES):
            size = (close - begin) // 2
            for half in range(2):
                first = max(q * cols, begin + half * size) - begin - half * size
                last = min((q + 1) * cols, begin + (half + 1) * size) - begin - half * size
                if first < last:
                    mine = load_ref[d, r, base + first : base + last, :]
                    pieces.append(jnp.where((time_index & 1) == half, mine, other_ref[d, r, first:last, :]))
        return pieces

    lanes = iota((cols, 128), 1) < 64
    more = (time_index < lax.axis_size("tm") - TEAM).astype(F32)
    for j in range(TEAM + 1):
        halves = [[], []]
        for r in range(rows):
            pair = jnp.concatenate(pieces_of(j, r), axis=0).astype(F32)
            if j == TEAM:
                pair = pair * more
            row = iota(pair.shape, 0)
            ahead = jnp.where(row < cols - 1, pltpu.roll(pair, cols - 1, 0), 0.0)
            behind = jnp.where(row > 0, pltpu.roll(pair, 1, 0), 0.0)
            left = jnp.where(lanes, ahead, pltpu.roll(pair, 64, 1))
            right = jnp.where(lanes, pltpu.roll(ahead, 64, 1), pair)
            halves[0].append(jnp.concatenate([left, behind[:, 0:64]], axis=1))
            halves[1].append(jnp.concatenate([right, behind[:, 64:128]], axis=1))
        for f in range(2):
            ups = jnp.concatenate(halves[f], axis=0).astype(BF16)
            frame = 2 * j + f
            depth = min(3, frames + 2 - frame)
            taps = [
                hidden[frame + a, b : b + rows].reshape(rows * cols, wide) for a in range(depth) for b in range(3)
            ]
            term = lax.dot_general(
                ups, jnp.concatenate(taps, axis=1), (((0,), (0,)), ((), ())), preferred_element_type=F32
            )
            if frame == 0:
                acc[...] = term
            else:
                acc[:, 0 : 3 * depth * wide] += term

    groups = out_ref.shape[0]
    tail = None
    for ab in range(9):
        block = acc[:, ab * wide : (ab + 1) * wide].T
        out_ref[:, ab * step : (ab + 1) * step, :] = block[:, 0:128].reshape(groups, step, 128)
        last = block[:, 128:192]
        if ab % 2 == 0:
            tail = last
        if ab % 2 == 1 or ab == 8:
            both = jnp.concatenate([tail, last], axis=1)
            at = (9 + ab // 2) * step
            out_ref[:, at : at + step, :] = both.reshape(groups, step, 128)


def final_kernel(
    count, load_ref, act_ref, feats_ref, norm_ref, gain_ref, out_ref, grad_ref, gain_out_ref, bias_out_ref
):
    chans = gain_ref.shape[1]
    pieces = chans // 128
    step = grad_ref.shape[2]
    total = load_ref[0]
    for g in range(1, load_ref.shape[0]):
        total = total + load_ref[g]
    for ab in range(9):
        part = total[ab * step : (ab + 1) * step]
        grad_ref[ab, 0] = part[:, 0:64]
        grad_ref[ab, 1] = part[:, 64:128]
        at = (9 + ab // 2) * step
        side = 64 * (ab % 2)
        grad_ref[ab, 2] = total[at : at + step, side : side + 64]
    total = total[14 * step :]
    gains = jnp.concatenate([total[p : p + 1] for p in range(pieces)], axis=1)
    biases = jnp.concatenate([total[pieces + p : pieces + p + 1] for p in range(pieces)], axis=1)
    gain_out_ref[...] = gains
    bias_out_ref[...] = biases
    gain = gain_ref[...]
    owner = members(chans, 0)

    def spread(value):
        value = exact_dot(jnp.broadcast_to(value, (8, chans)), owner) / count
        return exact_dot(value, owner, ((1,), (1,)))[0:1]

    first = spread(gain * biases)
    second = spread(gain * gains)
    centre = norm_ref[0:1]
    inverse = norm_ref[8:9]
    normed = (feats_ref[...].astype(F32) - centre) * inverse
    out_ref[...] = (inverse * (act_ref[...] * gain - first - normed * second)).astype(BF16)


def on_device(features, norm_gain, norm_bias, weight, upstream):
    frames, rows_dev, cols, chans = features.shape
    outs = upstream.shape[3]
    tms = lax.axis_size("tm")
    rows = lax.axis_size("rows")
    devices = tms * rows
    positions = frames * rows_dev * cols
    step = chans // tms
    groups = tms // TEAM
    wide = chans // TEAM
    count = positions * devices * (chans // GROUPS)
    vmem = pl.BlockSpec(memory_space=pltpu.VMEM)

    def params(mebibytes):
        return pltpu.CompilerParams(vmem_limit_bytes=mebibytes * 1024 * 1024)

    feats = features.reshape(positions, chans)
    ups = upstream.reshape(frames, cols, outs)
    gain = norm_gain.reshape(1, chans)
    bias = norm_bias.reshape(1, chans)
    size = TEAM * rows
    length = positions + HALF + 16
    teams = [[size * g + i for i in range(size)] for g in range(groups)]
    ranks = [[TEAM * g + j for g in range(groups)] for j in range(TEAM)]

    def in_teams(value):
        return lax.all_to_all(value, ("tm", "rows"), 0, 0, tiled=True, axis_index_groups=teams)

    def in_ranks(value):
        return lax.all_to_all(value, "tm", 0, 0, tiled=True, axis_index_groups=ranks)

    def neighbour(tm_step, row_step):
        pairs = [
            (((t + tm_step) % tms) * rows + (r + row_step) % rows, t * rows + r)
            for t in range(tms)
            for r in range(rows)
        ]
        return lax.ppermute(ups, ("tm", "rows"), pairs)

    halos = [neighbour(a, b) for a, b in EDGES]

    load = pl.pallas_call(
        functools.partial(pack_kernel, tms),
        out_shape=jax.ShapeDtypeStruct((TEAM, rows, length, wide), BF16),
        compiler_params=params(62),
        name="pack",
    )(feats, ups, halos[0])
    load = in_teams(load.reshape(size, length, wide)).reshape(TEAM, rows, length, wide)

    def whole(shape):
        return pl.BlockSpec(shape, lambda *s: (0,) * len(shape))

    dense_call = pl.pallas_call(
        dense_kernel,
        grid=(9,),
        in_specs=[
            *[whole((frames, cols, outs))] * 6,
            pl.BlockSpec((1, 1, 3, chans, outs), lambda s: (s // 3, s % 3, 0, 0, 0)),
        ],
        out_specs=whole((positions, chans)),
        out_shape=jax.ShapeDtypeStruct((positions, chans), F32),
        scratch_shapes=[pltpu.VMEM((3, 3, 4, cols, outs), BF16)],
        compiler_params=params(62),
        name="dense",
    )
    dense = dense_call(ups, halos[1], halos[2], halos[0], halos[3], halos[4], weight)

    stats, swap = pl.pallas_call(
        functools.partial(combine_kernel, float(positions * (chans // GROUPS))),
        in_specs=[vmem],
        out_shape=(
            jax.ShapeDtypeStruct((groups, 8, 128), F32),
            jax.ShapeDtypeStruct((TEAM, rows, HALF, wide), BF16),
        ),
        compiler_params=params(40),
        name="combine",
    )(load)
    other = lax.ppermute(swap, "tm", [(t, t ^ 1) for t in range(tms)])
    stats = in_ranks(stats)

    act, sums, norm = pl.pallas_call(
        functools.partial(act_kernel, positions * size),
        in_specs=[pl.BlockSpec(), pl.BlockSpec(), pl.BlockSpec(), vmem, pl.BlockSpec()],
        out_shape=(
            jax.ShapeDtypeStruct((positions, chans), F32),
            jax.ShapeDtypeStruct((size, 8, 128), F32),
            jax.ShapeDtypeStruct((16, chans), F32),
        ),
        compiler_params=params(62),
        name="act",
    )(feats, gain, bias, stats, dense)
    sums = in_teams(sums)

    weight_call = pl.pallas_call(
        functools.partial(weight_kernel, tms),
        in_specs=[vmem] + [pl.BlockSpec()] * 4,
        out_specs=vmem,
        out_shape=jax.ShapeDtypeStruct((groups, 14 * step + 8, 128), F32),
        scratch_shapes=[
            pltpu.VMEM((2 * TEAM + 2, rows + 2, cols, wide), BF16),
            pltpu.VMEM((3 * 64, 9 * wide), F32),
        ],
        compiler_params=params(61),
        name="wgrad",
    )
    part = weight_call(load, other, norm, gain, bias)
    part = pl.pallas_call(
        append_kernel,
        in_specs=[vmem, vmem],
        out_specs=vmem,
        out_shape=jax.ShapeDtypeStruct((groups, 14 * step + 8, 128), F32),
        input_output_aliases={0: 0},
        compiler_params=params(16),
        name="append",
    )(part, sums)
    part = in_ranks(part)

    grad_features, grad_weight, grad_gain, grad_bias = pl.pallas_call(
        functools.partial(final_kernel, count),
        in_specs=[vmem] + [pl.BlockSpec()] * 4,
        out_shape=(
            jax.ShapeDtypeStruct((positions, chans), BF16),
            jax.ShapeDtypeStruct((9, 3, step, outs // rows), F32),
            jax.ShapeDtypeStruct((1, chans), F32),
            jax.ShapeDtypeStruct((1, chans), F32),
        ),
        compiler_params=params(16),
        name="final",
    )(part, act, feats, norm, gain)
    return (
        grad_features.reshape(features.shape),
        grad_weight.reshape(3, 3, 3, step, outs // rows),
        grad_gain.reshape(chans),
        grad_bias.reshape(chans),
    )


def solution(mesh):
    in_specs = (P("tm", "rows", None, None), P(), P(), P(), P("tm", "rows", None, None))
    out_specs = (P("tm", "rows", None, None), P(None, None, None, "tm", "rows"), P(), P())
    return jax.shard_map(on_device, mesh=mesh, in_specs=in_specs, out_specs=out_specs, check_vma=False)
```

```python
import functools

import jax
import jax.numpy as jnp
from jax import lax
from jax.experimental import pallas as pl
from jax.experimental.pallas import tpu as pltpu
from jax.sharding import PartitionSpec as P


GROUPS = 32
EPS = 1e-06
TEAM = 4
SHARES = ((0, 192), (192, 384), (384, 576), (576, 800))
HALF = 112
EDGES = ((1, 0), (0, -1), (0, 1), (1, -1), (1, 1))
F32 = jnp.float32
BF16 = jnp.bfloat16


def iota(shape, dim):
    return lax.broadcasted_iota(jnp.int32, shape, dim)


def shift_of(value):
    return value.bit_length() - 1


def exact_dot(a, ones, dims=((1,), (0,))):
    high = a.astype(BF16).astype(F32)
    rest = a - high
    mid = rest.astype(BF16).astype(F32)
    parts = jnp.concatenate([high, mid, rest - mid, jnp.zeros_like(a)], axis=0).astype(BF16)
    out = lax.dot_general(parts, ones, (dims, ((), ())), preferred_element_type=F32)
    return out[0:8] + out[8:16] + out[16:24]


def ones_where(mask):
    return jnp.where(mask, 1.0, 0.0).astype(BF16)


def members(chans, offset):
    bits = shift_of(chans // GROUPS)
    return ones_where(lax.shift_right_logical(iota((chans, 128), 0), bits) == iota((chans, 128), 1) - offset)


def sources(lane, chans, teams, spot):
    step = chans // teams
    return (lane & -step) * TEAM + spot * step + (lane & (step - 1))


def sigmoid(value):
    return 0.5 * jnp.tanh(0.5 * value) + 0.5


def col_shifts(slab):
    cols = slab.shape[0]
    wide = slab.astype(F32)
    row = iota(wide.shape, 0)
    ahead = jnp.where(row < cols - 1, pltpu.roll(wide, cols - 1, 0), 0.0).astype(BF16)
    behind = jnp.where(row > 0, pltpu.roll(wide, 1, 0), 0.0).astype(BF16)
    return ahead, slab, behind


def pack_kernel(teams, feats_ref, up_ref, later_ref, load_ref):
    positions, chans = feats_ref.shape
    cols = up_ref.shape[1]
    rows = load_ref.shape[1]
    feats = feats_ref[...]
    wide = chans // TEAM
    lane = iota((1, chans), 1)
    source = sources(lane & (wide - 1), chans, teams, lax.shift_right_logical(lane, shift_of(wide)))
    mover = ones_where(iota((chans, chans), 0) == source)
    moved = jnp.dot(feats, mover, preferred_element_type=F32).astype(BF16)
    outs = up_ref.shape[2] // rows
    for j in range(TEAM):
        for r in range(rows):
            load_ref[j, r, 0:positions, :] = moved[:, j * wide : (j + 1) * wide]
    order = lax.axis_index("tm") & (TEAM - 1)
    for r in range(rows):
        own, after = (
            jnp.concatenate(
                [ref[0, :, r * outs : (r + 1) * outs], ref[1, :, r * outs : (r + 1) * outs]], axis=1
            )
            for ref in (up_ref, later_ref)
        )
        for d in range(TEAM):

            @pl.when(order == d)
            def _():
                first, last = (value - d * cols for value in SHARES[d])
                share = jnp.concatenate([own[first:], after[0 : last - cols]], axis=0)
                size = (last - first) // 2
                for j in range(TEAM):
                    core = j % 2
                    part = share[core * size : (core + 1) * size]
                    load_ref[j, r, positions : positions + size, :] = part


def stats_kernel(feats_ref, out_ref):
    positions, chans = feats_ref.shape
    floats = feats_ref[...].astype(F32)
    first = members(chans, 0)
    second = members(chans, GROUPS)
    total = jnp.broadcast_to(jnp.sum(floats, axis=0, keepdims=True), (8, chans))
    mean = exact_dot(total, first) / (positions * (chans // GROUPS))
    diffs = floats - exact_dot(mean, first, ((1,), (1,)))[0:1]
    squares = jnp.broadcast_to(jnp.sum(diffs * diffs, axis=0, keepdims=True), (8, chans))
    out_ref[...] = jnp.broadcast_to((mean + exact_dot(squares, second))[None], out_ref.shape)


def combine_kernel(count, load_ref, stats_ref, out_ref, parts, sem):
    stats = [stats_ref[g] for g in range(stats_ref.shape[0])]
    total = stats[0]
    for stat in stats[1:]:
        total = total + stat
    mean = total / len(stats)
    spans = jnp.zeros_like(mean)
    for stat in stats:
        spans = spans + (stat - mean) * (stat - mean)
    lane = iota((8, 128), 1)
    stat = jnp.where(lane < GROUPS, mean, total + count * pltpu.roll(spans, GROUPS, 1))
    high = stat.astype(BF16).astype(F32)
    mid = (stat - high).astype(BF16).astype(F32)
    low = stat - high - mid
    row = iota((8, 128), 0)
    rows = jnp.where(row == 0, high, jnp.where(row == 1, mid, jnp.where(row == 2, low, 0.0)))
    rows = jnp.concatenate([rows, jnp.zeros_like(rows)], axis=0).astype(BF16)
    parts[...] = jnp.broadcast_to(rows[None], parts.shape)
    copy = pltpu.make_async_copy(parts, out_ref.at[:, pl.ds(out_ref.shape[1] - 16, 16)], sem)
    copy.start()
    copy.wait()


def dense_kernel(
    up_ref, above_ref, below_ref, later_ref, later_above_ref, later_below_ref, weight_ref, out_ref, slabs
):
    step = pl.program_id(0)
    time_tap = step // 3
    row_tap = step % 3
    time_index = lax.axis_index("tm")
    row_index = lax.axis_index("rows")
    positions = out_ref.shape[0]
    cols = up_ref.shape[1]

    @pl.when(step == 0)
    def _():
        out_ref[...] = jnp.zeros_like(out_ref)
        more = (time_index < lax.axis_size("tm") - 1).astype(F32)
        up_ok = (row_index > 0).astype(F32)
        down_ok = (row_index < lax.axis_size("rows") - 1).astype(F32)
        for f in range(4):
            trio = (above_ref, up_ref, below_ref) if f < 2 else (later_above_ref, later_ref, later_below_ref)
            tail = jnp.float32(1.0) if f < 2 else more
            for r, keep in enumerate((up_ok, jnp.float32(1.0), down_ok)):
                slab = (trio[r][f % 2].astype(F32) * (keep * tail)).astype(BF16)
                for c, moved in enumerate(col_shifts(slab)):
                    slabs[c, r, f] = moved

    def product(slab, c):
        return lax.dot_general(
            slab, weight_ref[0, 0, c], (((1,), (1,)), ((), ())), preferred_element_type=F32
        )

    total = out_ref[...]
    for c in range(3):
        slab = slabs[c, 2 - row_tap, pl.ds(2 - time_tap, 2)].reshape(positions, -1)
        total = total + product(slab, c)
    out_ref[...] = total

    @pl.when(jnp.logical_and(time_index == 0, time_tap == 0))
    def _():
        for c in range(3):
            both = slabs[c, 2 - row_tap, pl.ds(0, 2)].reshape(positions, -1)
            both = product(both, c)
            out_ref[0:cols, :] += both[0:cols] + both[cols:]

    @pl.when(jnp.logical_and(time_index == 0, time_tap == 1))
    def _():
        for c in range(3):
            out_ref[0:cols, :] += product(slabs[c, 2 - row_tap, 0], c)


def norm_rows(stats, chans, positions):
    devices = stats.shape[0]
    size = chans // GROUPS
    first = members(chans, 0)
    second = members(chans, GROUPS)
    total = jnp.sum(stats, axis=0, keepdims=True)
    centre = total / devices
    spans = stats - centre
    spans = jnp.sum(spans * spans, axis=0, keepdims=True)
    dims = ((1,), (1,))
    parts = exact_dot(jnp.broadcast_to(total, (8, 128)), second, dims) / (devices * positions * size)
    parts = parts + exact_dot(jnp.broadcast_to(spans, (8, 128)), first, dims) / devices
    inverse = lax.rsqrt(parts + EPS)
    centre = exact_dot(jnp.broadcast_to(centre, (8, 128)), first, dims)
    return centre, inverse


def act_kernel(
    positions, feats_ref, gain_ref, bias_ref, load_ref, dense_ref, act_ref, sums_ref, norm_ref, swap_ref
):
    chans = gain_ref.shape[1]
    start = load_ref.shape[2] - 16
    stats = []
    for j in range(load_ref.shape[0]):
        for r in range(load_ref.shape[1]):
            parts = load_ref[j, r, start:].astype(F32)
            stats.append(parts[0:1] + parts[1:2] + parts[2:3])
    swap_ref[...] = load_ref[:, :, start - HALF : start, :]
    centre, inverse = norm_rows(jnp.concatenate(stats, axis=0), chans, positions)
    norm_ref[0:8] = centre
    norm_ref[8:16] = inverse
    centre = centre[0:1]
    inverse = inverse[0:1]
    normed = (feats_ref[...].astype(F32) - centre) * inverse
    preact = normed * gain_ref[...] + bias_ref[...]
    sig = sigmoid(preact)
    act = dense_ref[...] * sig * (1.0 + preact * (1.0 - sig))
    act_ref[...] = act
    gains = jnp.sum(act * normed, axis=0, keepdims=True)
    biases = jnp.sum(act, axis=0, keepdims=True)
    pieces = chans // 128
    rows = [gains[:, p * 128 : (p + 1) * 128] for p in range(pieces)]
    rows = rows + [biases[:, p * 128 : (p + 1) * 128] for p in range(pieces)]
    sums_ref[...] = jnp.broadcast_to(jnp.concatenate(rows, axis=0)[None], sums_ref.shape)


def append_kernel(part_ref, load_ref, out_ref):
    total = load_ref[0]
    for g in range(1, load_ref.shape[0]):
        total = total + load_ref[g]
    place = (out_ref.shape[0],) + total.shape
    out_ref[:, out_ref.shape[1] - total.shape[0] :, :] = jnp.broadcast_to(total[None], place)


def weight_kernel(teams, load_ref, other_ref, norm_ref, gain_ref, bias_ref, out_ref, hidden, acc):
    time_index = lax.axis_index("tm")
    rows = load_ref.shape[1]
    cols = hidden.shape[2]
    chans = gain_ref.shape[1]
    wide = chans // TEAM
    step = chans // teams
    mover = ones_where(
        iota((chans, wide), 0) == sources(iota((1, wide), 1), chans, teams, time_index & (TEAM - 1))
    )

    def slice_of(value):
        return exact_dot(value, mover)[0:1]

    centre = slice_of(norm_ref[0:8])
    inverse = slice_of(norm_ref[8:16])
    gain = slice_of(jnp.broadcast_to(gain_ref[...], (8, chans)))
    bias = slice_of(jnp.broadcast_to(bias_ref[...], (8, chans)))

    def silu(value):
        preact = (value.astype(F32) - centre) * inverse * gain + bias
        return (preact * sigmoid(preact)).astype(BF16)

    frames = 2 * TEAM
    for f in range(frames + 2):
        hidden[f, 0] = jnp.zeros(hidden.shape[2:], BF16)
        hidden[f, rows + 1] = jnp.zeros(hidden.shape[2:], BF16)
    opening = (time_index < TEAM).astype(F32)
    for j in range(TEAM):
        for r in range(rows):
            for f in range(2):
                value = silu(load_ref[j, r, f * cols : (f + 1) * cols, :])
                hidden[2 + 2 * j + f, 1 + r] = value
                if j == 0 and f == 0:
                    value = (value.astype(F32) * opening).astype(BF16)
                    hidden[0, 1 + r] = value
                    hidden[1, 1 + r] = value

    base = 2 * cols

    def pieces_of(q, r):
        pieces = []
        for d, (begin, close) in enumerate(SHARES):
            size = (close - begin) // 2
            for half in range(2):
                first = max(q * cols, begin + half * size) - begin - half * size
                last = min((q + 1) * cols, begin + (half + 1) * size) - begin - half * size
                if first < last:
                    mine = load_ref[d, r, base + first : base + last, :]
                    pieces.append(jnp.where((time_index & 1) == half, mine, other_ref[d, r, first:last, :]))
        return pieces

    lanes = iota((cols, 128), 1) < 64
    more = (time_index < lax.axis_size("tm") - TEAM).astype(F32)
    for j in range(TEAM + 1):
        halves = [[], []]
        for r in range(rows):
            pair = jnp.concatenate(pieces_of(j, r), axis=0).astype(F32)
            if j == TEAM:
                pair = pair * more
            row = iota(pair.shape, 0)
            ahead = jnp.where(row < cols - 1, pltpu.roll(pair, cols - 1, 0), 0.0)
            behind = jnp.where(row > 0, pltpu.roll(pair, 1, 0), 0.0)
            left = jnp.where(lanes, ahead, pltpu.roll(pair, 64, 1))
            right = jnp.where(lanes, pltpu.roll(ahead, 64, 1), pair)
            halves[0].append(jnp.concatenate([left, behind[:, 0:64]], axis=1))
            halves[1].append(jnp.concatenate([right, behind[:, 64:128]], axis=1))

        def taps_of(frame, depth):
            taps = [
                hidden[frame + a, b : b + rows].reshape(rows * cols, wide) for a in range(depth) for b in range(3)
            ]
            return jnp.concatenate(taps, axis=1)

        sides = [jnp.concatenate(halves[f], axis=0).astype(BF16) for f in range(2)]
        if j < TEAM:
            jobs = [(jnp.concatenate(sides, axis=0), [taps_of(2 * j + f, 3) for f in range(2)], 3)]
        else:
            jobs = [(sides[f], [taps_of(2 * j + f, 2 - f)], 2 - f) for f in range(2)]
        for side, taps, depth in jobs:
            term = lax.dot_general(
                side, jnp.concatenate(taps, axis=0), (((0,), (0,)), ((), ())), preferred_element_type=F32
            )
            if j == 0:
                acc[...] = term
            else:
                acc[:, 0 : 3 * depth * wide] += term

    groups = out_ref.shape[0]
    tail = None
    for ab in range(9):
        block = acc[:, ab * wide : (ab + 1) * wide].T
        out_ref[:, ab * step : (ab + 1) * step, :] = block[:, 0:128].reshape(groups, step, 128)
        last = block[:, 128:192]
        if ab % 2 == 0:
            tail = last
        if ab % 2 == 1 or ab == 8:
            both = jnp.concatenate([tail, last], axis=1)
            at = (9 + ab // 2) * step
            out_ref[:, at : at + step, :] = both.reshape(groups, step, 128)


def final_kernel(
    count, load_ref, act_ref, feats_ref, norm_ref, gain_ref, out_ref, grad_ref, gain_out_ref, bias_out_ref
):
    chans = gain_ref.shape[1]
    pieces = chans // 128
    step = grad_ref.shape[2]
    total = load_ref[0]
    for g in range(1, load_ref.shape[0]):
        total = total + load_ref[g]
    for ab in range(9):
        part = total[ab * step : (ab + 1) * step]
        grad_ref[ab, 0] = part[:, 0:64]
        grad_ref[ab, 1] = part[:, 64:128]
        at = (9 + ab // 2) * step
        side = 64 * (ab % 2)
        grad_ref[ab, 2] = total[at : at + step, side : side + 64]
    total = total[14 * step :]
    gains = jnp.concatenate([total[p : p + 1] for p in range(pieces)], axis=1)
    biases = jnp.concatenate([total[pieces + p : pieces + p + 1] for p in range(pieces)], axis=1)
    gain_out_ref[...] = gains
    bias_out_ref[...] = biases
    gain = gain_ref[...]
    owner = members(chans, 0)

    def spread(value):
        value = exact_dot(jnp.broadcast_to(value, (8, chans)), owner) / count
        return exact_dot(value, owner, ((1,), (1,)))[0:1]

    first = spread(gain * biases)
    second = spread(gain * gains)
    centre = norm_ref[0:1]
    inverse = norm_ref[8:9]
    normed = (feats_ref[...].astype(F32) - centre) * inverse
    out_ref[...] = (inverse * (act_ref[...] * gain - first - normed * second)).astype(BF16)


def on_device(features, norm_gain, norm_bias, weight, upstream):
    frames, rows_dev, cols, chans = features.shape
    outs = upstream.shape[3]
    tms = lax.axis_size("tm")
    rows = lax.axis_size("rows")
    devices = tms * rows
    positions = frames * rows_dev * cols
    step = chans // tms
    groups = tms // TEAM
    wide = chans // TEAM
    count = positions * devices * (chans // GROUPS)
    vmem = pl.BlockSpec(memory_space=pltpu.VMEM)
    far = pl.BlockSpec(memory_space=pltpu.HBM)

    def params(mebibytes):
        return pltpu.CompilerParams(vmem_limit_bytes=mebibytes * 1024 * 1024)

    feats = features.reshape(positions, chans)
    ups = upstream.reshape(frames, cols, outs)
    gain = norm_gain.reshape(1, chans)
    bias = norm_bias.reshape(1, chans)
    size = TEAM * rows
    length = positions + HALF + 16
    teams = [[size * g + i for i in range(size)] for g in range(groups)]
    ranks = [[TEAM * g + j for g in range(groups)] for j in range(TEAM)]

    def in_teams(value):
        return lax.all_to_all(value, ("tm", "rows"), 0, 0, tiled=True, axis_index_groups=teams)

    def in_ranks(value):
        return lax.all_to_all(value, "tm", 0, 0, tiled=True, axis_index_groups=ranks)

    def neighbour(tm_step, row_step):
        pairs = [
            (((t + tm_step) % tms) * rows + (r + row_step) % rows, t * rows + r)
            for t in range(tms)
            for r in range(rows)
        ]
        return lax.ppermute(ups, ("tm", "rows"), pairs)

    halos = [neighbour(a, b) for a, b in EDGES]

    stats = pl.pallas_call(
        stats_kernel,
        out_shape=jax.ShapeDtypeStruct((groups, 8, 128), F32),
        compiler_params=params(62),
        name="stats",
    )(feats)
    stats = in_ranks(stats)
    pack_call = pl.pallas_call(
        functools.partial(pack_kernel, tms),
        out_shape=jax.ShapeDtypeStruct((TEAM, rows, length, wide), BF16),
        compiler_params=params(62),
        name="pack",
    )
    load = pack_call(feats, ups, halos[0])
    load = pl.pallas_call(
        functools.partial(combine_kernel, float(positions * (chans // GROUPS))),
        in_specs=[far, vmem],
        out_specs=far,
        out_shape=jax.ShapeDtypeStruct((size, length, wide), BF16),
        scratch_shapes=[pltpu.VMEM((size, 16, wide), BF16), pltpu.SemaphoreType.DMA],
        input_output_aliases={0: 0},
        compiler_params=params(61),
        name="combine",
    )(load.reshape(size, length, wide), stats)
    load = in_teams(load).reshape(TEAM, rows, length, wide)

    def whole(shape):
        return pl.BlockSpec(shape, lambda *s: (0,) * len(shape))

    dense_call = pl.pallas_call(
        dense_kernel,
        grid=(9,),
        in_specs=[
            *[whole((frames, cols, outs))] * 6,
            pl.BlockSpec((1, 1, 3, chans, outs), lambda s: (s // 3, s % 3, 0, 0, 0)),
        ],
        out_specs=whole((positions, chans)),
        out_shape=jax.ShapeDtypeStruct((positions, chans), F32),
        scratch_shapes=[pltpu.VMEM((3, 3, 4, cols, outs), BF16)],
        compiler_params=params(62),
        name="dense",
    )
    dense = dense_call(ups, halos[1], halos[2], halos[0], halos[3], halos[4], weight)

    act, sums, norm, swap = pl.pallas_call(
        functools.partial(act_kernel, positions * groups),
        in_specs=[pl.BlockSpec()] * 3 + [vmem, pl.BlockSpec()],
        out_shape=(
            jax.ShapeDtypeStruct((positions, chans), F32),
            jax.ShapeDtypeStruct((size, 8, 128), F32),
            jax.ShapeDtypeStruct((16, chans), F32),
            jax.ShapeDtypeStruct((TEAM, rows, HALF, wide), BF16),
        ),
        compiler_params=params(60),
        name="act",
    )(feats, gain, bias, load, dense)
    other = lax.ppermute(swap, "tm", [(t, t ^ 1) for t in range(tms)])
    sums = in_teams(sums)

    weight_call = pl.pallas_call(
        functools.partial(weight_kernel, tms),
        in_specs=[vmem] + [pl.BlockSpec()] * 4,
        out_specs=vmem,
        out_shape=jax.ShapeDtypeStruct((groups, 14 * step + 8, 128), F32),
        scratch_shapes=[
            pltpu.VMEM((2 * TEAM + 2, rows + 2, cols, wide), BF16),
            pltpu.VMEM((3 * 64, 9 * wide), F32),
        ],
        compiler_params=params(52),
        name="wgrad",
    )
    part = weight_call(load, other, norm, gain, bias)
    part = pl.pallas_call(
        append_kernel,
        in_specs=[vmem, vmem],
        out_specs=vmem,
        out_shape=jax.ShapeDtypeStruct((groups, 14 * step + 8, 128), F32),
        input_output_aliases={0: 0},
        compiler_params=params(16),
        name="append",
    )(part, sums)
    part = in_ranks(part)

    grad_features, grad_weight, grad_gain, grad_bias = pl.pallas_call(
        functools.partial(final_kernel, count),
        in_specs=[vmem] + [pl.BlockSpec()] * 4,
        out_shape=(
            jax.ShapeDtypeStruct((positions, chans), BF16),
            jax.ShapeDtypeStruct((9, 3, step, outs // rows), F32),
            jax.ShapeDtypeStruct((1, chans), F32),
            jax.ShapeDtypeStruct((1, chans), F32),
        ),
        compiler_params=params(16),
        name="final",
    )(part, act, feats, norm, gain)
    return (
        grad_features.reshape(features.shape),
        grad_weight.reshape(3, 3, 3, step, outs // rows),
        grad_gain.reshape(chans),
        grad_bias.reshape(chans),
    )


def solution(mesh):
    in_specs = (P("tm", "rows", None, None), P(), P(), P(), P("tm", "rows", None, None))
    out_specs = (P("tm", "rows", None, None), P(None, None, None, "tm", "rows"), P(), P())
    return jax.shard_map(on_device, mesh=mesh, in_specs=in_specs, out_specs=out_specs, check_vma=False)
```

```python
import functools

import jax
import jax.numpy as jnp
from jax import lax
from jax.experimental import pallas as pl
from jax.experimental.pallas import tpu as pltpu
from jax.sharding import PartitionSpec as P


GROUPS = 32
EPS = 1e-06
TEAM = 4
SHARES = ((0, 192), (192, 384), (384, 576), (576, 800))
HALF = 112
EDGES = ((1, 0), (0, -1), (0, 1), (1, -1), (1, 1))
F32 = jnp.float32
BF16 = jnp.bfloat16


def iota(shape, dim):
    return lax.broadcasted_iota(jnp.int32, shape, dim)


def shift_of(value):
    return value.bit_length() - 1


def exact_dot(a, ones, dims=((1,), (0,))):
    high = a.astype(BF16).astype(F32)
    rest = a - high
    mid = rest.astype(BF16).astype(F32)
    parts = jnp.concatenate([high, mid, rest - mid, jnp.zeros_like(a)], axis=0).astype(BF16)
    out = lax.dot_general(parts, ones, (dims, ((), ())), preferred_element_type=F32)
    return out[0:8] + out[8:16] + out[16:24]


def ones_where(mask):
    return jnp.where(mask, 1.0, 0.0).astype(BF16)


def members(chans, offset):
    bits = shift_of(chans // GROUPS)
    return ones_where(lax.shift_right_logical(iota((chans, 128), 0), bits) == iota((chans, 128), 1) - offset)


def sources(lane, chans, teams, spot):
    step = chans // teams
    return (lane & -step) * TEAM + spot * step + (lane & (step - 1))


def sigmoid(value):
    return 0.5 * jnp.tanh(0.5 * value) + 0.5


def col_shifts(slab):
    cols = slab.shape[0]
    wide = slab.astype(F32)
    row = iota(wide.shape, 0)
    ahead = jnp.where(row < cols - 1, pltpu.roll(wide, cols - 1, 0), 0.0).astype(BF16)
    behind = jnp.where(row > 0, pltpu.roll(wide, 1, 0), 0.0).astype(BF16)
    return ahead, slab, behind


def pack_kernel(teams, count, feats_ref, up_ref, later_ref, stats_ref, load_ref):
    positions, chans = feats_ref.shape
    cols = up_ref.shape[1]
    rows = load_ref.shape[1]
    feats = feats_ref[...]
    wide = chans // TEAM
    lane = iota((1, chans), 1)
    source = sources(lane & (wide - 1), chans, teams, lax.shift_right_logical(lane, shift_of(wide)))
    mover = ones_where(iota((chans, chans), 0) == source)
    moved = jnp.dot(feats, mover, preferred_element_type=F32).astype(BF16)
    outs = up_ref.shape[2] // rows
    for j in range(TEAM):
        for r in range(rows):
            load_ref[j, r, 0:positions, :] = moved[:, j * wide : (j + 1) * wide]
    order = lax.axis_index("tm") & (TEAM - 1)
    for r in range(rows):
        own, after = (
            jnp.concatenate(
                [ref[0, :, r * outs : (r + 1) * outs], ref[1, :, r * outs : (r + 1) * outs]], axis=1
            )
            for ref in (up_ref, later_ref)
        )
        for d in range(TEAM):

            @pl.when(order == d)
            def _():
                first, last = (value - d * cols for value in SHARES[d])
                share = jnp.concatenate([own[first:], after[0 : last - cols]], axis=0)
                size = (last - first) // 2
                for j in range(TEAM):
                    core = j % 2
                    part = share[core * size : (core + 1) * size]
                    load_ref[j, r, positions : positions + size, :] = part
    parts = joined_stats(count, stats_ref)
    for j in range(TEAM):
        for r in range(rows):
            load_ref[j, r, positions + HALF :, :] = parts


def stats_kernel(feats_ref, out_ref):
    positions, chans = feats_ref.shape
    floats = feats_ref[...].astype(F32)
    first = members(chans, 0)
    second = members(chans, GROUPS)
    total = jnp.broadcast_to(jnp.sum(floats, axis=0, keepdims=True), (8, chans))
    mean = exact_dot(total, first) / (positions * (chans // GROUPS))
    diffs = floats - exact_dot(mean, first, ((1,), (1,)))[0:1]
    squares = jnp.broadcast_to(jnp.sum(diffs * diffs, axis=0, keepdims=True), (8, chans))
    out_ref[...] = jnp.broadcast_to((mean + exact_dot(squares, second))[None], out_ref.shape)


def joined_stats(count, stats_ref):
    stats = [stats_ref[g] for g in range(stats_ref.shape[0])]
    total = stats[0]
    for stat in stats[1:]:
        total = total + stat
    mean = total / len(stats)
    spans = jnp.zeros_like(mean)
    for stat in stats:
        spans = spans + (stat - mean) * (stat - mean)
    lane = iota((8, 128), 1)
    stat = jnp.where(lane < GROUPS, mean, total + count * pltpu.roll(spans, GROUPS, 1))
    high = stat.astype(BF16).astype(F32)
    mid = (stat - high).astype(BF16).astype(F32)
    low = stat - high - mid
    row = iota((8, 128), 0)
    parts = jnp.where(row == 0, high, jnp.where(row == 1, mid, jnp.where(row == 2, low, 0.0)))
    return jnp.concatenate([parts, jnp.zeros_like(parts)], axis=0).astype(BF16)


def dense_kernel(
    up_ref, above_ref, below_ref, later_ref, later_above_ref, later_below_ref, weight_ref, out_ref, slabs
):
    step = pl.program_id(0)
    time_tap = step // 3
    row_tap = step % 3
    time_index = lax.axis_index("tm")
    row_index = lax.axis_index("rows")
    positions = out_ref.shape[0]
    cols = up_ref.shape[1]

    @pl.when(step == 0)
    def _():
        out_ref[...] = jnp.zeros_like(out_ref)
        more = (time_index < lax.axis_size("tm") - 1).astype(F32)
        up_ok = (row_index > 0).astype(F32)
        down_ok = (row_index < lax.axis_size("rows") - 1).astype(F32)
        for f in range(4):
            trio = (above_ref, up_ref, below_ref) if f < 2 else (later_above_ref, later_ref, later_below_ref)
            tail = jnp.float32(1.0) if f < 2 else more
            for r, keep in enumerate((up_ok, jnp.float32(1.0), down_ok)):
                slab = (trio[r][f % 2].astype(F32) * (keep * tail)).astype(BF16)
                for c, moved in enumerate(col_shifts(slab)):
                    slabs[c, r, f] = moved

    def product(slab, c):
        return lax.dot_general(
            slab, weight_ref[0, 0, c], (((1,), (1,)), ((), ())), preferred_element_type=F32
        )

    total = out_ref[...]
    for c in range(3):
        slab = slabs[c, 2 - row_tap, pl.ds(2 - time_tap, 2)].reshape(positions, -1)
        total = total + product(slab, c)
    out_ref[...] = total

    @pl.when(jnp.logical_and(time_index == 0, time_tap == 0))
    def _():
        for c in range(3):
            both = slabs[c, 2 - row_tap, pl.ds(0, 2)].reshape(positions, -1)
            both = product(both, c)
            out_ref[0:cols, :] += both[0:cols] + both[cols:]

    @pl.when(jnp.logical_and(time_index == 0, time_tap == 1))
    def _():
        for c in range(3):
            out_ref[0:cols, :] += product(slabs[c, 2 - row_tap, 0], c)


def norm_rows(stats, chans, positions):
    devices = stats.shape[0]
    size = chans // GROUPS
    first = members(chans, 0)
    second = members(chans, GROUPS)
    total = jnp.sum(stats, axis=0, keepdims=True)
    centre = total / devices
    spans = stats - centre
    spans = jnp.sum(spans * spans, axis=0, keepdims=True)
    dims = ((1,), (1,))
    parts = exact_dot(jnp.broadcast_to(total, (8, 128)), second, dims) / (devices * positions * size)
    parts = parts + exact_dot(jnp.broadcast_to(spans, (8, 128)), first, dims) / devices
    inverse = lax.rsqrt(parts + EPS)
    centre = exact_dot(jnp.broadcast_to(centre, (8, 128)), first, dims)
    return centre, inverse


def act_kernel(
    positions, feats_ref, gain_ref, bias_ref, load_ref, dense_ref, act_ref, sums_ref, norm_ref, swap_ref
):
    chans = gain_ref.shape[1]
    start = load_ref.shape[2] - 16
    stats = []
    for j in range(load_ref.shape[0]):
        for r in range(load_ref.shape[1]):
            parts = load_ref[j, r, start:].astype(F32)
            stats.append(parts[0:1] + parts[1:2] + parts[2:3])
    swap_ref[...] = load_ref[:, :, start - HALF : start, :]
    centre, inverse = norm_rows(jnp.concatenate(stats, axis=0), chans, positions)
    norm_ref[0:8] = centre
    norm_ref[8:16] = inverse
    centre = centre[0:1]
    inverse = inverse[0:1]
    normed = (feats_ref[...].astype(F32) - centre) * inverse
    preact = normed * gain_ref[...] + bias_ref[...]
    sig = sigmoid(preact)
    act = dense_ref[...] * sig * (1.0 + preact * (1.0 - sig))
    act_ref[...] = act
    gains = jnp.sum(act * normed, axis=0, keepdims=True)
    biases = jnp.sum(act, axis=0, keepdims=True)
    pieces = chans // 128
    rows = [gains[:, p * 128 : (p + 1) * 128] for p in range(pieces)]
    rows = rows + [biases[:, p * 128 : (p + 1) * 128] for p in range(pieces)]
    sums_ref[...] = jnp.broadcast_to(jnp.concatenate(rows, axis=0)[None], sums_ref.shape)


def append_kernel(part_ref, load_ref, out_ref):
    total = load_ref[0]
    for g in range(1, load_ref.shape[0]):
        total = total + load_ref[g]
    place = (out_ref.shape[0],) + total.shape
    out_ref[:, out_ref.shape[1] - total.shape[0] :, :] = jnp.broadcast_to(total[None], place)


def weight_kernel(teams, load_ref, other_ref, norm_ref, gain_ref, bias_ref, out_ref, hidden, acc):
    time_index = lax.axis_index("tm")
    rows = load_ref.shape[1]
    cols = hidden.shape[2]
    chans = gain_ref.shape[1]
    wide = chans // TEAM
    step = chans // teams
    mover = ones_where(
        iota((chans, wide), 0) == sources(iota((1, wide), 1), chans, teams, time_index & (TEAM - 1))
    )

    def slice_of(value):
        return exact_dot(value, mover)[0:1]

    centre = slice_of(norm_ref[0:8])
    inverse = slice_of(norm_ref[8:16])
    gain = slice_of(jnp.broadcast_to(gain_ref[...], (8, chans)))
    bias = slice_of(jnp.broadcast_to(bias_ref[...], (8, chans)))

    def silu(value):
        preact = (value.astype(F32) - centre) * inverse * gain + bias
        return (preact * sigmoid(preact)).astype(BF16)

    frames = 2 * TEAM
    for f in range(frames + 2):
        hidden[f, 0] = jnp.zeros(hidden.shape[2:], BF16)
        hidden[f, rows + 1] = jnp.zeros(hidden.shape[2:], BF16)
    opening = (time_index < TEAM).astype(F32)
    for j in range(TEAM):
        for r in range(rows):
            for f in range(2):
                value = silu(load_ref[j, r, f * cols : (f + 1) * cols, :])
                hidden[2 + 2 * j + f, 1 + r] = value
                if j == 0 and f == 0:
                    value = (value.astype(F32) * opening).astype(BF16)
                    hidden[0, 1 + r] = value
                    hidden[1, 1 + r] = value

    base = 2 * cols

    def pieces_of(q, r):
        pieces = []
        for d, (begin, close) in enumerate(SHARES):
            size = (close - begin) // 2
            for half in range(2):
                first = max(q * cols, begin + half * size) - begin - half * size
                last = min((q + 1) * cols, begin + (half + 1) * size) - begin - half * size
                if first < last:
                    mine = load_ref[d, r, base + first : base + last, :]
                    pieces.append(jnp.where((time_index & 1) == half, mine, other_ref[d, r, first:last, :]))
        return pieces

    lanes = iota((cols, 128), 1) < 64
    more = (time_index < lax.axis_size("tm") - TEAM).astype(F32)
    for j in range(TEAM + 1):
        halves = [[], []]
        for r in range(rows):
            pair = jnp.concatenate(pieces_of(j, r), axis=0).astype(F32)
            if j == TEAM:
                pair = pair * more
            row = iota(pair.shape, 0)
            ahead = jnp.where(row < cols - 1, pltpu.roll(pair, cols - 1, 0), 0.0)
            behind = jnp.where(row > 0, pltpu.roll(pair, 1, 0), 0.0)
            left = jnp.where(lanes, ahead, pltpu.roll(pair, 64, 1))
            right = jnp.where(lanes, pltpu.roll(ahead, 64, 1), pair)
            halves[0].append(jnp.concatenate([left, behind[:, 0:64]], axis=1))
            halves[1].append(jnp.concatenate([right, behind[:, 64:128]], axis=1))

        def taps_of(frame, depth):
            taps = [
                hidden[frame + a, b : b + rows].reshape(rows * cols, wide) for a in range(depth) for b in range(3)
            ]
            return jnp.concatenate(taps, axis=1)

        sides = [jnp.concatenate(halves[f], axis=0).astype(BF16) for f in range(2)]
        if j < TEAM:
            jobs = [(jnp.concatenate(sides, axis=0), [taps_of(2 * j + f, 3) for f in range(2)], 3)]
        else:
            jobs = [(sides[f], [taps_of(2 * j + f, 2 - f)], 2 - f) for f in range(2)]
        for side, taps, depth in jobs:
            term = lax.dot_general(
                side, jnp.concatenate(taps, axis=0), (((0,), (0,)), ((), ())), preferred_element_type=F32
            )
            if j == 0:
                acc[...] = term
            else:
                acc[:, 0 : 3 * depth * wide] += term

    groups = out_ref.shape[0]
    tail = None
    for ab in range(9):
        block = acc[:, ab * wide : (ab + 1) * wide].T
        out_ref[:, ab * step : (ab + 1) * step, :] = block[:, 0:128].reshape(groups, step, 128)
        last = block[:, 128:192]
        if ab % 2 == 0:
            tail = last
        if ab % 2 == 1 or ab == 8:
            both = jnp.concatenate([tail, last], axis=1)
            at = (9 + ab // 2) * step
            out_ref[:, at : at + step, :] = both.reshape(groups, step, 128)


def final_kernel(
    count, load_ref, act_ref, feats_ref, norm_ref, gain_ref, out_ref, grad_ref, gain_out_ref, bias_out_ref
):
    chans = gain_ref.shape[1]
    pieces = chans // 128
    step = grad_ref.shape[2]
    total = load_ref[0]
    for g in range(1, load_ref.shape[0]):
        total = total + load_ref[g]
    for ab in range(9):
        part = total[ab * step : (ab + 1) * step]
        grad_ref[ab, 0] = part[:, 0:64]
        grad_ref[ab, 1] = part[:, 64:128]
        at = (9 + ab // 2) * step
        side = 64 * (ab % 2)
        grad_ref[ab, 2] = total[at : at + step, side : side + 64]
    total = total[14 * step :]
    gains = jnp.concatenate([total[p : p + 1] for p in range(pieces)], axis=1)
    biases = jnp.concatenate([total[pieces + p : pieces + p + 1] for p in range(pieces)], axis=1)
    gain_out_ref[...] = gains
    bias_out_ref[...] = biases
    gain = gain_ref[...]
    owner = members(chans, 0)

    def spread(value):
        value = exact_dot(jnp.broadcast_to(value, (8, chans)), owner) / count
        return exact_dot(value, owner, ((1,), (1,)))[0:1]

    first = spread(gain * biases)
    second = spread(gain * gains)
    centre = norm_ref[0:1]
    inverse = norm_ref[8:9]
    normed = (feats_ref[...].astype(F32) - centre) * inverse
    out_ref[...] = (inverse * (act_ref[...] * gain - first - normed * second)).astype(BF16)


def on_device(features, norm_gain, norm_bias, weight, upstream):
    frames, rows_dev, cols, chans = features.shape
    outs = upstream.shape[3]
    tms = lax.axis_size("tm")
    rows = lax.axis_size("rows")
    devices = tms * rows
    positions = frames * rows_dev * cols
    step = chans // tms
    groups = tms // TEAM
    wide = chans // TEAM
    count = positions * devices * (chans // GROUPS)
    vmem = pl.BlockSpec(memory_space=pltpu.VMEM)

    def params(mebibytes):
        return pltpu.CompilerParams(vmem_limit_bytes=mebibytes * 1024 * 1024)

    feats = features.reshape(positions, chans)
    ups = upstream.reshape(frames, cols, outs)
    gain = norm_gain.reshape(1, chans)
    bias = norm_bias.reshape(1, chans)
    size = TEAM * rows
    length = positions + HALF + 16
    teams = [[size * g + i for i in range(size)] for g in range(groups)]
    ranks = [[TEAM * g + j for g in range(groups)] for j in range(TEAM)]

    def in_teams(value):
        return lax.all_to_all(value, ("tm", "rows"), 0, 0, tiled=True, axis_index_groups=teams)

    def in_ranks(value):
        return lax.all_to_all(value, "tm", 0, 0, tiled=True, axis_index_groups=ranks)

    def neighbour(tm_step, row_step):
        pairs = [
            (((t + tm_step) % tms) * rows + (r + row_step) % rows, t * rows + r)
            for t in range(tms)
            for r in range(rows)
        ]
        return lax.ppermute(ups, ("tm", "rows"), pairs)

    halos = [neighbour(a, b) for a, b in EDGES]

    stats = pl.pallas_call(
        stats_kernel,
        out_shape=jax.ShapeDtypeStruct((groups, 8, 128), F32),
        compiler_params=params(62),
        name="stats",
    )(feats)
    stats = in_ranks(stats)
    pack_call = pl.pallas_call(
        functools.partial(pack_kernel, tms, float(positions * (chans // GROUPS))),
        in_specs=[pl.BlockSpec()] * 3 + [vmem],
        out_shape=jax.ShapeDtypeStruct((TEAM, rows, length, wide), BF16),
        compiler_params=params(62),
        name="pack",
    )
    load = pack_call(feats, ups, halos[0], stats)
    load = in_teams(load.reshape(size, length, wide)).reshape(TEAM, rows, length, wide)

    def whole(shape):
        return pl.BlockSpec(shape, lambda *s: (0,) * len(shape))

    dense_call = pl.pallas_call(
        dense_kernel,
        grid=(9,),
        in_specs=[
            *[whole((frames, cols, outs))] * 6,
            pl.BlockSpec((1, 1, 3, chans, outs), lambda s: (s // 3, s % 3, 0, 0, 0)),
        ],
        out_specs=whole((positions, chans)),
        out_shape=jax.ShapeDtypeStruct((positions, chans), F32),
        scratch_shapes=[pltpu.VMEM((3, 3, 4, cols, outs), BF16)],
        compiler_params=params(62),
        name="dense",
    )
    dense = dense_call(ups, halos[1], halos[2], halos[0], halos[3], halos[4], weight)

    act, sums, norm, swap = pl.pallas_call(
        functools.partial(act_kernel, positions * groups),
        in_specs=[pl.BlockSpec()] * 3 + [vmem, pl.BlockSpec()],
        out_shape=(
            jax.ShapeDtypeStruct((positions, chans), F32),
            jax.ShapeDtypeStruct((size, 8, 128), F32),
            jax.ShapeDtypeStruct((16, chans), F32),
            jax.ShapeDtypeStruct((TEAM, rows, HALF, wide), BF16),
        ),
        compiler_params=params(60),
        name="act",
    )(feats, gain, bias, load, dense)
    other = lax.ppermute(swap, "tm", [(t, t ^ 1) for t in range(tms)])
    sums = in_teams(sums)

    weight_call = pl.pallas_call(
        functools.partial(weight_kernel, tms),
        in_specs=[vmem] + [pl.BlockSpec()] * 4,
        out_specs=vmem,
        out_shape=jax.ShapeDtypeStruct((groups, 14 * step + 8, 128), F32),
        scratch_shapes=[
            pltpu.VMEM((2 * TEAM + 2, rows + 2, cols, wide), BF16),
            pltpu.VMEM((3 * 64, 9 * wide), F32),
        ],
        compiler_params=params(52),
        name="wgrad",
    )
    part = weight_call(load, other, norm, gain, bias)
    part = pl.pallas_call(
        append_kernel,
        in_specs=[vmem, vmem],
        out_specs=vmem,
        out_shape=jax.ShapeDtypeStruct((groups, 14 * step + 8, 128), F32),
        input_output_aliases={0: 0},
        compiler_params=params(16),
        name="append",
    )(part, sums)
    part = in_ranks(part)

    grad_features, grad_weight, grad_gain, grad_bias = pl.pallas_call(
        functools.partial(final_kernel, count),
        in_specs=[vmem] + [pl.BlockSpec()] * 4,
        out_shape=(
            jax.ShapeDtypeStruct((positions, chans), BF16),
            jax.ShapeDtypeStruct((9, 3, step, outs // rows), F32),
            jax.ShapeDtypeStruct((1, chans), F32),
            jax.ShapeDtypeStruct((1, chans), F32),
        ),
        compiler_params=params(16),
        name="final",
    )(part, act, feats, norm, gain)
    return (
        grad_features.reshape(features.shape),
        grad_weight.reshape(3, 3, 3, step, outs // rows),
        grad_gain.reshape(chans),
        grad_bias.reshape(chans),
    )


def solution(mesh):
    in_specs = (P("tm", "rows", None, None), P(), P(), P(), P("tm", "rows", None, None))
    out_specs = (P("tm", "rows", None, None), P(None, None, None, "tm", "rows"), P(), P())
    return jax.shard_map(on_device, mesh=mesh, in_specs=in_specs, out_specs=out_specs, check_vma=False)
```

```python
import functools

import jax
import jax.numpy as jnp
from jax import lax
from jax.experimental import pallas as pl
from jax.experimental.pallas import tpu as pltpu
from jax.sharding import PartitionSpec as P


GROUPS = 32
EPS = 1e-06
TEAM = 4
SHARES = ((0, 192), (192, 384), (384, 576), (576, 800))
HALF = 112
EDGES = ((1, 0), (0, -1), (0, 1), (1, -1), (1, 1))
F32 = jnp.float32
BF16 = jnp.bfloat16


def iota(shape, dim):
    return lax.broadcasted_iota(jnp.int32, shape, dim)


def shift_of(value):
    return value.bit_length() - 1


def exact_dot(a, ones, dims=((1,), (0,))):
    high = a.astype(BF16).astype(F32)
    rest = a - high
    mid = rest.astype(BF16).astype(F32)
    parts = jnp.concatenate([high, mid, rest - mid, jnp.zeros_like(a)], axis=0).astype(BF16)
    out = lax.dot_general(parts, ones, (dims, ((), ())), preferred_element_type=F32)
    return out[0:8] + out[8:16] + out[16:24]


def ones_where(mask):
    return jnp.where(mask, 1.0, 0.0).astype(BF16)


def members(chans, offset):
    bits = shift_of(chans // GROUPS)
    return ones_where(lax.shift_right_logical(iota((chans, 128), 0), bits) == iota((chans, 128), 1) - offset)


def sources(lane, chans, teams, spot):
    step = chans // teams
    return (lane & -step) * TEAM + spot * step + (lane & (step - 1))


def sigmoid(value):
    return 0.5 * jnp.tanh(0.5 * value) + 0.5


def col_shifts(slab):
    cols = slab.shape[0]
    wide = slab.astype(F32)
    row = iota(wide.shape, 0)
    ahead = jnp.where(row < cols - 1, pltpu.roll(wide, cols - 1, 0), 0.0).astype(BF16)
    behind = jnp.where(row > 0, pltpu.roll(wide, 1, 0), 0.0).astype(BF16)
    return ahead, slab, behind


def pack_kernel(teams, count, feats_ref, up_ref, later_ref, stats_ref, load_ref):
    positions, chans = feats_ref.shape
    cols = up_ref.shape[1]
    rows = load_ref.shape[1]
    feats = feats_ref[...]
    wide = chans // TEAM
    lane = iota((1, chans), 1)
    source = sources(lane & (wide - 1), chans, teams, lax.shift_right_logical(lane, shift_of(wide)))
    mover = ones_where(iota((chans, chans), 0) == source)
    moved = jnp.dot(feats, mover, preferred_element_type=F32).astype(BF16)
    outs = up_ref.shape[2] // rows
    for j in range(TEAM):
        for r in range(rows):
            load_ref[j, r, 0:positions, :] = moved[:, j * wide : (j + 1) * wide]
    order = lax.axis_index("tm") & (TEAM - 1)
    for r in range(rows):
        own, after = (
            jnp.concatenate(
                [ref[0, :, r * outs : (r + 1) * outs], ref[1, :, r * outs : (r + 1) * outs]], axis=1
            )
            for ref in (up_ref, later_ref)
        )
        for d in range(TEAM):

            @pl.when(order == d)
            def _():
                first, last = (value - d * cols for value in SHARES[d])
                share = jnp.concatenate([own[first:], after[0 : last - cols]], axis=0)
                size = (last - first) // 2
                for j in range(TEAM):
                    core = j % 2
                    part = share[core * size : (core + 1) * size]
                    load_ref[j, r, positions : positions + size, :] = part
    parts = joined_stats(count, stats_ref)
    for j in range(TEAM):
        for r in range(rows):
            load_ref[j, r, positions + HALF :, :] = parts


def stats_kernel(feats_ref, out_ref):
    positions, chans = feats_ref.shape
    floats = feats_ref[...].astype(F32)
    first = members(chans, 0)
    second = members(chans, GROUPS)
    total = jnp.broadcast_to(jnp.sum(floats, axis=0, keepdims=True), (8, chans))
    mean = exact_dot(total, first) / (positions * (chans // GROUPS))
    diffs = floats - exact_dot(mean, first, ((1,), (1,)))[0:1]
    squares = jnp.broadcast_to(jnp.sum(diffs * diffs, axis=0, keepdims=True), (8, chans))
    out_ref[...] = jnp.broadcast_to((mean + exact_dot(squares, second))[None], out_ref.shape)


def joined_stats(count, stats_ref):
    stats = [stats_ref[g] for g in range(stats_ref.shape[0])]
    total = stats[0]
    for stat in stats[1:]:
        total = total + stat
    mean = total / len(stats)
    spans = jnp.zeros_like(mean)
    for stat in stats:
        spans = spans + (stat - mean) * (stat - mean)
    lane = iota((8, 128), 1)
    stat = jnp.where(lane < GROUPS, mean, total + count * pltpu.roll(spans, GROUPS, 1))
    high = stat.astype(BF16).astype(F32)
    mid = (stat - high).astype(BF16).astype(F32)
    low = stat - high - mid
    row = iota((8, 128), 0)
    parts = jnp.where(row == 0, high, jnp.where(row == 1, mid, jnp.where(row == 2, low, 0.0)))
    return jnp.concatenate([parts, jnp.zeros_like(parts)], axis=0).astype(BF16)


def dense_kernel(
    up_ref, above_ref, below_ref, later_ref, later_above_ref, later_below_ref, weight_ref, out_ref, slabs
):
    step = pl.program_id(0)
    time_tap = step // 3
    row_tap = step % 3
    time_index = lax.axis_index("tm")
    row_index = lax.axis_index("rows")
    positions = out_ref.shape[0]
    cols = up_ref.shape[1]

    @pl.when(step == 0)
    def _():
        out_ref[...] = jnp.zeros_like(out_ref)
        more = (time_index < lax.axis_size("tm") - 1).astype(F32)
        up_ok = (row_index > 0).astype(F32)
        down_ok = (row_index < lax.axis_size("rows") - 1).astype(F32)
        for f in range(4):
            trio = (above_ref, up_ref, below_ref) if f < 2 else (later_above_ref, later_ref, later_below_ref)
            tail = jnp.float32(1.0) if f < 2 else more
            for r, keep in enumerate((up_ok, jnp.float32(1.0), down_ok)):
                slab = (trio[r][f % 2].astype(F32) * (keep * tail)).astype(BF16)
                for c, moved in enumerate(col_shifts(slab)):
                    slabs[c, r, f] = moved

    def product(slab, c):
        return lax.dot_general(
            slab, weight_ref[0, 0, c], (((1,), (1,)), ((), ())), preferred_element_type=F32
        )

    total = out_ref[...]
    for c in range(3):
        slab = slabs[c, 2 - row_tap, pl.ds(2 - time_tap, 2)].reshape(positions, -1)
        total = total + product(slab, c)
    out_ref[...] = total

    @pl.when(jnp.logical_and(time_index == 0, time_tap == 0))
    def _():
        for c in range(3):
            both = slabs[c, 2 - row_tap, pl.ds(0, 2)].reshape(positions, -1)
            both = product(both, c)
            out_ref[0:cols, :] += both[0:cols] + both[cols:]

    @pl.when(jnp.logical_and(time_index == 0, time_tap == 1))
    def _():
        for c in range(3):
            out_ref[0:cols, :] += product(slabs[c, 2 - row_tap, 0], c)


def norm_rows(load_ref, chans, positions):
    stats = []
    for j in range(load_ref.shape[0]):
        for r in range(load_ref.shape[1]):
            parts = load_ref[j, r, load_ref.shape[2] - 16 :].astype(F32)
            stats.append(parts[0:1] + parts[1:2] + parts[2:3])
    stats = jnp.concatenate(stats, axis=0)
    devices = stats.shape[0]
    size = chans // GROUPS
    first = members(chans, 0)
    second = members(chans, GROUPS)
    total = jnp.sum(stats, axis=0, keepdims=True)
    centre = total / devices
    spans = stats - centre
    spans = jnp.sum(spans * spans, axis=0, keepdims=True)
    dims = ((1,), (1,))
    parts = exact_dot(jnp.broadcast_to(total, (8, 128)), second, dims) / (devices * positions * size)
    parts = parts + exact_dot(jnp.broadcast_to(spans, (8, 128)), first, dims) / devices
    inverse = lax.rsqrt(parts + EPS)
    centre = exact_dot(jnp.broadcast_to(centre, (8, 128)), first, dims)
    return centre, inverse


def act_kernel(
    positions, feats_ref, gain_ref, bias_ref, load_ref, dense_ref, act_ref, sums_ref, norm_ref, swap_ref
):
    chans = gain_ref.shape[1]
    start = load_ref.shape[2] - 16
    swap_ref[...] = load_ref[:, :, start - HALF : start, :]
    centre, inverse = norm_rows(load_ref, chans, positions)
    norm_ref[0:8] = centre
    norm_ref[8:16] = inverse
    centre = centre[0:1]
    inverse = inverse[0:1]
    normed = (feats_ref[...].astype(F32) - centre) * inverse
    preact = normed * gain_ref[...] + bias_ref[...]
    sig = sigmoid(preact)
    act = dense_ref[...] * sig * (1.0 + preact * (1.0 - sig))
    act_ref[...] = act
    gains = jnp.sum(act * normed, axis=0, keepdims=True)
    biases = jnp.sum(act, axis=0, keepdims=True)
    pieces = chans // 128
    rows = [gains[:, p * 128 : (p + 1) * 128] for p in range(pieces)]
    rows = rows + [biases[:, p * 128 : (p + 1) * 128] for p in range(pieces)]
    sums_ref[...] = jnp.broadcast_to(jnp.concatenate(rows, axis=0)[None], sums_ref.shape)


def append_kernel(part_ref, load_ref, out_ref):
    total = load_ref[0]
    for g in range(1, load_ref.shape[0]):
        total = total + load_ref[g]
    place = (out_ref.shape[0],) + total.shape
    out_ref[:, out_ref.shape[1] - total.shape[0] :, :] = jnp.broadcast_to(total[None], place)


def weight_kernel(teams, positions, load_ref, other_ref, gain_ref, bias_ref, out_ref, hidden, acc):
    time_index = lax.axis_index("tm")
    rows = load_ref.shape[1]
    cols = hidden.shape[2]
    chans = gain_ref.shape[1]
    wide = chans // TEAM
    step = chans // teams
    mover = ones_where(
        iota((chans, wide), 0) == sources(iota((1, wide), 1), chans, teams, time_index & (TEAM - 1))
    )

    def slice_of(value):
        return exact_dot(value, mover)[0:1]

    centre, inverse = (slice_of(value) for value in norm_rows(load_ref, chans, positions))
    gain = slice_of(jnp.broadcast_to(gain_ref[...], (8, chans)))
    bias = slice_of(jnp.broadcast_to(bias_ref[...], (8, chans)))

    def silu(value):
        preact = (value.astype(F32) - centre) * inverse * gain + bias
        return (preact * sigmoid(preact)).astype(BF16)

    frames = 2 * TEAM
    for f in range(frames + 2):
        hidden[f, 0] = jnp.zeros(hidden.shape[2:], BF16)
        hidden[f, rows + 1] = jnp.zeros(hidden.shape[2:], BF16)
    opening = (time_index < TEAM).astype(F32)
    for j in range(TEAM):
        for r in range(rows):
            for f in range(2):
                value = silu(load_ref[j, r, f * cols : (f + 1) * cols, :])
                hidden[2 + 2 * j + f, 1 + r] = value
                if j == 0 and f == 0:
                    value = (value.astype(F32) * opening).astype(BF16)
                    hidden[0, 1 + r] = value
                    hidden[1, 1 + r] = value

    base = 2 * cols

    def pieces_of(q, r):
        pieces = []
        for d, (begin, close) in enumerate(SHARES):
            size = (close - begin) // 2
            for half in range(2):
                first = max(q * cols, begin + half * size) - begin - half * size
                last = min((q + 1) * cols, begin + (half + 1) * size) - begin - half * size
                if first < last:
                    mine = load_ref[d, r, base + first : base + last, :]
                    pieces.append(jnp.where((time_index & 1) == half, mine, other_ref[d, r, first:last, :]))
        return pieces

    lanes = iota((cols, 128), 1) < 64
    more = (time_index < lax.axis_size("tm") - TEAM).astype(F32)
    for j in range(TEAM + 1):
        halves = [[], []]
        for r in range(rows):
            pair = jnp.concatenate(pieces_of(j, r), axis=0).astype(F32)
            if j == TEAM:
                pair = pair * more
            row = iota(pair.shape, 0)
            ahead = jnp.where(row < cols - 1, pltpu.roll(pair, cols - 1, 0), 0.0)
            behind = jnp.where(row > 0, pltpu.roll(pair, 1, 0), 0.0)
            left = jnp.where(lanes, ahead, pltpu.roll(pair, 64, 1))
            right = jnp.where(lanes, pltpu.roll(ahead, 64, 1), pair)
            halves[0].append(jnp.concatenate([left, behind[:, 0:64]], axis=1))
            halves[1].append(jnp.concatenate([right, behind[:, 64:128]], axis=1))

        def taps_of(frame, depth):
            taps = [
                hidden[frame + a, b : b + rows].reshape(rows * cols, wide) for a in range(depth) for b in range(3)
            ]
            return jnp.concatenate(taps, axis=1)

        sides = [jnp.concatenate(halves[f], axis=0).astype(BF16) for f in range(2)]
        if j < TEAM:
            jobs = [(jnp.concatenate(sides, axis=0), [taps_of(2 * j + f, 3) for f in range(2)], 3)]
        else:
            jobs = [(sides[f], [taps_of(2 * j + f, 2 - f)], 2 - f) for f in range(2)]
        for side, taps, depth in jobs:
            term = lax.dot_general(
                side, jnp.concatenate(taps, axis=0), (((0,), (0,)), ((), ())), preferred_element_type=F32
            )
            if j == 0:
                acc[...] = term
            else:
                acc[:, 0 : 3 * depth * wide] += term

    groups = out_ref.shape[0]
    tail = None
    for ab in range(9):
        block = acc[:, ab * wide : (ab + 1) * wide].T
        out_ref[:, ab * step : (ab + 1) * step, :] = block[:, 0:128].reshape(groups, step, 128)
        last = block[:, 128:192]
        if ab % 2 == 0:
            tail = last
        if ab % 2 == 1 or ab == 8:
            both = jnp.concatenate([tail, last], axis=1)
            at = (9 + ab // 2) * step
            out_ref[:, at : at + step, :] = both.reshape(groups, step, 128)


def final_kernel(
    count, load_ref, act_ref, feats_ref, norm_ref, gain_ref, out_ref, grad_ref, gain_out_ref, bias_out_ref
):
    chans = gain_ref.shape[1]
    pieces = chans // 128
    step = grad_ref.shape[2]
    total = load_ref[0]
    for g in range(1, load_ref.shape[0]):
        total = total + load_ref[g]
    for ab in range(9):
        part = total[ab * step : (ab + 1) * step]
        grad_ref[ab, 0] = part[:, 0:64]
        grad_ref[ab, 1] = part[:, 64:128]
        at = (9 + ab // 2) * step
        side = 64 * (ab % 2)
        grad_ref[ab, 2] = total[at : at + step, side : side + 64]
    total = total[14 * step :]
    gains = jnp.concatenate([total[p : p + 1] for p in range(pieces)], axis=1)
    biases = jnp.concatenate([total[pieces + p : pieces + p + 1] for p in range(pieces)], axis=1)
    gain_out_ref[...] = gains
    bias_out_ref[...] = biases
    gain = gain_ref[...]
    owner = members(chans, 0)

    def spread(value):
        value = exact_dot(jnp.broadcast_to(value, (8, chans)), owner) / count
        return exact_dot(value, owner, ((1,), (1,)))[0:1]

    first = spread(gain * biases)
    second = spread(gain * gains)
    centre = norm_ref[0:1]
    inverse = norm_ref[8:9]
    normed = (feats_ref[...].astype(F32) - centre) * inverse
    out_ref[...] = (inverse * (act_ref[...] * gain - first - normed * second)).astype(BF16)


def on_device(features, norm_gain, norm_bias, weight, upstream):
    frames, rows_dev, cols, chans = features.shape
    outs = upstream.shape[3]
    tms = lax.axis_size("tm")
    rows = lax.axis_size("rows")
    devices = tms * rows
    positions = frames * rows_dev * cols
    step = chans // tms
    groups = tms // TEAM
    wide = chans // TEAM
    count = positions * devices * (chans // GROUPS)
    vmem = pl.BlockSpec(memory_space=pltpu.VMEM)

    def params(mebibytes):
        return pltpu.CompilerParams(vmem_limit_bytes=mebibytes * 1024 * 1024)

    feats = features.reshape(positions, chans)
    ups = upstream.reshape(frames, cols, outs)
    gain = norm_gain.reshape(1, chans)
    bias = norm_bias.reshape(1, chans)
    size = TEAM * rows
    length = positions + HALF + 16
    teams = [[size * g + i for i in range(size)] for g in range(groups)]
    ranks = [[TEAM * g + j for g in range(groups)] for j in range(TEAM)]

    def in_teams(value):
        return lax.all_to_all(value, ("tm", "rows"), 0, 0, tiled=True, axis_index_groups=teams)

    def in_ranks(value):
        return lax.all_to_all(value, "tm", 0, 0, tiled=True, axis_index_groups=ranks)

    def neighbour(tm_step, row_step):
        pairs = [
            (((t + tm_step) % tms) * rows + (r + row_step) % rows, t * rows + r)
            for t in range(tms)
            for r in range(rows)
        ]
        return lax.ppermute(ups, ("tm", "rows"), pairs)

    halos = [neighbour(a, b) for a, b in EDGES]

    stats = pl.pallas_call(
        stats_kernel,
        out_shape=jax.ShapeDtypeStruct((groups, 8, 128), F32),
        compiler_params=params(62),
        name="stats",
    )(feats)
    stats = in_ranks(stats)
    pack_call = pl.pallas_call(
        functools.partial(pack_kernel, tms, float(positions * (chans // GROUPS))),
        in_specs=[pl.BlockSpec()] * 3 + [vmem],
        out_shape=jax.ShapeDtypeStruct((TEAM, rows, length, wide), BF16),
        compiler_params=params(62),
        name="pack",
    )
    load = pack_call(feats, ups, halos[0], stats)
    load = in_teams(load.reshape(size, length, wide)).reshape(TEAM, rows, length, wide)

    def whole(shape):
        return pl.BlockSpec(shape, lambda *s: (0,) * len(shape))

    dense_call = pl.pallas_call(
        dense_kernel,
        grid=(9,),
        in_specs=[
            *[whole((frames, cols, outs))] * 6,
            pl.BlockSpec((1, 1, 3, chans, outs), lambda s: (s // 3, s % 3, 0, 0, 0)),
        ],
        out_specs=whole((positions, chans)),
        out_shape=jax.ShapeDtypeStruct((positions, chans), F32),
        scratch_shapes=[pltpu.VMEM((3, 3, 4, cols, outs), BF16)],
        compiler_params=params(62),
        name="dense",
    )
    dense = dense_call(ups, halos[1], halos[2], halos[0], halos[3], halos[4], weight)

    act, sums, norm, swap = pl.pallas_call(
        functools.partial(act_kernel, positions * groups),
        in_specs=[pl.BlockSpec()] * 3 + [vmem, pl.BlockSpec()],
        out_shape=(
            jax.ShapeDtypeStruct((positions, chans), F32),
            jax.ShapeDtypeStruct((size, 8, 128), F32),
            jax.ShapeDtypeStruct((16, chans), F32),
            jax.ShapeDtypeStruct((TEAM, rows, HALF, wide), BF16),
        ),
        compiler_params=params(60),
        name="act",
    )(feats, gain, bias, load, dense)
    other = lax.ppermute(swap, "tm", [(t, t ^ 1) for t in range(tms)])
    sums = in_teams(sums)

    weight_call = pl.pallas_call(
        functools.partial(weight_kernel, tms, positions * groups),
        in_specs=[vmem] + [pl.BlockSpec()] * 3,
        out_specs=vmem,
        out_shape=jax.ShapeDtypeStruct((groups, 14 * step + 8, 128), F32),
        scratch_shapes=[
            pltpu.VMEM((2 * TEAM + 2, rows + 2, cols, wide), BF16),
            pltpu.VMEM((3 * 64, 9 * wide), F32),
        ],
        compiler_params=params(52),
        name="wgrad",
    )
    part = weight_call(load, other, gain, bias)
    part = pl.pallas_call(
        append_kernel,
        in_specs=[vmem, vmem],
        out_specs=vmem,
        out_shape=jax.ShapeDtypeStruct((groups, 14 * step + 8, 128), F32),
        input_output_aliases={0: 0},
        compiler_params=params(16),
        name="append",
    )(part, sums)
    part = in_ranks(part)

    grad_features, grad_weight, grad_gain, grad_bias = pl.pallas_call(
        functools.partial(final_kernel, count),
        in_specs=[vmem] + [pl.BlockSpec()] * 4,
        out_shape=(
            jax.ShapeDtypeStruct((positions, chans), BF16),
            jax.ShapeDtypeStruct((9, 3, step, outs // rows), F32),
            jax.ShapeDtypeStruct((1, chans), F32),
            jax.ShapeDtypeStruct((1, chans), F32),
        ),
        compiler_params=params(16),
        name="final",
    )(part, act, feats, norm, gain)
    return (
        grad_features.reshape(features.shape),
        grad_weight.reshape(3, 3, 3, step, outs // rows),
        grad_gain.reshape(chans),
        grad_bias.reshape(chans),
    )


def solution(mesh):
    in_specs = (P("tm", "rows", None, None), P(), P(), P(), P("tm", "rows", None, None))
    out_specs = (P("tm", "rows", None, None), P(None, None, None, "tm", "rows"), P(), P())
    return jax.shard_map(on_device, mesh=mesh, in_specs=in_specs, out_specs=out_specs, check_vma=False)
```
